32 devices in a mesh: req: 16 (over z, y, x), unit: 2 (over core).
Axes of the slice: x: 2, y: 2, z: 4, core: 2. Of those that a mesh axis runs over, the one named last changes fastest.
Arguments:
- queries: bfloat16 [4096, 1536], P(('req', 'unit')), as said below
- kv_new: bfloat16 [4096, 512], P(('req', 'unit')), as said below
- kv_pool: bfloat16 [416, 128, 512], P(('req', 'unit')), may hold values from -6 to 6
- page_table: int32 [32, 13], P(('req', 'unit')), may hold values from 0 to 12, as said below
- ctx_pages: int32 [32], P(('req', 'unit')), may hold values from 4 to 12
- ssm_x: bfloat16 [4096, 3072], P(('req', 'unit')), may hold values from -6 to 6
- ssm_z: bfloat16 [4096, 3072], P(('req', 'unit')), may hold values from -6 to 6
- ssm_bc: bfloat16 [4096, 512], P(('req', 'unit')), may hold values from -1.5 to 1.5
- dt_raw: float32 [4096, 24], P(('req', 'unit'))
- dt_bias: float32 [24], replicated, may hold values from -1 to 0.5
- decay_rate: float32 [24], replicated, may hold values from 0.002 to 0.06
- skip_gain: float32 [24], replicated, may hold values from 0.5 to 1.5
- ssm_state: float32 [32, 24, 128, 256], P(('req', 'unit')), may hold values from -6 to 6
- ssm_norm_gain: float32 [3072], replicated, may hold values from 0.25 to 1.75
- resid: bfloat16 [4096, 3072], P(('req', 'unit')), as said below
- out_weight: bfloat16 [4608, 3072], P('unit'), may hold values from -0.09375 to 0.09375
- ffn_hidden: bfloat16 [4096, 6144], P(('req', 'unit')), may hold values from -6 to 6
- down_weight: bfloat16 [6144, 3072], P(('req', 'unit')), may hold values from -0.078125 to 0.078125
- page_owner: int32 [32, 13, 1], P(('req', 'unit')), may hold values from 0 to 1; in each aligned block of 13 rows (0 to 12, 13 to 25, ..., all dimensions but the last counted through in order) at most 7 rows name the same one
Outputs:
- layer_out: bfloat16 [4096, 3072], P(('req', 'unit'))
- decode_kv: bfloat16 [448, 128, 512], P(('req', 'unit'))
- decode_state: float32 [32, 24, 128, 256], P('req', 'unit')
The draws below stay inside these ranges and needn't reach their ends.
Inputs may be any that keep to these rules, and one draw needn't show every extreme that they name: queries of the block. `kv_new`: keys and values of the block. `page_table`: each device's 1 * 13 entries name each of its 13 pool slots once. `resid`: residual stream. `page_owner`: among the 13 pages of one device at most 7 name the same owner.
All inputs are finite; a program needn't handle non-finite values.
Results may differ from the reference program's by a relative error of at most 0.007.
Values may be sent and summed in bfloat16 or wider, within the bound.
No kernel may reach another device: no remote copies, remote signals or barrier semaphores. Data moves between devices by JAX's collectives and lax.ppermute only.
A program may use at most 192 MiB of HBM per device.

```python
import math
import jax
import jax.numpy as jnp
import numpy as np
from jax import lax

D = 3072
FF = 6144
QUERY_HEADS = 12
KEY_VALUE_HEADS = 2
HEAD_WIDTH = 128
MIXER_HEADS = 24
PM = 128
NS = 256
PAGE_TOKENS = 128
CTXP = 12
MINP = 4
REQ_DEV = 1
TABLE_PAGES = 13
POOL = 13
OWNERS = 2
CAP = 7
DSLOTS = 14
REQUEST_COUNT = 32
TOKEN_COUNT = 4096
YW = 4608
KVW = 512
N_REQ = 16
N_UNIT = 2


def attention_pair(key):
    queries = 2.5 * jax.random.normal(jax.random.fold_in(key, 11), (TOKEN_COUNT, QUERY_HEADS * HEAD_WIDTH), jnp.float32)
    key_value_rows = jax.random.normal(jax.random.fold_in(key, 12), (TOKEN_COUNT, 2 * KEY_VALUE_HEADS * HEAD_WIDTH), jnp.float32)
    return (queries, key_value_rows)


def draw_queries(key, part):
    return attention_pair(key)[0].astype(jnp.bfloat16)


def draw_kv_new(key, part):
    return attention_pair(key)[1].astype(jnp.bfloat16)


def draw_page_table(key, part):
    device_count = REQUEST_COUNT // REQ_DEV
    keys = jax.random.split(jax.random.fold_in(key, 31), device_count)
    perms = jax.vmap(lambda one_key: jax.random.permutation(one_key, POOL))(keys)
    return perms.reshape(REQUEST_COUNT, TABLE_PAGES).astype(jnp.int32)


def draw_ctx_pages(key, part):
    counts = jax.random.randint(jax.random.fold_in(key, 21), (REQUEST_COUNT,), MINP, CTXP + 1, jnp.int32)
    highest = jax.random.randint(jax.random.fold_in(key, 22), (), 0, REQUEST_COUNT, jnp.int32)
    lowest = (highest + 1 + jax.random.randint(jax.random.fold_in(key, 23), (), 0, REQUEST_COUNT - 1, jnp.int32)) % REQUEST_COUNT
    counts = counts.at[highest].set(CTXP)
    counts = counts.at[lowest].set(MINP)
    return counts.astype(jnp.int32)


def draw_dt_raw(key, part):
    start_offset = 0.5 * jax.random.normal(jax.random.fold_in(key, 41), (TOKEN_COUNT, MIXER_HEADS), jnp.float32)
    block_tokens = jax.random.randint(jax.random.fold_in(key, 42), (TOKEN_COUNT, MIXER_HEADS), 0, 32, jnp.int32) == 0
    return start_offset + jnp.where(block_tokens, 3.0, 0.0)


def draw_resid(key, part):
    row_scale = jnp.exp(jax.random.uniform(jax.random.fold_in(key, 51), (TOKEN_COUNT, 1), jnp.float32, 0.0, math.log(10.0)))
    col_scale = jnp.exp(jax.random.uniform(jax.random.fold_in(key, 52), (1, D), jnp.float32, 0.0, math.log(10.0)))
    noise = jax.random.normal(jax.random.fold_in(key, 54), (TOKEN_COUNT, D), jnp.float32)
    values = 0.05 * row_scale * col_scale * noise
    return values.astype(jnp.bfloat16)


def steps_of(key, shape, cuts, low, top_value):
    def one(dim, shards_of):
        steps = jax.random.uniform(jax.random.fold_in(jax.random.fold_in(key, 6), dim), (shards_of,), jnp.float32, low / len(cuts), top_value / len(cuts))
        return jnp.repeat(jnp.exp(steps), shape[dim] // shards_of).reshape((-1,) + (1,) * (len(shape) - dim - 1))

    factor_of = one(*cuts[0])
    for cut in cuts[1:]:
        factor_of = factor_of * one(*cut)
    return factor_of


def assign_block(key, own, number, rows, amount, top, bound, lean):
    ranking = jax.random.permutation(key, amount)
    heavy_load, common = shares(amount, rows * top, bound, lean, True), shares(amount, rows * top, bound, lean, False)
    places = jnp.arange(amount)

    def named(sizes, rotation):
        used = int((sizes > 0).sum())
        fixed = max(1, used // 4)
        moved = fixed + (places - fixed + rotation * (used - fixed)) % max(1, amount - fixed)
        return jnp.zeros((amount,), jnp.int32).at[ranking[jnp.where(places < fixed, places, moved)]].set(jnp.asarray(sizes, jnp.int32))

    sizes = jnp.where(number % 4 == 0, named(heavy_load, number // 4), named(common, number - number // 4 - 1))
    mixed = jax.random.permutation(jax.random.fold_in(own, 3), amount)
    source_of, sink = mixed[0:amount // 2 * 2:2], mixed[1:amount // 2 * 2:2]
    room = jnp.minimum(sizes[source_of] - 1, bound - sizes[sink]) // 2
    room = jnp.where((source_of == ranking[0]) | (sink == ranking[0]) | (sizes[sink] == 0), 0, jnp.maximum(room, 0))
    moved = jax.random.randint(jax.random.fold_in(own, 4), (amount // 2,), 0, 1 << 20) % (room + 1)
    sizes = sizes.at[source_of].add(-moved).at[sink].add(moved)
    members = jnp.searchsorted(jnp.cumsum(sizes), jnp.arange(rows * top), side="right").astype(jnp.int32)
    table = members.reshape(top, rows).T
    table = table[jax.random.permutation(jax.random.fold_in(own, 1), rows)]
    rotation = jax.random.randint(jax.random.fold_in(own, 2), (rows, 1), 0, top)
    return jnp.take_along_axis(table, (jnp.arange(top)[None, :] + rotation) % top, axis=1)


def shares(amount, total, limit, skew, full):
    weights = [(1 << 20) // math.isqrt(standing ** skew) + 1 for standing in range(1, amount + 1)]
    largest = limit if full else min(limit, max(-(-total // amount), total * weights[0] // sum(weights)))
    least = 1 if total - largest >= amount - 1 else 0
    given, rest = [largest] + [least] * (amount - 1), total - largest - least * (amount - 1)
    while rest > 0:
        free = [i for i in range(1, amount) if given[i] < largest] or [i for i in range(1, amount) if given[i] < limit]
        whole, remaining = sum([weights[i] for i in free]), rest
        for i in free:
            extra = min(limit - given[i], max(1, remaining * weights[i] // whole), rest)
            given[i] = given[i] + extra
            rest = rest - extra
    return np.array(given)


def scatter_about(stream_key, dims, deviation, bound, cuts=(), kind=jnp.bfloat16):
    values = jax.random.normal(stream_key, dims, jnp.float32) * deviation
    if len(cuts) > 0:
        values = steps_of(stream_key, dims, cuts, -0.22, 0.18) * values
    return jnp.clip(values, min=-bound, max=bound).astype(kind)


def setup_inputs(seed: int = 0) -> dict:
    splits = jax.random.split(jax.random.key(seed), 20)
    queries = draw_queries(jax.random.fold_in(splits[19], 71), 0)
    kv_new = draw_kv_new(jax.random.fold_in(splits[19], 71), 0)
    kv_pool = scatter_about(splits[2], (REQUEST_COUNT * TABLE_PAGES, PAGE_TOKENS, KVW), 1.0, 6.0, ((0, 32),))
    page_table = draw_page_table(jax.random.fold_in(splits[19], 71), 0)
    ctx_pages = draw_ctx_pages(jax.random.fold_in(splits[19], 71), 0)
    ssm_x = scatter_about(splits[5], (TOKEN_COUNT, MIXER_HEADS * PM), 1.0, 6.0, ((0, 32),))
    ssm_z = scatter_about(splits[6], (TOKEN_COUNT, MIXER_HEADS * PM), 1.0, 6.0, ((0, 32),))
    ssm_bc = scatter_about(splits[7], (TOKEN_COUNT, 2 * NS), 0.25, 1.5, ((0, 32),))
    dt_raw = draw_dt_raw(jax.random.fold_in(splits[19], 71), 0)
    dt_bias = jnp.clip(jax.random.uniform(splits[9], (MIXER_HEADS,), jnp.float32, -1.0, 0.5), -1.0, 0.5)
    decay_rate = jnp.clip(jnp.exp(jax.random.uniform(splits[10], (MIXER_HEADS,), jnp.float32, math.log(0.002), math.log(0.06))), 0.002, 0.06)
    skip_gain = jnp.clip(jax.random.uniform(splits[11], (MIXER_HEADS,), jnp.float32, 0.5, 1.5), 0.5, 1.5)
    ssm_state = scatter_about(splits[12], (REQUEST_COUNT, MIXER_HEADS, PM, NS), 1.0, 6.0, ((0, 32),), jnp.float32)
    ssm_norm_gain = jnp.clip(1.0 + 0.15 * jax.random.normal(splits[13], (MIXER_HEADS * PM,), jnp.float32), 0.25, 1.75)
    resid = draw_resid(jax.random.fold_in(splits[19], 71), 0)
    out_weight = scatter_about(splits[15], (YW, D), YW ** -0.5, 0.09375, ((0, 2),))
    ffn_hidden = scatter_about(splits[16], (TOKEN_COUNT, FF), 1.0, 6.0, ((0, 32),))
    down_weight = scatter_about(splits[17], (FF, D), FF ** -0.5, 0.078125, ((0, 32),))
    page_owner_keys = jax.random.split(jax.random.fold_in(splits[18], 1), REQUEST_COUNT * TABLE_PAGES // (REQ_DEV * TABLE_PAGES))
    page_owner_turns = jax.random.permutation(jax.random.fold_in(splits[18], 3), REQUEST_COUNT * TABLE_PAGES // (REQ_DEV * TABLE_PAGES))
    page_owner = jax.vmap(lambda own, number: assign_block(jax.random.fold_in(splits[18], 2), own, number, REQ_DEV * TABLE_PAGES, OWNERS, 1, CAP, 1))(page_owner_keys, page_owner_turns).reshape((REQUEST_COUNT, TABLE_PAGES, 1))
    return {"queries": queries, "kv_new": kv_new, "kv_pool": kv_pool, "page_table": page_table, "ctx_pages": ctx_pages, "ssm_x": ssm_x, "ssm_z": ssm_z, "ssm_bc": ssm_bc, "dt_raw": dt_raw, "dt_bias": dt_bias, "decay_rate": decay_rate, "skip_gain": skip_gain, "ssm_state": ssm_state, "ssm_norm_gain": ssm_norm_gain, "resid": resid, "out_weight": out_weight, "ffn_hidden": ffn_hidden, "down_weight": down_weight, "page_owner": page_owner}


norm_eps = 1e-05

def attend(query_block, pages_now, live_count):
    pages_flattened = pages_now.reshape(TABLE_PAGES * PAGE_TOKENS, KVW).astype(jnp.float32)
    key_block_rows = pages_flattened[:, :KEY_VALUE_HEADS * HEAD_WIDTH].reshape(TABLE_PAGES * PAGE_TOKENS, KEY_VALUE_HEADS, HEAD_WIDTH)
    value_block_rows = pages_flattened[:, KEY_VALUE_HEADS * HEAD_WIDTH:].reshape(TABLE_PAGES * PAGE_TOKENS, KEY_VALUE_HEADS, HEAD_WIDTH)
    heads_per_group = QUERY_HEADS // KEY_VALUE_HEADS
    query_head_rows = query_block.astype(jnp.float32).reshape(PAGE_TOKENS, KEY_VALUE_HEADS, heads_per_group, HEAD_WIDTH)
    scores = jnp.einsum('tkgd,skd->kgts', query_head_rows, key_block_rows) * (1.0 / math.sqrt(HEAD_WIDTH))
    key_pos = jnp.arange(TABLE_PAGES * PAGE_TOKENS, dtype=jnp.int32)
    q_limit = live_count * PAGE_TOKENS + jnp.arange(PAGE_TOKENS, dtype=jnp.int32)
    visible = key_pos[None, :] <= q_limit[:, None]
    scores = jnp.where(visible[None, None], scores, -1e+30)
    row_max = lax.optimization_barrier(jnp.max(scores, axis=-1, keepdims=True))
    exponent = jnp.exp(scores - row_max)
    weights = (exponent / lax.optimization_barrier(jnp.sum(exponent, axis=-1, keepdims=True))).astype(jnp.bfloat16)
    attended = jnp.einsum('kgts,skd->tkgd', weights.astype(jnp.float32), value_block_rows)
    return attended.reshape(PAGE_TOKENS, QUERY_HEADS * HEAD_WIDTH).astype(jnp.bfloat16)

def ssm_block(ssm_in, gate_in, bc_rows, dt_rows, dt_bias, decay_rate, skip_gain, prior_state, norm_gain):
    step_size = jax.nn.softplus(dt_rows + dt_bias[None, :])
    cum = jnp.cumsum(-step_size * decay_rate[None, :], axis=0)
    b_rows = bc_rows[:, :NS]
    c_rows = bc_rows[:, NS:]
    cb_dots = jnp.dot(c_rows, b_rows.T, preferred_element_type=jnp.float32)
    cum_heads = cum.T
    log_gap = cum_heads[:, :, None] - cum_heads[:, None, :]
    causal = jnp.arange(PAGE_TOKENS)[:, None] >= jnp.arange(PAGE_TOKENS)[None, :]
    decay = jnp.exp(jnp.where(causal[None], log_gap, -1e+30))
    mixing = (cb_dots[None] * decay * step_size.T[:, None, :]).astype(jnp.bfloat16)
    x_heads = ssm_in.astype(jnp.float32).reshape(PAGE_TOKENS, MIXER_HEADS, PM)
    within = jnp.einsum('hts,shp->thp', mixing.astype(jnp.float32), x_heads)
    carried = jnp.einsum('tn,hpn->thp', c_rows.astype(jnp.float32), prior_state, precision=lax.Precision.HIGHEST)
    carried = carried * jnp.exp(cum)[:, :, None]
    ssm_y = within + carried + skip_gain[None, :, None] * x_heads
    total_decay = cum[PAGE_TOKENS - 1]
    tail_weight = jnp.exp(total_decay[None, :] - cum) * step_size
    x_weighted = x_heads * tail_weight[:, :, None]
    new_state = jnp.exp(total_decay)[:, None, None] * prior_state + jnp.einsum('shp,sn->hpn', x_weighted, b_rows.astype(jnp.float32), precision=lax.Precision.HIGHEST)
    gated = ssm_y.reshape(PAGE_TOKENS, MIXER_HEADS * PM) * jax.nn.silu(gate_in.astype(jnp.float32))
    gated = gated * lax.rsqrt(lax.optimization_barrier(jnp.mean(gated * gated, axis=-1, keepdims=True)) + norm_eps) * norm_gain[None, :]
    return (gated.astype(jnp.bfloat16), new_state)

def reference(queries, kv_new, kv_pool, page_table, ctx_pages, ssm_x, ssm_z, ssm_bc, dt_raw, dt_bias, decay_rate, skip_gain, ssm_state, ssm_norm_gain, resid, out_weight, ffn_hidden, down_weight, page_owner):
    device = jnp.arange(REQUEST_COUNT, dtype=jnp.int32) // REQ_DEV
    slot_index = (device[:, None] * POOL + page_table).astype(jnp.int32)

    def per_request(inputs):
        query_block, fresh_kv, slot_row, live_count, ssm_in, gate_in, bc_rows, dt_rows, prior_state = inputs
        stored = kv_pool[slot_row]
        pages_now = lax.dynamic_update_slice(stored, fresh_kv[None], (live_count, jnp.int32(0), jnp.int32(0)))
        attn_out = attend(query_block, pages_now, live_count)
        live = jnp.arange(TABLE_PAGES, dtype=jnp.int32) <= live_count
        kept_pages = jnp.where(live[:, None, None], pages_now, jnp.zeros_like(pages_now))
        ssm_out, new_state = ssm_block(ssm_in, gate_in, bc_rows, dt_rows, dt_bias, decay_rate, skip_gain, prior_state, ssm_norm_gain)
        return (jnp.concatenate([attn_out, ssm_out], axis=1), kept_pages, new_state)
    mixed_rows, kept_pages, new_state = lax.map(per_request, (queries.reshape(REQUEST_COUNT, PAGE_TOKENS, QUERY_HEADS * HEAD_WIDTH), kv_new.reshape(REQUEST_COUNT, PAGE_TOKENS, KVW), slot_index, ctx_pages, ssm_x.reshape(REQUEST_COUNT, PAGE_TOKENS, MIXER_HEADS * PM), ssm_z.reshape(REQUEST_COUNT, PAGE_TOKENS, MIXER_HEADS * PM), ssm_bc.reshape(REQUEST_COUNT, PAGE_TOKENS, 2 * NS), dt_raw.reshape(REQUEST_COUNT, PAGE_TOKENS, MIXER_HEADS), ssm_state))
    mixed_rows = mixed_rows.reshape(TOKEN_COUNT, YW)
    group_width = YW // N_UNIT
    mixer_sum = jnp.zeros((TOKEN_COUNT, D), jnp.float32)
    for unit_idx in range(N_UNIT):
        partial_term = jnp.dot(mixed_rows[:, unit_idx * group_width:(unit_idx + 1) * group_width], out_weight[unit_idx * group_width:(unit_idx + 1) * group_width], preferred_element_type=jnp.float32)
        mixer_sum = mixer_sum + lax.optimization_barrier(partial_term.astype(jnp.bfloat16)).astype(jnp.float32)
    after_mixers = resid.astype(jnp.float32) + mixer_sum
    block_rows = FF // (N_REQ * N_UNIT)
    hidden_blocks = ffn_hidden.reshape(TOKEN_COUNT, N_REQ, N_UNIT, block_rows)
    down_blocks = down_weight.reshape(N_REQ, N_UNIT, block_rows, D)
    ffn_sum = jnp.zeros((TOKEN_COUNT, D), jnp.float32)
    for unit_idx in range(N_UNIT):
        partial_term = jnp.dot(hidden_blocks[:, :, unit_idx].reshape(TOKEN_COUNT, N_REQ * block_rows), down_blocks[:, unit_idx].reshape(N_REQ * block_rows, D), preferred_element_type=jnp.float32)
        ffn_sum = ffn_sum + lax.optimization_barrier(partial_term.astype(jnp.bfloat16)).astype(jnp.float32)
    layer_out = (after_mixers + ffn_sum).astype(jnp.bfloat16)
    device_count = REQUEST_COUNT // REQ_DEV
    owners = page_owner[..., 0].reshape(device_count, REQ_DEV * TABLE_PAGES).astype(jnp.int32)
    onehot = (owners[..., None] == jnp.arange(N_UNIT, dtype=jnp.int32)[None, None, :]).astype(jnp.int32)
    before = jnp.cumsum(onehot, axis=1) - onehot
    page_rank = lax.optimization_barrier(jnp.sum(before * onehot, axis=-1))
    device_idx = jnp.arange(device_count, dtype=jnp.int32)[:, None]
    dest_slot = (device_idx // N_UNIT * N_UNIT + owners) * DSLOTS + device_idx % N_UNIT * CAP + page_rank
    decode_kv = jnp.zeros((device_count * DSLOTS, PAGE_TOKENS, KVW), jnp.bfloat16)
    decode_kv = decode_kv.at[dest_slot.reshape(-1)].set(kept_pages.reshape(-1, PAGE_TOKENS, KVW))
    return (layer_out, decode_kv, new_state)
```

```python
import math

import jax
import jax.numpy as jnp
from jax import lax
from jax.sharding import PartitionSpec as P

QUERY_HEADS = 12
KEY_VALUE_HEADS = 2
HEAD_WIDTH = 128
MIXER_HEADS = 24
PM = 128
NS = 256

PLANE = 4

norm_eps = 1e-05


def attend(query_block, pages_now, live_count):
    request_pages = pages_now.shape[0]
    block_length = pages_now.shape[1]
    kv_width = pages_now.shape[2]
    pages_flattened = pages_now.reshape(request_pages * block_length, kv_width)
    key_block_rows = pages_flattened[:, : KEY_VALUE_HEADS * HEAD_WIDTH].reshape(
        request_pages * block_length, KEY_VALUE_HEADS, HEAD_WIDTH
    )
    value_block_rows = pages_flattened[:, KEY_VALUE_HEADS * HEAD_WIDTH :].reshape(
        request_pages * block_length, KEY_VALUE_HEADS, HEAD_WIDTH
    )
    heads_per_group = QUERY_HEADS // KEY_VALUE_HEADS
    query_head_rows = query_block.reshape(
        block_length, KEY_VALUE_HEADS, heads_per_group, HEAD_WIDTH
    )
    scores = jnp.einsum(
        "tkgd,skd->kgts", query_head_rows, key_block_rows, preferred_element_type=jnp.float32
    )
    scores = scores * (1.0 / math.sqrt(HEAD_WIDTH))
    key_pos = jnp.arange(request_pages * block_length, dtype=jnp.int32)
    q_limit = live_count * block_length + jnp.arange(block_length, dtype=jnp.int32)
    visible = key_pos[None, :] <= q_limit[:, None]
    scores = jnp.where(visible[None, None], scores, -1e30)
    row_max = jnp.max(scores, axis=-1, keepdims=True)
    exponent = jnp.exp(scores - row_max)
    weights = (exponent / jnp.sum(exponent, axis=-1, keepdims=True)).astype(jnp.bfloat16)
    attended = jnp.einsum(
        "kgts,skd->tkgd", weights, value_block_rows, preferred_element_type=jnp.float32
    )
    return attended.reshape(block_length, QUERY_HEADS * HEAD_WIDTH).astype(jnp.bfloat16)


def ssm_block(
    ssm_in, gate_in, bc_rows, dt_rows, dt_bias, decay_rate, skip_gain, prior_state, norm_gain
):
    block_length = ssm_in.shape[0]
    causal = jnp.arange(block_length)[:, None] >= jnp.arange(block_length)[None, :]
    step_size = jax.nn.softplus(dt_rows + dt_bias[None, :])
    cum = jnp.dot(
        causal.astype(jnp.float32),
        -step_size * decay_rate[None, :],
        precision=lax.Precision.HIGHEST,
    )
    b_rows = bc_rows[:, :NS]
    c_rows = bc_rows[:, NS:]
    cb_dots = jnp.dot(c_rows, b_rows.T, preferred_element_type=jnp.float32)
    cum_heads = cum.T
    log_gap = cum_heads[:, :, None] - cum_heads[:, None, :]
    decay = jnp.exp(jnp.where(causal[None], log_gap, -1e30))
    mixing = (cb_dots[None] * decay * step_size.T[:, None, :]).astype(jnp.bfloat16)
    x_heads = ssm_in.reshape(block_length, MIXER_HEADS, PM)
    within = jnp.einsum("hts,shp->thp", mixing, x_heads, preferred_element_type=jnp.float32)
    carried = jnp.einsum(
        "tn,hpn->thp", c_rows.astype(jnp.float32), prior_state, precision=lax.Precision.HIGHEST
    )
    carried = carried * jnp.exp(cum)[:, :, None]
    x_float = x_heads.astype(jnp.float32)
    ssm_y = within + carried + skip_gain[None, :, None] * x_float
    total_decay = cum[block_length - 1]
    tail_weight = jnp.exp(total_decay[None, :] - cum) * step_size
    x_weighted = x_float * tail_weight[:, :, None]
    new_state = jnp.exp(total_decay)[:, None, None] * prior_state + jnp.einsum(
        "shp,sn->hpn", x_weighted, b_rows.astype(jnp.float32), precision=lax.Precision.HIGHEST
    )
    gated = ssm_y.reshape(block_length, MIXER_HEADS * PM) * jax.nn.silu(gate_in.astype(jnp.float32))
    gated = (
        gated
        * lax.rsqrt(jnp.mean(gated * gated, axis=-1, keepdims=True) + norm_eps)
        * norm_gain[None, :]
    )
    return (gated.astype(jnp.bfloat16), new_state)


def swap_units(x):
    return lax.ppermute(x, "unit", [(0, 1), (1, 0)])


def folded_ring(length):
    return [0] + list(range(1, length, 2)) + list(range(2, length, 2))[::-1]


def chunk_widths(width):
    third = width // 3 // 128 * 128
    return [third, third, width - 2 * third] if third else [width]


def on_device(
    queries,
    kv_new,
    kv_pool,
    page_table,
    ctx_pages,
    ssm_x,
    ssm_z,
    ssm_bc,
    dt_raw,
    dt_bias,
    decay_rate,
    skip_gain,
    ssm_state,
    ssm_norm_gain,
    resid,
    out_weight,
    ffn_hidden,
    down_weight,
    page_owner,
):
    tok_rows = queries.shape[0]
    block_length = kv_pool.shape[1]
    kv_width = kv_pool.shape[2]
    request_pages = page_table.shape[1]
    n_req = lax.axis_size("req")
    block_rows, width = down_weight.shape
    u = lax.axis_index("unit")
    req = lax.axis_index("req")
    layers = n_req // PLANE
    layer, place = req // PLANE, req % PLANE
    half = width // 2
    first = u == 0

    mine = lax.dynamic_slice(down_weight, (0, u * half), (block_rows, half))
    other = lax.dynamic_slice(down_weight, (0, (1 - u) * half), (block_rows, half))
    widths = chunk_widths(half)
    edges = [sum(widths[:i]) for i in range(len(widths) + 1)]
    ring = folded_ring(layers)
    ring_pairs = [
        (ring[i] * PLANE + p, ring[(i + 1) % layers] * PLANE + p)
        for i in range(layers)
        for p in range(PLANE)
    ]
    ring_place = jnp.asarray([ring.index(i) for i in range(layers)], jnp.int32)[layer]
    ring_table = jnp.asarray(ring, jnp.int32)
    pieces = []
    for lo, hi in zip(edges[:-1], edges[1:]):
        got = swap_units(other[:, lo:hi])
        kept = mine[:, lo:hi]
        pieces.append(
            [jnp.concatenate([jnp.where(first, kept, got), jnp.where(first, got, kept)], axis=0)]
        )
    for _ in range(layers - 1):
        for piece in pieces:
            piece.append(lax.ppermute(piece[-1], "req", ring_pairs))

    chip_rows = block_rows * 2
    by_place = ffn_hidden.reshape(tok_rows, layers, PLANE, chip_rows).transpose(2, 1, 0, 3)

    def plane_pairs(d):
        return [(r, r - r % PLANE + ((r % PLANE) ^ d)) for r in range(n_req)]

    def to_plane(x, d):
        block = lax.dynamic_index_in_dim(x, place ^ d, 0, keepdims=False)
        return lax.ppermute(block, "req", plane_pairs(d)) if d else block

    hidden = jnp.stack([to_plane(by_place, d) for d in range(PLANE)])
    hidden_other = swap_units(hidden)
    hidden = jnp.stack([hidden, hidden_other], axis=1)
    hidden = jnp.transpose(hidden, (2, 0, 1, 3, 4)).reshape(layers, PLANE * 2 * tok_rows, chip_rows)
    order = ring_table[(ring_place - jnp.arange(layers, dtype=jnp.int32)) % layers]
    hidden = jnp.concatenate(
        [lax.dynamic_index_in_dim(hidden, order[k], 0, keepdims=False) for k in range(layers)], axis=1
    )

    slot_row = page_table[0]
    live_count = ctx_pages[0]
    stored = jnp.stack(
        [
            lax.dynamic_index_in_dim(kv_pool, slot_row[j], 0, keepdims=False)
            for j in range(request_pages)
        ]
    )
    pages_now = lax.dynamic_update_slice(
        stored, kv_new[None], (live_count, jnp.int32(0), jnp.int32(0))
    )
    attn_out = attend(queries, pages_now, live_count)
    live = jnp.arange(request_pages, dtype=jnp.int32) <= live_count
    ssm_out, new_state = ssm_block(
        ssm_x,
        ssm_z,
        ssm_bc,
        dt_raw,
        dt_bias,
        decay_rate,
        skip_gain,
        ssm_state[0],
        ssm_norm_gain,
    )
    mixed_rows = jnp.concatenate([attn_out, ssm_out], axis=1)
    mix_width = mixed_rows.shape[1] // 2
    stay = lax.dynamic_slice(mixed_rows, (0, u * mix_width), (tok_rows, mix_width))
    leave = lax.dynamic_slice(mixed_rows, (0, (1 - u) * mix_width), (tok_rows, mix_width))
    exchanged = jnp.concatenate([stay, swap_units(leave)], axis=0)
    mixed = jnp.dot(exchanged, out_weight, preferred_element_type=jnp.float32).astype(jnp.bfloat16)
    mixer_sum = mixed[:tok_rows].astype(jnp.float32) + swap_units(mixed[tok_rows:]).astype(
        jnp.float32
    )
    after_mixers = resid.astype(jnp.float32) + mixer_sum

    slot_cap = max(2, (request_pages + 1) // 2)
    owners = page_owner.reshape(request_pages)
    earlier = jnp.arange(request_pages)[:, None] > jnp.arange(request_pages)[None, :]
    same = owners[:, None] == owners[None, :]
    page_rank = jnp.sum((earlier & same).astype(jnp.int32), axis=1)
    dest_slot = owners * slot_cap + page_rank

    def slots_of(owner):
        blocks = []
        for k in range(slot_cap):
            hit = dest_slot == owner * slot_cap + k
            page = jnp.sum(jnp.where(hit, jnp.arange(request_pages, dtype=jnp.int32), 0))
            block = lax.dynamic_index_in_dim(pages_now, page, 0, keepdims=False)
            blocks.append(jnp.where(jnp.any(hit & live), block, jnp.zeros_like(block)))
        return jnp.stack(blocks)

    keep = slots_of(u)
    came = swap_units(slots_of(1 - u))
    decode_kv = jnp.concatenate([jnp.where(first, keep, came), jnp.where(first, came, keep)], axis=0)
    heads = MIXER_HEADS // 2
    keep = lax.dynamic_slice(new_state, (u * heads, 0, 0), (heads, PM, NS))
    send = lax.dynamic_slice(new_state, ((1 - u) * heads, 0, 0), (heads, PM, NS))
    came = swap_units(send.astype(jnp.bfloat16)).astype(jnp.float32)
    decode_state = jnp.stack([jnp.where(first, keep, came), jnp.where(first, came, keep)])

    own_cols, other_cols = [], []
    for piece in pieces:
        weight = jnp.concatenate(piece, axis=0)
        part = jnp.dot(hidden, weight, preferred_element_type=jnp.float32).astype(jnp.bfloat16)
        part = part.reshape(PLANE, 2 * tok_rows, -1)
        total = part[0].astype(jnp.float32)
        for d in range(1, PLANE):
            total = total + lax.ppermute(part[d], "req", plane_pairs(d)).astype(jnp.float32)
        own_cols.append(total[:tok_rows])
        other_cols.append(swap_units(total[tok_rows:].astype(jnp.bfloat16)).astype(jnp.float32))
    own_cols = jnp.concatenate(own_cols, axis=1)
    other_cols = jnp.concatenate(other_cols, axis=1)
    ffn_sum = jnp.concatenate(
        [jnp.where(first, own_cols, other_cols), jnp.where(first, other_cols, own_cols)], axis=1
    )
    layer_out = (after_mixers + ffn_sum).astype(jnp.bfloat16)
    return (layer_out, decode_kv, decode_state)


def solution(mesh):
    return jax.shard_map(
        on_device,
        mesh=mesh,
        in_specs=(
            P(("req", "unit"), None),
            P(("req", "unit"), None),
            P(("req", "unit"), None, None),
            P(("req", "unit"), None),
            P(("req", "unit")),
            P(("req", "unit"), None),
            P(("req", "unit"), None),
            P(("req", "unit"), None),
            P(("req", "unit"), None),
            P(),
            P(),
            P(),
            P(("req", "unit"), None, None, None),
            P(),
            P(("req", "unit"), None),
            P("unit", None),
            P(("req", "unit"), None),
            P(("req", "unit"), None),
            P(("req", "unit"), None, None),
        ),
        out_specs=(
            P(("req", "unit"), None),
            P(("req", "unit"), None, None),
            P("req", "unit", None, None),
        ),
        check_vma=False,
    )
```

```python
import functools
import math

import jax
import jax.numpy as jnp
from jax import lax
from jax.experimental import pallas as pl
from jax.experimental.pallas import tpu as pltpu
from jax.sharding import PartitionSpec as P

QUERY_HEADS = 12
KEY_VALUE_HEADS = 2
HEAD_WIDTH = 128
MIXER_HEADS = 24
PM = 128
NS = 256

PLANE = 4

norm_eps = 1e-05

F32, BF16 = jnp.float32, jnp.bfloat16
VMEM = pl.BlockSpec(memory_space=pltpu.VMEM)
SMEM = pl.BlockSpec(memory_space=pltpu.SMEM)
ANY = pl.BlockSpec(memory_space=pl.ANY)
PARAMS = pltpu.CompilerParams(vmem_limit_bytes=48 * 1024 * 1024)


def cost(flops, moved, exps=0):
    return pl.CostEstimate(flops=flops, bytes_accessed=moved, transcendentals=exps)


def contract_last(a, b):
    return lax.dot_general(a, b, (((1,), (1,)), ((), ())), preferred_element_type=F32)


def two_terms(x):
    high = x.astype(BF16)
    return high, (x - high.astype(F32)).astype(BF16)


def attend_kernel(
    table, ctx, owner, unit, q_ref, new_ref, pool, out_ref, held, leave, pages, zero, sems, osems
):
    count, length, _ = pages.shape
    slots = leave.shape[0]
    live = ctx[0]
    u = unit[0]
    for j in range(count):

        @pl.when(j == live)
        def _():
            pltpu.make_async_copy(new_ref, pages.at[j], sems.at[j]).start()

        @pl.when(j != live)
        def _():
            pltpu.make_async_copy(pool.at[table[0, j]], pages.at[j], sems.at[j]).start()

    zero[...] = jnp.zeros_like(zero)
    for j in range(count):
        pltpu.make_async_copy(new_ref, pages.at[j], sems.at[j]).wait()

    named = [jnp.int32(0), jnp.int32(0)]
    for j in range(count):
        own = owner[0, j] == u
        rank = jnp.where(own, named[0], named[1])
        named = [named[0] + own.astype(jnp.int32), named[1] + 1 - own.astype(jnp.int32)]
        for source, when in ((pages.at[j], j <= live), (zero, j > live)):

            @pl.when(when & own)
            def _():
                pltpu.make_async_copy(source, held.at[u * slots + rank], osems.at[j]).start()

            @pl.when(when & jnp.logical_not(own))
            def _():
                pltpu.make_async_copy(source, leave.at[rank], osems.at[j]).start()

    for k in range(slots):

        @pl.when(k >= named[0])
        def _():
            pltpu.make_async_copy(zero, held.at[u * slots + k], osems.at[count + k]).start()

        @pl.when(k >= named[1])
        def _():
            pltpu.make_async_copy(zero, leave.at[k], osems.at[count + slots + k]).start()

    group = QUERY_HEADS // KEY_VALUE_HEADS
    heads = 3
    rows, keys = heads * length, count * length
    limit = live * length + lax.broadcasted_iota(jnp.int32, (rows, 1), 0) % length
    visible = lax.broadcasted_iota(jnp.int32, (rows, keys), 1) <= limit
    scale = 1.0 / math.sqrt(HEAD_WIDTH)
    for k in range(KEY_VALUE_HEADS):
        key_rows = pages[:, :, k * HEAD_WIDTH : (k + 1) * HEAD_WIDTH].reshape(keys, HEAD_WIDTH)
        lo = (KEY_VALUE_HEADS + k) * HEAD_WIDTH
        value_rows = pages[:, :, lo : lo + HEAD_WIDTH].reshape(keys, HEAD_WIDTH)
        for first in range(k * group, (k + 1) * group, heads):
            spans = [
                slice(h * HEAD_WIDTH, (h + 1) * HEAD_WIDTH) for h in range(first, first + heads)
            ]
            q = jnp.concatenate([q_ref[:, span] for span in spans], axis=0)
            scores = jnp.where(visible, contract_last(q, key_rows), -1e30)
            top = jnp.max(scores, axis=1, keepdims=True)
            exponent = jnp.exp((scores - top) * scale)
            weights = (exponent * (1.0 / jnp.sum(exponent, axis=1, keepdims=True))).astype(BF16)
            attended = jnp.dot(weights, value_rows, preferred_element_type=F32).astype(BF16)
            for i, span in enumerate(spans):
                out_ref[:, span] = attended[i * length : (i + 1) * length]

    for j in range(count):
        pltpu.make_async_copy(zero, leave.at[0], osems.at[j]).wait()
    for k in range(slots):

        @pl.when(k >= named[0])
        def _():
            pltpu.make_async_copy(zero, leave.at[0], osems.at[count + k]).wait()

        @pl.when(k >= named[1])
        def _():
            pltpu.make_async_copy(zero, leave.at[0], osems.at[count + slots + k]).wait()


def attend(table, ctx, owner, unit, queries, kv_new, pool):
    count, length, width = pool.shape
    slots = max(2, (count + 1) // 2)
    pairs = QUERY_HEADS * length * count * length
    return pl.pallas_call(
        attend_kernel,
        out_shape=(
            jax.ShapeDtypeStruct(queries.shape, BF16),
            jax.ShapeDtypeStruct((2 * slots, length, width), BF16),
            jax.ShapeDtypeStruct((slots, length, width), BF16),
        ),
        in_specs=[SMEM, SMEM, SMEM, SMEM, VMEM, VMEM, ANY],
        out_specs=(VMEM, ANY, ANY),
        scratch_shapes=[
            pltpu.VMEM((count, length, width), BF16),
            pltpu.VMEM((length, width), BF16),
            pltpu.SemaphoreType.DMA((count,)),
            pltpu.SemaphoreType.DMA((count + 2 * slots,)),
        ],
        compiler_params=PARAMS,
        cost_estimate=cost(4 * pairs * HEAD_WIDTH * 4, 6 << 20, pairs),
        name="attend",
    )(table, ctx, owner, unit, queries, kv_new, pool)


def state_kernel(
    unit,
    skip,
    attn_ref,
    x_ref,
    z_ref,
    bc_ref,
    dt_ref,
    bias_ref,
    rate_ref,
    gain_ref,
    state_ref,
    stay_ref,
    leave_ref,
    held,
    send_ref,
    gated,
    fresh,
    sems,
):
    length = x_ref.shape[0]
    heads, share = MIXER_HEADS, MIXER_HEADS // 2
    u = unit[0]
    rows = lax.broadcasted_iota(jnp.int32, (length, length), 0)
    cols = lax.broadcasted_iota(jnp.int32, (length, length), 1)
    causal = rows >= cols
    raw = dt_ref[...] + bias_ref[...]
    step = jnp.maximum(raw, 0.0) + jnp.log1p(jnp.exp(-jnp.abs(raw)))
    cum = jnp.dot(
        causal.astype(F32),
        -step * rate_ref[...],
        precision=lax.Precision.HIGHEST,
        preferred_element_type=F32,
    )
    blank = jnp.zeros((length, length - heads), F32)
    cum_rows = jnp.transpose(jnp.concatenate([cum, blank], axis=1))
    step_rows = jnp.transpose(jnp.concatenate([step, blank], axis=1))
    last = cum[length - 1 : length, :]
    b_rows, c_rows = bc_ref[:, :NS], bc_ref[:, NS:]
    dots = contract_last(c_rows, b_rows)
    square = jnp.zeros((length, PM), F32)
    for h in range(heads):
        span = slice(h * PM, (h + 1) * PM)
        cum_t, cum_s = cum[:, h : h + 1], cum_rows[h : h + 1, :]
        step_s, end = step_rows[h : h + 1, :], last[:, h : h + 1]
        decay = jnp.exp(jnp.where(causal, cum_t - cum_s, -1e30))
        mixing = (dots * decay * step_s).astype(BF16)
        x = x_ref[:, span]
        x_float = x.astype(F32)
        prior = state_ref[0, h]
        high, low = two_terms(prior)
        carried = contract_last(c_rows, high) + contract_last(c_rows, low)
        y = jnp.dot(mixing, x, preferred_element_type=F32)
        y = y + carried * jnp.exp(cum_t) + skip[h] * x_float
        z = z_ref[:, span].astype(F32)
        g = y * (z / (1.0 + jnp.exp(-z)))
        gated[:, span] = g
        square = square + g * g
        weighted = jnp.transpose(x_float) * (jnp.exp(end - cum_s) * step_s)
        high, low = two_terms(weighted)
        new = jnp.exp(end) * prior + (
            jnp.dot(high, b_rows, preferred_element_type=F32)
            + jnp.dot(low, b_rows, preferred_element_type=F32)
        )
        place = h % share

        @pl.when(u == h // share)
        def _():
            fresh[place] = new
            pltpu.make_async_copy(fresh.at[place], held.at[u, place], sems.at[place]).start()

        @pl.when(u != h // share)
        def _():
            send_ref[place] = new.astype(BF16)

    mean = jnp.sum(square, axis=1, keepdims=True) * (1.0 / (heads * PM))
    out = (gated[...] * lax.rsqrt(mean + norm_eps) * gain_ref[...]).astype(BF16)
    attn_width = attn_ref.shape[1]
    cut = stay_ref.shape[1] - attn_width
    for which, low_ref, high_ref in ((0, stay_ref, leave_ref), (1, leave_ref, stay_ref)):

        @pl.when(u == which)
        def _():
            low_ref[:, :attn_width] = attn_ref[...]
            low_ref[:, attn_width:] = out[:, :cut]
            high_ref[...] = out[:, cut:]

    for place in range(share):
        pltpu.make_async_copy(fresh.at[place], held.at[0, place], sems.at[place]).wait()


def state_space(unit, skip, attn, x, z, bc, dt, bias, rate, gain, state):
    length, width = x.shape
    share = MIXER_HEADS // 2
    half = (attn.shape[1] + width) // 2
    return pl.pallas_call(
        state_kernel,
        out_shape=(
            jax.ShapeDtypeStruct((length, half), BF16),
            jax.ShapeDtypeStruct((length, half), BF16),
            jax.ShapeDtypeStruct((2, share, PM, NS), F32),
            jax.ShapeDtypeStruct((share, PM, NS), BF16),
        ),
        in_specs=[SMEM, SMEM] + [VMEM] * 9,
        out_specs=(VMEM, VMEM, ANY, VMEM),
        scratch_shapes=[
            pltpu.VMEM((length, width), F32),
            pltpu.VMEM((share, PM, NS), F32),
            pltpu.SemaphoreType.DMA((share,)),
        ],
        compiler_params=PARAMS,
        cost_estimate=cost(4 << 30, 10 << 20, MIXER_HEADS * length * length * 2),
        name="state_space",
    )(unit, skip, attn, x, z, bc, dt, bias, rate, gain, state)


def settle_kernel(unit, pages, state, pages_in, state_in, pages_out, state_out, wide, sem):
    slots = pages.shape[0]
    u = unit[0]
    copy = pltpu.make_async_copy(pages, pages_out.at[pl.ds((1 - u) * slots, slots)], sem.at[0])
    copy.start()
    wide[...] = state[...].astype(F32)
    other = pltpu.make_async_copy(wide, state_out.at[1 - u], sem.at[1])
    other.start()
    copy.wait()
    other.wait()


def settle(unit, pages, state, pages_held, state_held):
    return pl.pallas_call(
        settle_kernel,
        out_shape=(
            jax.ShapeDtypeStruct(pages_held.shape, pages_held.dtype),
            jax.ShapeDtypeStruct(state_held.shape, state_held.dtype),
        ),
        in_specs=[SMEM, ANY, VMEM, ANY, ANY],
        out_specs=(ANY, ANY),
        scratch_shapes=[pltpu.VMEM(state.shape, F32), pltpu.SemaphoreType.DMA((2,))],
        input_output_aliases={3: 0, 4: 1},
        compiler_params=PARAMS,
        cost_estimate=cost(0, 5 << 20),
        name="settle",
    )(unit, pages, state, pages_held, state_held)


def spread_kernel(where, *refs):
    *sources, mine_ref, other_ref = refs
    half = sources[0].shape[1] // 2
    first = [s[:, :half] for s in sources]
    second = [s[:, half:] for s in sources]
    for which, low_ref, high_ref in ((0, mine_ref, other_ref), (1, other_ref, mine_ref)):

        @pl.when(where[1] == which)
        def _():
            low_ref[0] = jnp.concatenate(first, axis=1)
            high_ref[0] = jnp.concatenate(second, axis=1)


def spread(where, hidden, chip_rows, layers):
    rows = hidden.shape[0]
    half = layers * chip_rows // 2

    def block(req, d, k):
        layer, place = req // PLANE, req % PLANE
        source = ring_at((ring_place(layer, layers) + layers - k) % layers, layers)
        return source * PLANE + (place ^ d)

    if chip_rows % 128:
        low, high = [], []
        for d in range(PLANE):
            got = [
                lax.dynamic_slice(hidden, (0, block(where[0], d, k) * chip_rows), (rows, chip_rows))
                for k in range(layers)
            ]
            low.append(jnp.concatenate([x[:, : chip_rows // 2] for x in got], axis=1))
            high.append(jnp.concatenate([x[:, chip_rows // 2 :] for x in got], axis=1))
        low, high = jnp.stack(low), jnp.stack(high)
        return jnp.where(where[1] == 0, low, high), jnp.where(where[1] == 0, high, low)
    shape = jax.ShapeDtypeStruct((PLANE, rows, half), hidden.dtype)
    out_spec = pl.BlockSpec((1, rows, half), lambda d, _: (d, 0, 0))
    return pl.pallas_call(
        spread_kernel,
        out_shape=(shape, shape),
        grid_spec=pltpu.PrefetchScalarGridSpec(
            num_scalar_prefetch=1,
            grid=(PLANE,),
            in_specs=[
                pl.BlockSpec(
                    (rows, chip_rows), functools.partial(lambda k, d, w: (0, block(w[0], d, k)), k)
                )
                for k in range(layers)
            ],
            out_specs=(out_spec, out_spec),
        ),
        cost_estimate=cost(0, 4 << 20),
        name="spread",
    )(where, *([hidden] * layers))


def product_kernel(count, *refs):
    hidden, pieces, (keep_ref, send_ref, weight) = refs[:PLANE], refs[PLANE : PLANE + count], refs[-3:]
    block_rows = pieces[0].shape[0]
    for k, piece in enumerate(pieces):
        weight[k * block_rows : (k + 1) * block_rows, :] = piece[...]
    rows = keep_ref.shape[1]
    for d in range(PLANE):
        result = jnp.dot(hidden[d][...], weight[...], preferred_element_type=F32)
        keep_ref[d] = result[:rows].astype(keep_ref.dtype)
        send_ref[d] = result[rows:].astype(send_ref.dtype)


def product(hidden, pieces):
    rows, depth = hidden[0].shape
    width = pieces[0].shape[1]
    shape = jax.ShapeDtypeStruct((PLANE, rows // 2, width), BF16)
    return pl.pallas_call(
        functools.partial(product_kernel, len(pieces)),
        out_shape=(shape, shape),
        in_specs=[VMEM] * (PLANE + len(pieces)),
        out_specs=(VMEM, VMEM),
        scratch_shapes=[pltpu.VMEM((depth, width), BF16)],
        compiler_params=PARAMS,
        cost_estimate=cost(2 * PLANE * rows * depth * width, 6 << 20),
        name="product",
    )(*hidden, *pieces)


def swap_units(x):
    return lax.ppermute(x, "unit", [(0, 1), (1, 0)])


def after(x, *others):
    return lax.optimization_barrier((x, *others))[0]


def ring_at(step, length):
    if isinstance(step, int):
        return 2 * step - min(step, 1) if 2 * step <= length else 2 * (length - step)
    return jnp.where(2 * step <= length, 2 * step - jnp.minimum(step, 1), 2 * (length - step))


def ring_place(place, length):
    return jnp.where(place % 2 == 1, (place + 1) // 2, (length - place // 2) % length)


def chunk_edges(width):
    third = width // 3 // 128 * 128
    return [0, third, 2 * third, width]


def on_device(
    queries,
    kv_new,
    kv_pool,
    page_table,
    ctx_pages,
    ssm_x,
    ssm_z,
    ssm_bc,
    dt_raw,
    dt_bias,
    decay_rate,
    skip_gain,
    ssm_state,
    ssm_norm_gain,
    resid,
    out_weight,
    ffn_hidden,
    down_weight,
    page_owner,
):
    tok_rows = queries.shape[0]
    n_req = lax.axis_size("req")
    block_rows, width = down_weight.shape
    u = lax.axis_index("unit")
    unit = u.reshape(1)
    req = lax.axis_index("req")
    layers = n_req // PLANE

    ring = [ring_at(i, layers) for i in range(layers)]
    ring_pairs = [
        (ring[i] * PLANE + p, ring[(i + 1) % layers] * PLANE + p)
        for i in range(layers)
        for p in range(PLANE)
    ]

    def pass_on(x):
        return lax.ppermute(x, "req", ring_pairs)

    edges = chunk_edges(width)
    a, b, c = ([down_weight[:, lo:hi]] for lo, hi in zip(edges[:-1], edges[1:]))
    for chunk in (a, b, c):
        chunk.append(pass_on(chunk[-1]))

    where = jnp.stack([req, u])
    mine, other = spread(where, ffn_hidden, 2 * block_rows, layers)
    came = swap_units(other)

    def plane_swap(x, d):
        return lax.ppermute(
            x, "req", [(r, r - r % PLANE + ((r % PLANE) ^ d)) for r in range(n_req)]
        )

    attn, pages_held, pages_leave = attend(
        page_table, ctx_pages, page_owner[:, :, 0], unit, after(queries, mine), kv_new, kv_pool
    )
    a.append(pass_on(a[-1]))
    came = after(came, attn)
    hidden = [jnp.concatenate([mine[d], came[d]], axis=0) for d in range(PLANE)]
    hidden = [plane_swap(x, d) if d else x for d, x in enumerate(hidden)]

    stay, leave, state_held, state_leave = state_space(
        unit,
        skip_gain,
        after(attn, a[1]),
        ssm_x,
        ssm_z,
        ssm_bc,
        dt_raw,
        dt_bias[None, :],
        decay_rate[None, :],
        ssm_norm_gain[None, :],
        ssm_state,
    )
    b.append(pass_on(b[-1]))
    leave_came = swap_units(leave)
    pages_came = swap_units(pages_leave)
    state_came = swap_units(state_leave)
    exchanged = jnp.concatenate([after(stay, b[1]), leave_came], axis=0)
    mixed = jnp.dot(exchanged, out_weight, preferred_element_type=F32).astype(BF16)
    mixed_came = swap_units(mixed[tok_rows:])
    a.append(pass_on(a[-1]))
    pages_came = after(pages_came, a[2], mixed)
    decode_kv, decode_state = settle(unit, pages_came, state_came, pages_held, state_held)
    b.append(pass_on(b[-1]))
    for chunk in (a, b):
        while len(chunk) < layers:
            chunk.append(pass_on(chunk[-1]))

    def reduced(chunk):
        keep, send = product(hidden, chunk)
        total = keep.astype(F32) + swap_units(send).astype(F32)
        parts = [plane_swap(total[d].astype(BF16), d) for d in range(1, PLANE)]
        return total[0], parts

    sums = []
    sums.append(reduced(a))
    c.append(pass_on(after(c[-1], a[3])))
    sums.append(reduced(b))
    while len(c) < layers:
        c.append(pass_on(c[-1]))
    sums.append(reduced(c))
    outs = []
    for (lo, hi), (own, parts) in zip(zip(edges[:-1], edges[1:]), sums):
        total = own
        for part in parts:
            total = total + part.astype(F32)
        base = resid[:, lo:hi].astype(F32) + (
            mixed[:tok_rows, lo:hi].astype(F32) + mixed_came[:, lo:hi].astype(F32)
        )
        outs.append((base + total).astype(BF16))
    return (jnp.concatenate(outs, axis=1), decode_kv, decode_state)


def solution(mesh):
    return jax.shard_map(
        on_device,
        mesh=mesh,
        in_specs=(
            P(("req", "unit"), None),
            P(("req", "unit"), None),
            P(("req", "unit"), None, None),
            P(("req", "unit"), None),
            P(("req", "unit")),
            P(("req", "unit"), None),
            P(("req", "unit"), None),
            P(("req", "unit"), None),
            P(("req", "unit"), None),
            P(),
            P(),
            P(),
            P(("req", "unit"), None, None, None),
            P(),
            P(("req", "unit"), None),
            P("unit", None),
            P(("req", "unit"), None),
            P(("req", "unit"), None),
            P(("req", "unit"), None, None),
        ),
        out_specs=(
            P(("req", "unit"), None),
            P(("req", "unit"), None, None),
            P("req", "unit", None, None),
        ),
        check_vma=False,
    )
```

```python
import functools
import math

import jax
import jax.numpy as jnp
from jax import lax
from jax.experimental import pallas as pl
from jax.experimental.pallas import tpu as pltpu
from jax.sharding import PartitionSpec as P

QUERY_HEADS = 12
KEY_VALUE_HEADS = 2
HEAD_WIDTH = 128
MIXER_HEADS = 24
PM = 128
NS = 256

PLANE = 4

norm_eps = 1e-05

F32, BF16 = jnp.float32, jnp.bfloat16
VMEM = pl.BlockSpec(memory_space=pltpu.VMEM)
SMEM = pl.BlockSpec(memory_space=pltpu.SMEM)
ANY = pl.BlockSpec(memory_space=pl.ANY)
PARAMS = pltpu.CompilerParams(vmem_limit_bytes=48 * 1024 * 1024)


def cost(flops, moved, exps=0):
    return pl.CostEstimate(flops=flops, bytes_accessed=moved, transcendentals=exps)


def contract_last(a, b):
    return lax.dot_general(a, b, (((1,), (1,)), ((), ())), preferred_element_type=F32)


def two_terms(x):
    high = x.astype(BF16)
    return high, (x - high.astype(F32)).astype(BF16)


def attend_kernel(
    table, ctx, owner, unit, q_ref, new_ref, pool, out_ref, held, leave, pages, zero, sems, osems
):
    count, length, _ = pages.shape
    slots = leave.shape[0]
    live = ctx[0]
    u = unit[0]
    for j in range(count):

        @pl.when(j == live)
        def _():
            pltpu.make_async_copy(new_ref, pages.at[j], sems.at[j]).start()

        @pl.when(j != live)
        def _():
            pltpu.make_async_copy(pool.at[table[0, j]], pages.at[j], sems.at[j]).start()

    zero[...] = jnp.zeros_like(zero)
    for j in range(count):
        pltpu.make_async_copy(new_ref, pages.at[j], sems.at[j]).wait()

    named = [jnp.int32(0), jnp.int32(0)]
    for j in range(count):
        own = owner[0, j] == u
        rank = jnp.where(own, named[0], named[1])
        named = [named[0] + own.astype(jnp.int32), named[1] + 1 - own.astype(jnp.int32)]
        for source, when in ((pages.at[j], j <= live), (zero, j > live)):

            @pl.when(when & own)
            def _():
                pltpu.make_async_copy(source, held.at[u * slots + rank], osems.at[j]).start()

            @pl.when(when & jnp.logical_not(own))
            def _():
                pltpu.make_async_copy(source, leave.at[rank], osems.at[j]).start()

    for k in range(slots):

        @pl.when(k >= named[0])
        def _():
            pltpu.make_async_copy(zero, held.at[u * slots + k], osems.at[count + k]).start()

        @pl.when(k >= named[1])
        def _():
            pltpu.make_async_copy(zero, leave.at[k], osems.at[count + slots + k]).start()

    group = QUERY_HEADS // KEY_VALUE_HEADS
    heads = 3
    rows, keys = heads * length, count * length
    limit = live * length + lax.broadcasted_iota(jnp.int32, (rows, 1), 0) % length
    visible = lax.broadcasted_iota(jnp.int32, (rows, keys), 1) <= limit
    scale = 1.0 / math.sqrt(HEAD_WIDTH)
    for k in range(KEY_VALUE_HEADS):
        key_rows = pages[:, :, k * HEAD_WIDTH : (k + 1) * HEAD_WIDTH].reshape(keys, HEAD_WIDTH)
        lo = (KEY_VALUE_HEADS + k) * HEAD_WIDTH
        value_rows = pages[:, :, lo : lo + HEAD_WIDTH].reshape(keys, HEAD_WIDTH)
        for first in range(k * group, (k + 1) * group, heads):
            spans = [
                slice(h * HEAD_WIDTH, (h + 1) * HEAD_WIDTH) for h in range(first, first + heads)
            ]
            q = jnp.concatenate([q_ref[:, span] for span in spans], axis=0)
            scores = jnp.where(visible, contract_last(q, key_rows), -1e30)
            top = jnp.max(scores, axis=1, keepdims=True)
            exponent = jnp.exp((scores - top) * scale)
            weights = (exponent * (1.0 / jnp.sum(exponent, axis=1, keepdims=True))).astype(BF16)
            attended = jnp.dot(weights, value_rows, preferred_element_type=F32).astype(BF16)
            for i, span in enumerate(spans):
                out_ref[:, span] = attended[i * length : (i + 1) * length]

    for j in range(count):
        pltpu.make_async_copy(zero, leave.at[0], osems.at[j]).wait()
    for k in range(slots):

        @pl.when(k >= named[0])
        def _():
            pltpu.make_async_copy(zero, leave.at[0], osems.at[count + k]).wait()

        @pl.when(k >= named[1])
        def _():
            pltpu.make_async_copy(zero, leave.at[0], osems.at[count + slots + k]).wait()


def attend(table, ctx, owner, unit, queries, kv_new, pool):
    count, length, width = pool.shape
    slots = max(2, (count + 1) // 2)
    pairs = QUERY_HEADS * length * count * length
    return pl.pallas_call(
        attend_kernel,
        out_shape=(
            jax.ShapeDtypeStruct(queries.shape, BF16),
            jax.ShapeDtypeStruct((2 * slots, length, width), BF16),
            jax.ShapeDtypeStruct((slots, length, width), BF16),
        ),
        in_specs=[SMEM, SMEM, SMEM, SMEM, VMEM, VMEM, ANY],
        out_specs=(VMEM, ANY, ANY),
        scratch_shapes=[
            pltpu.VMEM((count, length, width), BF16),
            pltpu.VMEM((length, width), BF16),
            pltpu.SemaphoreType.DMA((count,)),
            pltpu.SemaphoreType.DMA((count + 2 * slots,)),
        ],
        compiler_params=PARAMS,
        cost_estimate=cost(4 * pairs * HEAD_WIDTH * 4, 6 << 20, pairs),
        name="attend",
    )(table, ctx, owner, unit, queries, kv_new, pool)


def state_kernel(
    unit,
    skip,
    attn_ref,
    x_ref,
    z_ref,
    bc_ref,
    dt_ref,
    bias_ref,
    rate_ref,
    gain_ref,
    state_ref,
    stay_ref,
    leave_ref,
    held,
    send_ref,
    gated,
    fresh,
    sems,
):
    length = x_ref.shape[0]
    heads, share = MIXER_HEADS, MIXER_HEADS // 2
    u = unit[0]
    rows = lax.broadcasted_iota(jnp.int32, (length, length), 0)
    cols = lax.broadcasted_iota(jnp.int32, (length, length), 1)
    causal = rows >= cols
    raw = dt_ref[...] + bias_ref[...]
    step = jnp.maximum(raw, 0.0) + jnp.log1p(jnp.exp(-jnp.abs(raw)))
    cum = jnp.dot(
        causal.astype(F32),
        -step * rate_ref[...],
        precision=lax.Precision.HIGHEST,
        preferred_element_type=F32,
    )
    blank = jnp.zeros((length, length - heads), F32)
    cum_rows = jnp.transpose(jnp.concatenate([cum, blank], axis=1))
    step_rows = jnp.transpose(jnp.concatenate([step, blank], axis=1))
    last = cum[length - 1 : length, :]
    b_rows, c_rows = bc_ref[:, :NS], bc_ref[:, NS:]
    dots = contract_last(c_rows, b_rows)
    square = jnp.zeros((length, PM), F32)
    for h in range(heads):
        span = slice(h * PM, (h + 1) * PM)
        cum_t, cum_s = cum[:, h : h + 1], cum_rows[h : h + 1, :]
        step_s, end = step_rows[h : h + 1, :], last[:, h : h + 1]
        decay = jnp.exp(jnp.where(causal, cum_t - cum_s, -1e30))
        mixing = (dots * decay * step_s).astype(BF16)
        x = x_ref[:, span]
        x_float = x.astype(F32)
        prior = state_ref[0, h]
        high, low = two_terms(prior)
        carried = contract_last(c_rows, high) + contract_last(c_rows, low)
        y = jnp.dot(mixing, x, preferred_element_type=F32)
        y = y + carried * jnp.exp(cum_t) + skip[h] * x_float
        z = z_ref[:, span].astype(F32)
        g = y * (z / (1.0 + jnp.exp(-z)))
        gated[:, span] = g
        square = square + g * g
        weighted = jnp.transpose(x_float) * (jnp.exp(end - cum_s) * step_s)
        high, low = two_terms(weighted)
        new = jnp.exp(end) * prior + (
            jnp.dot(high, b_rows, preferred_element_type=F32)
            + jnp.dot(low, b_rows, preferred_element_type=F32)
        )
        place = h % share

        @pl.when(u == h // share)
        def _():
            fresh[place] = new
            pltpu.make_async_copy(fresh.at[place], held.at[u, place], sems.at[place]).start()

        @pl.when(u != h // share)
        def _():
            send_ref[place] = new.astype(BF16)

    mean = jnp.sum(square, axis=1, keepdims=True) * (1.0 / (heads * PM))
    out = (gated[...] * lax.rsqrt(mean + norm_eps) * gain_ref[...]).astype(BF16)
    attn_width = attn_ref.shape[1]
    cut = stay_ref.shape[1] - attn_width
    for which, low_ref, high_ref in ((0, stay_ref, leave_ref), (1, leave_ref, stay_ref)):

        @pl.when(u == which)
        def _():
            low_ref[:, :attn_width] = attn_ref[...]
            low_ref[:, attn_width:] = out[:, :cut]
            high_ref[...] = out[:, cut:]

    for place in range(share):
        pltpu.make_async_copy(fresh.at[place], held.at[0, place], sems.at[place]).wait()


def state_space(unit, skip, attn, x, z, bc, dt, bias, rate, gain, state):
    length, width = x.shape
    share = MIXER_HEADS // 2
    half = (attn.shape[1] + width) // 2
    return pl.pallas_call(
        state_kernel,
        out_shape=(
            jax.ShapeDtypeStruct((length, half), BF16),
            jax.ShapeDtypeStruct((length, half), BF16),
            jax.ShapeDtypeStruct((2, share, PM, NS), F32),
            jax.ShapeDtypeStruct((share, PM, NS), BF16),
        ),
        in_specs=[SMEM, SMEM] + [VMEM] * 9,
        out_specs=(VMEM, VMEM, ANY, VMEM),
        scratch_shapes=[
            pltpu.VMEM((length, width), F32),
            pltpu.VMEM((share, PM, NS), F32),
            pltpu.SemaphoreType.DMA((share,)),
        ],
        compiler_params=PARAMS,
        cost_estimate=cost(4 << 30, 10 << 20, MIXER_HEADS * length * length * 2),
        name="state_space",
    )(unit, skip, attn, x, z, bc, dt, bias, rate, gain, state)


def settle_kernel(
    unit, pages, state, pages_in, state_in, rows_in, pages_out, state_out, rows_out, wide, sem
):
    slots = pages.shape[0]
    u = unit[0]
    copy = pltpu.make_async_copy(pages, pages_out.at[pl.ds((1 - u) * slots, slots)], sem.at[0])
    copy.start()
    wide[...] = state[...].astype(F32)
    other = pltpu.make_async_copy(wide, state_out.at[1 - u], sem.at[1])
    other.start()
    copy.wait()
    other.wait()


def settle(unit, pages, state, pages_held, state_held, rows):
    return pl.pallas_call(
        settle_kernel,
        out_shape=tuple(
            jax.ShapeDtypeStruct(x.shape, x.dtype) for x in (pages_held, state_held, rows)
        ),
        in_specs=[SMEM, ANY, VMEM, ANY, ANY, ANY],
        out_specs=(ANY, ANY, ANY),
        scratch_shapes=[pltpu.VMEM(state.shape, F32), pltpu.SemaphoreType.DMA((2,))],
        input_output_aliases={3: 0, 4: 1, 5: 2},
        compiler_params=PARAMS,
        cost_estimate=cost(0, 5 << 20),
        name="settle",
    )(unit, pages, state, pages_held, state_held, rows)


def spread_kernel(where, *refs):
    *sources, mine_ref, other_ref = refs
    half = sources[0].shape[1] // 2
    first = [s[:, :half] for s in sources]
    second = [s[:, half:] for s in sources]
    for which, low_ref, high_ref in ((0, mine_ref, other_ref), (1, other_ref, mine_ref)):

        @pl.when(where[1] == which)
        def _():
            low_ref[0] = jnp.concatenate(first, axis=1)
            high_ref[0] = jnp.concatenate(second, axis=1)


def spread(where, hidden, chip_rows, layers):
    rows = hidden.shape[0]
    half = layers * chip_rows // 2

    def block(req, d, k):
        layer, place = req // PLANE, req % PLANE
        source = ring_at((ring_place(layer, layers) + layers - k) % layers, layers)
        return source * PLANE + (place ^ d)

    if chip_rows % 128:
        low, high = [], []
        for d in range(PLANE):
            got = [
                lax.dynamic_slice(hidden, (0, block(where[0], d, k) * chip_rows), (rows, chip_rows))
                for k in range(layers)
            ]
            low.append(jnp.concatenate([x[:, : chip_rows // 2] for x in got], axis=1))
            high.append(jnp.concatenate([x[:, chip_rows // 2 :] for x in got], axis=1))
        low, high = jnp.stack(low), jnp.stack(high)
        return jnp.where(where[1] == 0, low, high), jnp.where(where[1] == 0, high, low)
    shape = jax.ShapeDtypeStruct((PLANE, rows, half), hidden.dtype)
    out_spec = pl.BlockSpec((1, rows, half), lambda d, _: (d, 0, 0))
    return pl.pallas_call(
        spread_kernel,
        out_shape=(shape, shape),
        grid_spec=pltpu.PrefetchScalarGridSpec(
            num_scalar_prefetch=1,
            grid=(PLANE,),
            in_specs=[
                pl.BlockSpec(
                    (rows, chip_rows), functools.partial(lambda k, d, w: (0, block(w[0], d, k)), k)
                )
                for k in range(layers)
            ],
            out_specs=(out_spec, out_spec),
        ),
        cost_estimate=cost(0, 4 << 20),
        name="spread",
    )(where, *([hidden] * layers))


def product_kernel(count, *refs):
    hidden, pieces, (keep_ref, send_ref, weight) = refs[:PLANE], refs[PLANE : PLANE + count], refs[-3:]
    block_rows = pieces[0].shape[0]
    for k, piece in enumerate(pieces):
        weight[k * block_rows : (k + 1) * block_rows, :] = piece[...]
    rows = keep_ref.shape[1]
    for d in range(PLANE):
        result = jnp.dot(hidden[d][...], weight[...], preferred_element_type=F32)
        keep_ref[d] = result[:rows].astype(keep_ref.dtype)
        send_ref[d] = result[rows:].astype(send_ref.dtype)


def product(hidden, pieces):
    rows, depth = hidden[0].shape
    width = pieces[0].shape[1]
    shape = jax.ShapeDtypeStruct((PLANE, rows // 2, width), BF16)
    return pl.pallas_call(
        functools.partial(product_kernel, len(pieces)),
        out_shape=(shape, shape),
        in_specs=[VMEM] * (PLANE + len(pieces)),
        out_specs=(VMEM, VMEM),
        scratch_shapes=[pltpu.VMEM((depth, width), BF16)],
        compiler_params=PARAMS,
        cost_estimate=cost(2 * PLANE * rows * depth * width, 6 << 20),
        name="product",
    )(*hidden, *pieces)


def swap_units(x):
    return lax.ppermute(x, "unit", [(0, 1), (1, 0)])


def after(x, *others):
    return lax.optimization_barrier((x, *others))[0]


def ring_at(step, length):
    if isinstance(step, int):
        return 2 * step - min(step, 1) if 2 * step <= length else 2 * (length - step)
    return jnp.where(2 * step <= length, 2 * step - jnp.minimum(step, 1), 2 * (length - step))


def ring_place(place, length):
    return jnp.where(place % 2 == 1, (place + 1) // 2, (length - place // 2) % length)


def chunk_edges(width):
    third = width // 3 // 128 * 128
    return [0, third, 2 * third, width]


def on_device(
    queries,
    kv_new,
    kv_pool,
    page_table,
    ctx_pages,
    ssm_x,
    ssm_z,
    ssm_bc,
    dt_raw,
    dt_bias,
    decay_rate,
    skip_gain,
    ssm_state,
    ssm_norm_gain,
    resid,
    out_weight,
    ffn_hidden,
    down_weight,
    page_owner,
):
    tok_rows = queries.shape[0]
    n_req = lax.axis_size("req")
    block_rows, width = down_weight.shape
    u = lax.axis_index("unit")
    unit = u.reshape(1)
    req = lax.axis_index("req")
    layers = n_req // PLANE

    ring = [ring_at(i, layers) for i in range(layers)]
    ring_pairs = [
        (ring[i] * PLANE + p, ring[(i + 1) % layers] * PLANE + p)
        for i in range(layers)
        for p in range(PLANE)
    ]

    def pass_on(x):
        return lax.ppermute(x, "req", ring_pairs)

    edges = chunk_edges(width)
    a, b, c = ([down_weight[:, lo:hi]] for lo, hi in zip(edges[:-1], edges[1:]))
    started = [a[0], b[0], c[0]]
    for chunk in (a, b, c):
        chunk.append(pass_on(chunk[-1]))

    def go_round(chunk, *others):
        chunk.append(pass_on(after(chunk[-1], *others)))

    where = jnp.stack([req, u])
    mine, other = spread(where, after(ffn_hidden, *started), 2 * block_rows, layers)
    attn, pages_held, pages_leave = attend(
        page_table, ctx_pages, page_owner[:, :, 0], unit, after(queries, mine), kv_new, kv_pool
    )
    came = swap_units(after(other, a[1], b[1], c[1], attn))

    def plane_swap(x, d):
        return lax.ppermute(
            x, "req", [(r, r - r % PLANE + ((r % PLANE) ^ d)) for r in range(n_req)]
        )

    go_round(a, attn)
    go_round(b, attn)
    hidden = [jnp.concatenate([mine[d], came[d]], axis=0) for d in range(PLANE)]
    stay, leave, state_held, state_leave = state_space(
        unit,
        skip_gain,
        after(attn, *hidden),
        ssm_x,
        ssm_z,
        ssm_bc,
        dt_raw,
        dt_bias[None, :],
        decay_rate[None, :],
        ssm_norm_gain[None, :],
        ssm_state,
    )
    hidden = [plane_swap(x, d) if d else x for d, x in enumerate(hidden)]
    leave, state_leave, pages_leave = after(
        (leave, state_leave, pages_leave), a[2], b[2], *hidden[1:]
    )
    go_round(a, stay)
    go_round(b, stay)
    leave_came = swap_units(leave)
    pages_came = swap_units(pages_leave)
    state_came = swap_units(state_leave)
    decode_kv, decode_state, stay = settle(
        unit, pages_came, state_came, pages_held, state_held, stay
    )
    exchanged = jnp.concatenate([stay, leave_came], axis=0)
    mixed = jnp.dot(exchanged, out_weight, preferred_element_type=F32).astype(BF16)
    mixed_came = swap_units(mixed[tok_rows:])
    for chunk in (a, b):
        while len(chunk) < layers:
            go_round(chunk)

    def half_sums(chunk, then, *others):
        keep, send = product(hidden, chunk[:-1] + [after(chunk[-1], *others)])
        return keep, swap_units(after(send, *then))

    def summed(keep, came):
        total = keep.astype(F32) + came.astype(F32)
        return total[0], [total[d].astype(BF16) for d in range(1, PLANE)]

    def gathered(own, parts):
        return [own] + [plane_swap(x, d) for d, x in enumerate(parts, 1)]

    keep_a, came_a = half_sums(a, b[-1:], mixed)
    go_round(c, b[-1])
    sum_a = summed(keep_a, came_a)
    keep_b, came_b = half_sums(b, c[-1:], *sum_a[1])
    sum_a = gathered(*sum_a)
    while len(c) < layers:
        go_round(c)
    came_b = after(came_b, *sum_a)
    sum_b = gathered(*summed(keep_b, came_b))
    sum_c = gathered(*summed(*half_sums(c, (), came_b)))
    outs = []
    for lo, hi, parts in zip(edges[:-1], edges[1:], (sum_a, sum_b, sum_c)):
        total = parts[0]
        for part in parts[1:]:
            total = total + part.astype(F32)
        base = resid[:, lo:hi].astype(F32) + (
            mixed[:tok_rows, lo:hi].astype(F32) + mixed_came[:, lo:hi].astype(F32)
        )
        outs.append((base + total).astype(BF16))
    return (jnp.concatenate(outs, axis=1), decode_kv, decode_state)


def solution(mesh):
    return jax.shard_map(
        on_device,
        mesh=mesh,
        in_specs=(
            P(("req", "unit"), None),
            P(("req", "unit"), None),
            P(("req", "unit"), None, None),
            P(("req", "unit"), None),
            P(("req", "unit")),
            P(("req", "unit"), None),
            P(("req", "unit"), None),
            P(("req", "unit"), None),
            P(("req", "unit"), None),
            P(),
            P(),
            P(),
            P(("req", "unit"), None, None, None),
            P(),
            P(("req", "unit"), None),
            P("unit", None),
            P(("req", "unit"), None),
            P(("req", "unit"), None),
            P(("req", "unit"), None, None),
        ),
        out_specs=(
            P(("req", "unit"), None),
            P(("req", "unit"), None, None),
            P("req", "unit", None, None),
        ),
        check_vma=False,
    )
```

```python
import functools
import math

import jax
import jax.numpy as jnp
from jax import lax
from jax.experimental import pallas as pl
from jax.experimental.pallas import tpu as pltpu
from jax.sharding import PartitionSpec as P

QUERY_HEADS = 12
KEY_VALUE_HEADS = 2
HEAD_WIDTH = 128
MIXER_HEADS = 24
PM = 128
NS = 256

PLANE = 4

norm_eps = 1e-05

F32, BF16 = jnp.float32, jnp.bfloat16
VMEM = pl.BlockSpec(memory_space=pltpu.VMEM)
SMEM = pl.BlockSpec(memory_space=pltpu.SMEM)
ANY = pl.BlockSpec(memory_space=pl.ANY)
PARAMS = pltpu.CompilerParams(vmem_limit_bytes=48 * 1024 * 1024)


def cost(flops, moved, exps=0):
    return pl.CostEstimate(flops=0, bytes_accessed=0, transcendentals=0)


def contract_last(a, b):
    return lax.dot_general(a, b, (((1,), (1,)), ((), ())), preferred_element_type=F32)


def two_terms(x):
    high = x.astype(BF16)
    return high, (x - high.astype(F32)).astype(BF16)


def attend_kernel(
    table, ctx, owner, unit, q_ref, new_ref, pool, out_ref, held, leave, pages, zero, sems, osems
):
    count, length, _ = pages.shape
    slots = leave.shape[0]
    live = ctx[0]
    u = unit[0]
    for j in range(count):

        @pl.when(j == live)
        def _():
            pltpu.make_async_copy(new_ref, pages.at[j], sems.at[j]).start()

        @pl.when(j != live)
        def _():
            pltpu.make_async_copy(pool.at[table[0, j]], pages.at[j], sems.at[j]).start()

    zero[...] = jnp.zeros_like(zero)
    for j in range(count):
        pltpu.make_async_copy(new_ref, pages.at[j], sems.at[j]).wait()

    named = [jnp.int32(0), jnp.int32(0)]
    for j in range(count):
        own = owner[0, j] == u
        rank = jnp.where(own, named[0], named[1])
        named = [named[0] + own.astype(jnp.int32), named[1] + 1 - own.astype(jnp.int32)]
        for source, when in ((pages.at[j], j <= live), (zero, j > live)):

            @pl.when(when & own)
            def _():
                pltpu.make_async_copy(source, held.at[u * slots + rank], osems.at[j]).start()

            @pl.when(when & jnp.logical_not(own))
            def _():
                pltpu.make_async_copy(source, leave.at[rank], osems.at[j]).start()

    for k in range(slots):

        @pl.when(k >= named[0])
        def _():
            pltpu.make_async_copy(zero, held.at[u * slots + k], osems.at[count + k]).start()

        @pl.when(k >= named[1])
        def _():
            pltpu.make_async_copy(zero, leave.at[k], osems.at[count + slots + k]).start()

    group = QUERY_HEADS // KEY_VALUE_HEADS
    heads = 3
    rows, keys = heads * length, count * length
    limit = live * length + lax.broadcasted_iota(jnp.int32, (rows, 1), 0) % length
    visible = lax.broadcasted_iota(jnp.int32, (rows, keys), 1) <= limit
    scale = 1.0 / math.sqrt(HEAD_WIDTH)
    for k in range(KEY_VALUE_HEADS):
        key_rows = pages[:, :, k * HEAD_WIDTH : (k + 1) * HEAD_WIDTH].reshape(keys, HEAD_WIDTH)
        lo = (KEY_VALUE_HEADS + k) * HEAD_WIDTH
        value_rows = pages[:, :, lo : lo + HEAD_WIDTH].reshape(keys, HEAD_WIDTH)
        for first in range(k * group, (k + 1) * group, heads):
            spans = [
                slice(h * HEAD_WIDTH, (h + 1) * HEAD_WIDTH) for h in range(first, first + heads)
            ]
            q = jnp.concatenate([q_ref[:, span] for span in spans], axis=0)
            scores = jnp.where(visible, contract_last(q, key_rows), -1e30)
            top = jnp.max(scores, axis=1, keepdims=True)
            exponent = jnp.exp((scores - top) * scale)
            weights = (exponent * (1.0 / jnp.sum(exponent, axis=1, keepdims=True))).astype(BF16)
            attended = jnp.dot(weights, value_rows, preferred_element_type=F32).astype(BF16)
            for i, span in enumerate(spans):
                out_ref[:, span] = attended[i * length : (i + 1) * length]

    for j in range(count):
        pltpu.make_async_copy(zero, leave.at[0], osems.at[j]).wait()
    for k in range(slots):

        @pl.when(k >= named[0])
        def _():
            pltpu.make_async_copy(zero, leave.at[0], osems.at[count + k]).wait()

        @pl.when(k >= named[1])
        def _():
            pltpu.make_async_copy(zero, leave.at[0], osems.at[count + slots + k]).wait()


def attend(table, ctx, owner, unit, queries, kv_new, pool):
    count, length, width = pool.shape
    slots = max(2, (count + 1) // 2)
    pairs = QUERY_HEADS * length * count * length
    return pl.pallas_call(
        attend_kernel,
        out_shape=(
            jax.ShapeDtypeStruct(queries.shape, BF16),
            jax.ShapeDtypeStruct((2 * slots, length, width), BF16),
            jax.ShapeDtypeStruct((slots, length, width), BF16),
        ),
        in_specs=[SMEM, SMEM, SMEM, SMEM, VMEM, VMEM, ANY],
        out_specs=(VMEM, ANY, ANY),
        scratch_shapes=[
            pltpu.VMEM((count, length, width), BF16),
            pltpu.VMEM((length, width), BF16),
            pltpu.SemaphoreType.DMA((count,)),
            pltpu.SemaphoreType.DMA((count + 2 * slots,)),
        ],
        compiler_params=PARAMS,
        cost_estimate=cost(4 * pairs * HEAD_WIDTH * 4, 6 << 20, pairs),
        name="attend",
    )(table, ctx, owner, unit, queries, kv_new, pool)


def state_kernel(
    unit,
    skip,
    attn_ref,
    x_ref,
    z_ref,
    bc_ref,
    dt_ref,
    bias_ref,
    rate_ref,
    gain_ref,
    state_ref,
    stay_ref,
    leave_a,
    leave_b,
    held,
    send_ref,
    gated,
    fresh,
    sems,
):
    length = x_ref.shape[0]
    heads, share = MIXER_HEADS, MIXER_HEADS // 2
    u = unit[0]
    rows = lax.broadcasted_iota(jnp.int32, (length, length), 0)
    cols = lax.broadcasted_iota(jnp.int32, (length, length), 1)
    causal = rows >= cols
    raw = dt_ref[...] + bias_ref[...]
    step = jnp.maximum(raw, 0.0) + jnp.log1p(jnp.exp(-jnp.abs(raw)))
    cum = jnp.dot(
        causal.astype(F32),
        -step * rate_ref[...],
        precision=lax.Precision.HIGHEST,
        preferred_element_type=F32,
    )
    blank = jnp.zeros((length, length - heads), F32)
    cum_rows = jnp.transpose(jnp.concatenate([cum, blank], axis=1))
    step_rows = jnp.transpose(jnp.concatenate([step, blank], axis=1))
    last = cum[length - 1 : length, :]
    b_rows, c_rows = bc_ref[:, :NS], bc_ref[:, NS:]
    dots = contract_last(c_rows, b_rows)
    square = jnp.zeros((length, PM), F32)
    for h in range(heads):
        span = slice(h * PM, (h + 1) * PM)
        cum_t, cum_s = cum[:, h : h + 1], cum_rows[h : h + 1, :]
        step_s, end = step_rows[h : h + 1, :], last[:, h : h + 1]
        decay = jnp.exp(jnp.where(causal, cum_t - cum_s, -1e30))
        mixing = (dots * decay * step_s).astype(BF16)
        x = x_ref[:, span]
        x_float = x.astype(F32)
        prior = state_ref[0, h]
        high, low = two_terms(prior)
        carried = contract_last(c_rows, high) + contract_last(c_rows, low)
        y = jnp.dot(mixing, x, preferred_element_type=F32)
        y = y + carried * jnp.exp(cum_t) + skip[h] * x_float
        z = z_ref[:, span].astype(F32)
        g = y * (z / (1.0 + jnp.exp(-z)))
        gated[:, span] = g
        square = square + g * g
        weighted = jnp.transpose(x_float) * (jnp.exp(end - cum_s) * step_s)
        high, low = two_terms(weighted)
        new = jnp.exp(end) * prior + (
            jnp.dot(high, b_rows, preferred_element_type=F32)
            + jnp.dot(low, b_rows, preferred_element_type=F32)
        )
        place = h % share

        @pl.when(u == h // share)
        def _():
            fresh[place] = new
            pltpu.make_async_copy(fresh.at[place], held.at[u, place], sems.at[place]).start()

        @pl.when(u != h // share)
        def _():
            send_ref[place] = new.astype(BF16)

    mean = jnp.sum(square, axis=1, keepdims=True) * (1.0 / (heads * PM))
    out = (gated[...] * lax.rsqrt(mean + norm_eps) * gain_ref[...]).astype(BF16)
    attn_width = attn_ref.shape[1]
    cut = stay_ref.shape[1] - attn_width
    part = leave_a.shape[1]

    @pl.when(u == 0)
    def _():
        stay_ref[:, :attn_width] = attn_ref[...]
        stay_ref[:, attn_width:] = out[:, :cut]
        leave_a[...] = out[:, cut : cut + part]
        leave_b[...] = out[:, cut + part :]

    @pl.when(u == 1)
    def _():
        stay_ref[...] = out[:, cut:]
        leave_a[...] = attn_ref[:, :part]
        leave_b[:, : attn_width - part] = attn_ref[:, part:]
        leave_b[:, attn_width - part :] = out[:, :cut]

    for place in range(share):
        pltpu.make_async_copy(fresh.at[place], held.at[0, place], sems.at[place]).wait()


def state_space(unit, skip, attn, x, z, bc, dt, bias, rate, gain, state):
    length, width = x.shape
    share = MIXER_HEADS // 2
    half = (attn.shape[1] + width) // 2
    return pl.pallas_call(
        state_kernel,
        out_shape=(
            jax.ShapeDtypeStruct((length, half), BF16),
            jax.ShapeDtypeStruct((length, half // 2), BF16),
            jax.ShapeDtypeStruct((length, half - half // 2), BF16),
            jax.ShapeDtypeStruct((2, share, PM, NS), F32),
            jax.ShapeDtypeStruct((share, PM, NS), BF16),
        ),
        in_specs=[SMEM, SMEM] + [VMEM] * 9,
        out_specs=(VMEM, VMEM, VMEM, ANY, VMEM),
        scratch_shapes=[
            pltpu.VMEM((length, width), F32),
            pltpu.VMEM((share, PM, NS), F32),
            pltpu.SemaphoreType.DMA((share,)),
        ],
        compiler_params=PARAMS,
        cost_estimate=cost(4 << 30, 10 << 20, MIXER_HEADS * length * length * 2),
        name="state_space",
    )(unit, skip, attn, x, z, bc, dt, bias, rate, gain, state)


def settle_kernel(
    unit, pages, state, pages_in, state_in, rows_in, pages_out, state_out, rows_out, wide, sem
):
    slots = pages.shape[0]
    u = unit[0]
    copy = pltpu.make_async_copy(pages, pages_out.at[pl.ds((1 - u) * slots, slots)], sem.at[0])
    copy.start()
    wide[...] = state[...].astype(F32)
    other = pltpu.make_async_copy(wide, state_out.at[1 - u], sem.at[1])
    other.start()
    copy.wait()
    other.wait()


def settle(unit, pages, state, pages_held, state_held, rows):
    return pl.pallas_call(
        settle_kernel,
        out_shape=tuple(
            jax.ShapeDtypeStruct(x.shape, x.dtype) for x in (pages_held, state_held, rows)
        ),
        in_specs=[SMEM, ANY, VMEM, ANY, ANY, ANY],
        out_specs=(ANY, ANY, ANY),
        scratch_shapes=[pltpu.VMEM(state.shape, F32), pltpu.SemaphoreType.DMA((2,))],
        input_output_aliases={3: 0, 4: 1, 5: 2},
        compiler_params=PARAMS,
        cost_estimate=cost(0, 5 << 20),
        name="settle",
    )(unit, pages, state, pages_held, state_held, rows)


def cut_kernel(unit, weight_ref, *refs):
    count = len(refs) // 2
    kept, sent = refs[:count], refs[count:]
    half = weight_ref.shape[1] // 2
    for u in range(2):

        @pl.when(unit[0] == u)
        def _():
            for outs, base in ((kept, u * half), (sent, (1 - u) * half)):
                for out in outs:
                    out[...] = weight_ref[:, base : base + out.shape[1]]
                    base += out.shape[1]


def cut(unit, weight, widths):
    rows = weight.shape[0]
    outs = pl.pallas_call(
        cut_kernel,
        out_shape=tuple(jax.ShapeDtypeStruct((rows, w), weight.dtype) for w in widths * 2),
        in_specs=[SMEM, VMEM],
        out_specs=(VMEM,) * (2 * len(widths)),
        compiler_params=PARAMS,
        cost_estimate=cost(0, 3 << 20),
        name="cut",
    )(unit, weight)
    return outs[: len(widths)], outs[len(widths) :]


def block_of(req, d, k, layers):
    layer, place = req // PLANE, req % PLANE
    source = ring_at((ring_place(layer, layers) + layers - k) % layers, layers)
    return source * PLANE + (place ^ d)


def spread_kernel(req, hidden, *refs):
    outs, sem = refs[:-1], refs[-1]
    rows, depth = outs[0].shape
    layers = sem.shape[0] // PLANE
    chip_rows = depth // layers
    copies = []
    for d in range(PLANE):
        for k in range(layers):
            column = pl.multiple_of(chip_rows * block_of(req[0], d, k, layers), 128)
            copies.append(
                pltpu.make_async_copy(
                    hidden.at[:, pl.ds(column, chip_rows)],
                    outs[d].at[:, k * chip_rows : (k + 1) * chip_rows],
                    sem.at[d * layers + k],
                )
            )
    for copy in copies:
        copy.start()
    for copy in copies:
        copy.wait()


def spread(req, hidden, chip_rows, layers):
    rows = hidden.shape[0]
    if chip_rows % 128:
        return [
            jnp.concatenate(
                [
                    lax.dynamic_slice(
                        hidden, (0, block_of(req[0], d, k, layers) * chip_rows), (rows, chip_rows)
                    )
                    for k in range(layers)
                ],
                axis=1,
            )
            for d in range(PLANE)
        ]
    return pl.pallas_call(
        spread_kernel,
        out_shape=(jax.ShapeDtypeStruct((rows, layers * chip_rows), hidden.dtype),) * PLANE,
        in_specs=[SMEM, ANY],
        out_specs=(VMEM,) * PLANE,
        scratch_shapes=[pltpu.SemaphoreType.DMA((PLANE * layers,))],
        compiler_params=PARAMS,
        cost_estimate=cost(0, 4 << 20),
        name="spread",
    )(req, hidden)


def product_kernel(count, low, unit, *refs):
    hidden, pieces = refs[: PLANE + 1], refs[PLANE + 1 : PLANE + 1 + count]
    own_ref, *parts = refs[PLANE + 1 + count : -1]
    weight = refs[-1]
    block_rows = pieces[0].shape[0] // 2
    u = unit[0]
    for k, piece in enumerate(pieces):
        for which, place in ((0, u), (1, 1 - u)):
            at = pl.multiple_of((2 * k + place) * block_rows, 16)
            rows = slice(which * block_rows, (which + 1) * block_rows)
            base = low if piece.shape[1] > weight.shape[1] else 0
            weight[pl.ds(at, block_rows), :] = piece[rows, base : base + weight.shape[1]]
    rows = hidden[0].shape[0]
    for d in range(PLANE):
        other = hidden[-1][d * rows : (d + 1) * rows, :]
        both = jnp.concatenate([hidden[d][...], other], axis=0)
        result = jnp.dot(both, weight[...], preferred_element_type=F32)
        if d:
            parts[d - 1][...] = result.astype(BF16)
        else:
            own_ref[...] = result


def product(unit, hidden, pieces, low=0):
    rows, depth = hidden[0].shape
    width = pieces[-1].shape[1]
    outs = pl.pallas_call(
        functools.partial(product_kernel, len(pieces), low),
        out_shape=(jax.ShapeDtypeStruct((2 * rows, width), F32),)
        + (jax.ShapeDtypeStruct((2 * rows, width), BF16),) * (PLANE - 1),
        in_specs=[SMEM] + [VMEM] * (PLANE + 1 + len(pieces)),
        out_specs=(VMEM,) * PLANE,
        scratch_shapes=[pltpu.VMEM((depth, width), BF16)],
        compiler_params=PARAMS,
        cost_estimate=cost(0, 6 << 20),
        name="product",
    )(unit, *hidden, *pieces)
    return outs[0], outs[1:]


def total_kernel(own_ref, *refs):
    came, (keep_ref, send_ref) = refs[:-2], refs[-2:]
    total = own_ref[...]
    for ref in came:
        total = total + ref[...].astype(F32)
    rows = keep_ref.shape[0]
    keep_ref[...] = total[:rows]
    send_ref[...] = total[rows:].astype(BF16)


def total(own, came):
    rows, width = own.shape
    return pl.pallas_call(
        total_kernel,
        out_shape=(
            jax.ShapeDtypeStruct((rows // 2, width), F32),
            jax.ShapeDtypeStruct((rows // 2, width), BF16),
        ),
        in_specs=[VMEM] * (1 + len(came)),
        out_specs=(VMEM, VMEM),
        compiler_params=PARAMS,
        cost_estimate=cost(0, 4 << 20),
        name="total",
    )(own, *came)


def finish_kernel(unit, resid_ref, mixed_ref, mixed_came_ref, *refs):
    count = len(refs) // 2
    kept, came, out_ref = refs[:count], refs[count:-1], refs[-1]
    half = out_ref.shape[1] // 2
    for u in range(2):

        @pl.when(unit[0] == u)
        def _():
            for group, base in ((kept, u * half), (came, (1 - u) * half)):
                for ref in group:
                    span = slice(base, base + ref.shape[1])
                    mixed = mixed_ref[:, span].astype(F32) + mixed_came_ref[:, span].astype(F32)
                    sums = resid_ref[:, span].astype(F32) + mixed + ref[...].astype(F32)
                    out_ref[:, span] = sums.astype(BF16)
                    base += ref.shape[1]


def finish(unit, resid, mixed, mixed_came, kept, came):
    return pl.pallas_call(
        finish_kernel,
        out_shape=jax.ShapeDtypeStruct(resid.shape, BF16),
        in_specs=[SMEM] + [VMEM] * (3 + len(kept) + len(came)),
        out_specs=VMEM,
        compiler_params=PARAMS,
        cost_estimate=cost(0, 4 << 20),
        name="finish",
    )(unit, resid, mixed, mixed_came, *kept, *came)


def project_kernel(stay_ref, a_ref, b_ref, weight_ref, keep_ref, send_ref):
    rows = stay_ref.shape[0]
    came = jnp.concatenate([a_ref[...], b_ref[...]], axis=1)
    both = jnp.concatenate([stay_ref[...], came], axis=0)
    result = jnp.dot(both, weight_ref[...], preferred_element_type=F32).astype(BF16)
    keep_ref[...] = result[:rows]
    send_ref[...] = result[rows:]


def project(stay, came_a, came_b, weight):
    rows, depth = stay.shape
    width = weight.shape[1]
    tile = 512 if width % 512 == 0 else width
    fixed = [pl.BlockSpec(x.shape, lambda i: (0, 0)) for x in (stay, came_a, came_b)]
    out_spec = pl.BlockSpec((rows, tile), lambda i: (0, i))
    shape = jax.ShapeDtypeStruct((rows, width), BF16)
    return pl.pallas_call(
        project_kernel,
        grid=(width // tile,),
        out_shape=(shape, shape),
        in_specs=fixed + [pl.BlockSpec((depth, tile), lambda i: (0, i))],
        out_specs=(out_spec, out_spec),
        compiler_params=PARAMS,
        cost_estimate=cost(0, 15 << 20),
        name="project",
    )(stay, came_a, came_b, weight)


def split_kernel(x_ref, *outs):
    base = 0
    for out in outs:
        out[...] = x_ref[:, base : base + out.shape[1]]
        base += out.shape[1]


def split_columns(x, widths):
    return pl.pallas_call(
        split_kernel,
        out_shape=tuple(jax.ShapeDtypeStruct((x.shape[0], w), x.dtype) for w in widths),
        in_specs=[VMEM],
        out_specs=(VMEM,) * len(widths),
        compiler_params=PARAMS,
        cost_estimate=cost(0, 2 << 20),
        name="split_columns",
    )(x)


def stack_kernel(*refs):
    *parts, out = refs
    rows = parts[0].shape[0]
    for i, part in enumerate(parts):
        out[i * rows : (i + 1) * rows, :] = part[...]


def stack_rows(parts):
    rows, width = parts[0].shape
    return pl.pallas_call(
        stack_kernel,
        out_shape=jax.ShapeDtypeStruct((len(parts) * rows, width), parts[0].dtype),
        in_specs=[VMEM] * len(parts),
        out_specs=VMEM,
        compiler_params=PARAMS,
        cost_estimate=cost(0, 2 << 20),
        name="stack_rows",
    )(*parts)


def swap_units(x):
    return lax.ppermute(x, "unit", [(0, 1), (1, 0)])


def after(x, *others):
    return lax.optimization_barrier((x, *others))[0]


def ring_at(step, length):
    if isinstance(step, int):
        return 2 * step - min(step, 1) if 2 * step <= length else 2 * (length - step)
    return jnp.where(2 * step <= length, 2 * step - jnp.minimum(step, 1), 2 * (length - step))


def ring_place(place, length):
    return jnp.where(place % 2 == 1, (place + 1) // 2, (length - place // 2) % length)


def chunk_widths(width):
    first = width * 5 // 12 // 128 * 128
    return [first, width - first]


def on_device(
    queries,
    kv_new,
    kv_pool,
    page_table,
    ctx_pages,
    ssm_x,
    ssm_z,
    ssm_bc,
    dt_raw,
    dt_bias,
    decay_rate,
    skip_gain,
    ssm_state,
    ssm_norm_gain,
    resid,
    out_weight,
    ffn_hidden,
    down_weight,
    page_owner,
):
    tok_rows = queries.shape[0]
    n_req = lax.axis_size("req")
    block_rows, width = down_weight.shape
    u = lax.axis_index("unit")
    unit = u.reshape(1)
    req = lax.axis_index("req")
    layers = n_req // PLANE

    ring = [ring_at(i, layers) for i in range(layers)]
    ring_pairs = [
        (ring[i] * PLANE + p, ring[(i + 1) % layers] * PLANE + p)
        for i in range(layers)
        for p in range(PLANE)
    ]

    def pass_on(x):
        return lax.ppermute(x, "req", ring_pairs)

    widths = chunk_widths(width // 2)
    kept, sent = cut(unit, down_weight, widths)
    a, b = ([stack_rows([k, swap_units(s)])] for k, s in zip(kept, sent))
    started = [a[0], b[0]]
    for chunk in (a, b):
        chunk.append(pass_on(chunk[-1]))

    def go_round(chunk, *others):
        chunk.append(pass_on(after(chunk[-1], *others)))

    def plane_swap(x, d):
        return lax.ppermute(
            x, "req", [(r, r - r % PLANE + ((r % PLANE) ^ d)) for r in range(n_req)]
        )

    mine = spread(req.reshape(1), after(ffn_hidden, *started), 2 * block_rows, layers)
    hidden = [plane_swap(x, d) if d else x for d, x in enumerate(mine)]
    attn, pages_held, pages_leave = attend(
        page_table, ctx_pages, page_owner[:, :, 0], unit, after(queries, mine[0]), kv_new, kv_pool
    )
    go_round(a, attn)
    stay, leave_a, leave_b, state_held, state_leave = state_space(
        unit,
        skip_gain,
        after(attn, a[1]),
        ssm_x,
        ssm_z,
        ssm_bc,
        dt_raw,
        dt_bias[None, :],
        decay_rate[None, :],
        ssm_norm_gain[None, :],
        ssm_state,
    )
    go_round(b, stay)
    leave_came = [swap_units(x) for x in after((leave_a, leave_b), b[1], a[2 % len(a)])]
    hidden = after(hidden, stay)
    gathered = after(stack_rows(hidden), *leave_came)
    hidden = list(hidden) + [swap_units(gathered)]
    mixed, mixed_leave = project(stay, *leave_came, out_weight)
    while len(a) < layers:
        go_round(a, mixed)
    mixed_leave, state_leave, pages_leave = after((mixed_leave, state_leave, pages_leave), mixed)
    decode_kv, decode_state, mixed = settle(
        unit,
        swap_units(pages_leave),
        swap_units(state_leave),
        pages_held,
        state_held,
        after(mixed, hidden[-1]),
    )
    mixed_came = swap_units(mixed_leave)
    while len(b) < layers - 1:
        go_round(b, mixed)
    b_last = b[-1]
    split = b_last.shape[1] // 256 * 128
    ends = ((0, split), (split, b_last.shape[1]))
    last = [pass_on(x) for x in split_columns(b_last, [hi - lo for lo, hi in ends])]

    own, parts = product(unit, hidden, a[:-1] + [after(a[-1], mixed, mixed_came)])
    sums, received = [], [plane_swap(x, d) for d, x in enumerate(parts, 1)]
    sums.append(total(own, received))
    order = parts
    for (lo, hi), end in zip(ends, last):
        own, parts = product(unit, hidden, b + [after(end, *order)], lo)
        parts = after(parts, *received)
        received = [plane_swap(x, d) for d, x in enumerate(parts, 1)]
        order = sums[-1]
        sums.append(total(own, after(received, *order)))
    kept, leave = zip(*sums)
    came = [swap_units(x) for x in leave]
    layer_out = finish(unit, resid, mixed, mixed_came, kept, came)
    return (layer_out, decode_kv, decode_state)


def solution(mesh):
    return jax.shard_map(
        on_device,
        mesh=mesh,
        in_specs=(
            P(("req", "unit"), None),
            P(("req", "unit"), None),
            P(("req", "unit"), None, None),
            P(("req", "unit"), None),
            P(("req", "unit")),
            P(("req", "unit"), None),
            P(("req", "unit"), None),
            P(("req", "unit"), None),
            P(("req", "unit"), None),
            P(),
            P(),
            P(),
            P(("req", "unit"), None, None, None),
            P(),
            P(("req", "unit"), None),
            P("unit", None),
            P(("req", "unit"), None),
            P(("req", "unit"), None),
            P(("req", "unit"), None, None),
        ),
        out_specs=(
            P(("req", "unit"), None),
            P(("req", "unit"), None, None),
            P("req", "unit", None, None),
        ),
        check_vma=False,
    )
```

```python
import functools
import math

import jax
import jax.numpy as jnp
from jax import lax
from jax.experimental import pallas as pl
from jax.experimental.pallas import tpu as pltpu
from jax.sharding import PartitionSpec as P

QUERY_HEADS = 12
KEY_VALUE_HEADS = 2
HEAD_WIDTH = 128
MIXER_HEADS = 24
PM = 128
NS = 256

PLANE = 4

norm_eps = 1e-05

F32, BF16 = jnp.float32, jnp.bfloat16
VMEM = pl.BlockSpec(memory_space=pltpu.VMEM)
SMEM = pl.BlockSpec(memory_space=pltpu.SMEM)
ANY = pl.BlockSpec(memory_space=pl.ANY)
PARAMS = pltpu.CompilerParams(vmem_limit_bytes=48 * 1024 * 1024)


def cost(flops, moved, exps=0):
    return pl.CostEstimate(flops=0, bytes_accessed=0, transcendentals=0)


def contract_last(a, b):
    return lax.dot_general(a, b, (((1,), (1,)), ((), ())), preferred_element_type=F32)


def two_terms(x):
    high = x.astype(BF16)
    return high, (x - high.astype(F32)).astype(BF16)


def attend_kernel(
    table, ctx, owner, unit, q_ref, new_ref, pool, out_ref, held, leave, pages, zero, sems, osems
):
    count, length, _ = pages.shape
    slots = leave.shape[0]
    live = ctx[0]
    u = unit[0]
    for j in range(count):

        @pl.when(j == live)
        def _():
            pltpu.make_async_copy(new_ref, pages.at[j], sems.at[j]).start()

        @pl.when(j != live)
        def _():
            pltpu.make_async_copy(pool.at[table[0, j]], pages.at[j], sems.at[j]).start()

    zero[...] = jnp.zeros_like(zero)
    for j in range(count):
        pltpu.make_async_copy(new_ref, pages.at[j], sems.at[j]).wait()

    named = [jnp.int32(0), jnp.int32(0)]
    for j in range(count):
        own = owner[0, j] == u
        rank = jnp.where(own, named[0], named[1])
        named = [named[0] + own.astype(jnp.int32), named[1] + 1 - own.astype(jnp.int32)]
        for source, when in ((pages.at[j], j <= live), (zero, j > live)):

            @pl.when(when & own)
            def _():
                pltpu.make_async_copy(source, held.at[u * slots + rank], osems.at[j]).start()

            @pl.when(when & jnp.logical_not(own))
            def _():
                pltpu.make_async_copy(source, leave.at[rank], osems.at[j]).start()

    for k in range(slots):

        @pl.when(k >= named[0])
        def _():
            pltpu.make_async_copy(zero, held.at[u * slots + k], osems.at[count + k]).start()

        @pl.when(k >= named[1])
        def _():
            pltpu.make_async_copy(zero, leave.at[k], osems.at[count + slots + k]).start()

    group = QUERY_HEADS // KEY_VALUE_HEADS
    heads = 3
    rows, keys = heads * length, count * length
    limit = live * length + lax.broadcasted_iota(jnp.int32, (rows, 1), 0) % length
    visible = lax.broadcasted_iota(jnp.int32, (rows, keys), 1) <= limit
    scale = 1.0 / math.sqrt(HEAD_WIDTH)
    for k in range(KEY_VALUE_HEADS):
        key_rows = pages[:, :, k * HEAD_WIDTH : (k + 1) * HEAD_WIDTH].reshape(keys, HEAD_WIDTH)
        lo = (KEY_VALUE_HEADS + k) * HEAD_WIDTH
        value_rows = pages[:, :, lo : lo + HEAD_WIDTH].reshape(keys, HEAD_WIDTH)
        for first in range(k * group, (k + 1) * group, heads):
            spans = [
                slice(h * HEAD_WIDTH, (h + 1) * HEAD_WIDTH) for h in range(first, first + heads)
            ]
            q = jnp.concatenate([q_ref[:, span] for span in spans], axis=0)
            scores = jnp.where(visible, contract_last(q, key_rows), -1e30)
            top = jnp.max(scores, axis=1, keepdims=True)
            exponent = jnp.exp((scores - top) * scale)
            weights = (exponent * (1.0 / jnp.sum(exponent, axis=1, keepdims=True))).astype(BF16)
            attended = jnp.dot(weights, value_rows, preferred_element_type=F32).astype(BF16)
            for i, span in enumerate(spans):
                out_ref[:, span] = attended[i * length : (i + 1) * length]

    for j in range(count):
        pltpu.make_async_copy(zero, leave.at[0], osems.at[j]).wait()
    for k in range(slots):

        @pl.when(k >= named[0])
        def _():
            pltpu.make_async_copy(zero, leave.at[0], osems.at[count + k]).wait()

        @pl.when(k >= named[1])
        def _():
            pltpu.make_async_copy(zero, leave.at[0], osems.at[count + slots + k]).wait()


def attend(table, ctx, owner, unit, queries, kv_new, pool):
    count, length, width = pool.shape
    slots = max(2, (count + 1) // 2)
    pairs = QUERY_HEADS * length * count * length
    return pl.pallas_call(
        attend_kernel,
        out_shape=(
            jax.ShapeDtypeStruct(queries.shape, BF16),
            jax.ShapeDtypeStruct((2 * slots, length, width), BF16),
            jax.ShapeDtypeStruct((slots, length, width), BF16),
        ),
        in_specs=[SMEM, SMEM, SMEM, SMEM, VMEM, VMEM, ANY],
        out_specs=(VMEM, ANY, ANY),
        scratch_shapes=[
            pltpu.VMEM((count, length, width), BF16),
            pltpu.VMEM((length, width), BF16),
            pltpu.SemaphoreType.DMA((count,)),
            pltpu.SemaphoreType.DMA((count + 2 * slots,)),
        ],
        compiler_params=PARAMS,
        cost_estimate=cost(4 * pairs * HEAD_WIDTH * 4, 6 << 20, pairs),
        name="attend",
    )(table, ctx, owner, unit, queries, kv_new, pool)


def state_kernel(
    unit,
    skip,
    attn_ref,
    x_ref,
    z_ref,
    bc_ref,
    dt_ref,
    bias_ref,
    rate_ref,
    gain_ref,
    state_ref,
    stay_ref,
    leave_a,
    leave_b,
    held,
    send_ref,
    gated,
    fresh,
    sems,
):
    length = x_ref.shape[0]
    heads, share = MIXER_HEADS, MIXER_HEADS // 2
    u = unit[0]
    rows = lax.broadcasted_iota(jnp.int32, (length, length), 0)
    cols = lax.broadcasted_iota(jnp.int32, (length, length), 1)
    causal = rows >= cols
    raw = dt_ref[...] + bias_ref[...]
    step = jnp.maximum(raw, 0.0) + jnp.log1p(jnp.exp(-jnp.abs(raw)))
    cum = jnp.dot(
        causal.astype(F32),
        -step * rate_ref[...],
        precision=lax.Precision.HIGHEST,
        preferred_element_type=F32,
    )
    blank = jnp.zeros((length, length - heads), F32)
    cum_rows = jnp.transpose(jnp.concatenate([cum, blank], axis=1))
    step_rows = jnp.transpose(jnp.concatenate([step, blank], axis=1))
    last = cum[length - 1 : length, :]
    b_rows, c_rows = bc_ref[:, :NS], bc_ref[:, NS:]
    dots = contract_last(c_rows, b_rows)
    square = jnp.zeros((length, PM), F32)
    for h in range(heads):
        span = slice(h * PM, (h + 1) * PM)
        cum_t, cum_s = cum[:, h : h + 1], cum_rows[h : h + 1, :]
        step_s, end = step_rows[h : h + 1, :], last[:, h : h + 1]
        decay = jnp.exp(jnp.where(causal, cum_t - cum_s, -1e30))
        mixing = (dots * decay * step_s).astype(BF16)
        x = x_ref[:, span]
        x_float = x.astype(F32)
        prior = state_ref[0, h]
        high, low = two_terms(prior)
        carried = contract_last(c_rows, high) + contract_last(c_rows, low)
        y = jnp.dot(mixing, x, preferred_element_type=F32)
        y = y + carried * jnp.exp(cum_t) + skip[h] * x_float
        z = z_ref[:, span].astype(F32)
        g = y * (z / (1.0 + jnp.exp(-z)))
        gated[:, span] = g
        square = square + g * g
        weighted = jnp.transpose(x_float) * (jnp.exp(end - cum_s) * step_s)
        high, low = two_terms(weighted)
        new = jnp.exp(end) * prior + (
            jnp.dot(high, b_rows, preferred_element_type=F32)
            + jnp.dot(low, b_rows, preferred_element_type=F32)
        )
        place = h % share

        @pl.when(u == h // share)
        def _():
            fresh[place] = new
            pltpu.make_async_copy(fresh.at[place], held.at[u, place], sems.at[place]).start()

        @pl.when(u != h // share)
        def _():
            send_ref[place] = new.astype(BF16)

    mean = jnp.sum(square, axis=1, keepdims=True) * (1.0 / (heads * PM))
    out = (gated[...] * lax.rsqrt(mean + norm_eps) * gain_ref[...]).astype(BF16)
    attn_width = attn_ref.shape[1]
    cut = stay_ref.shape[1] - attn_width
    part = leave_a.shape[1]

    @pl.when(u == 0)
    def _():
        stay_ref[:, :attn_width] = attn_ref[...]
        stay_ref[:, attn_width:] = out[:, :cut]
        leave_a[...] = out[:, cut : cut + part]
        leave_b[...] = out[:, cut + part :]

    @pl.when(u == 1)
    def _():
        stay_ref[...] = out[:, cut:]
        leave_a[...] = attn_ref[:, :part]
        leave_b[:, : attn_width - part] = attn_ref[:, part:]
        leave_b[:, attn_width - part :] = out[:, :cut]

    for place in range(share):
        pltpu.make_async_copy(fresh.at[place], held.at[0, place], sems.at[place]).wait()


def state_space(unit, skip, attn, x, z, bc, dt, bias, rate, gain, state):
    length, width = x.shape
    share = MIXER_HEADS // 2
    half = (attn.shape[1] + width) // 2
    return pl.pallas_call(
        state_kernel,
        out_shape=(
            jax.ShapeDtypeStruct((length, half), BF16),
            jax.ShapeDtypeStruct((length, half // 2), BF16),
            jax.ShapeDtypeStruct((length, half - half // 2), BF16),
            jax.ShapeDtypeStruct((2, share, PM, NS), F32),
            jax.ShapeDtypeStruct((share, PM, NS), BF16),
        ),
        in_specs=[SMEM, SMEM] + [VMEM] * 9,
        out_specs=(VMEM, VMEM, VMEM, ANY, VMEM),
        scratch_shapes=[
            pltpu.VMEM((length, width), F32),
            pltpu.VMEM((share, PM, NS), F32),
            pltpu.SemaphoreType.DMA((share,)),
        ],
        compiler_params=PARAMS,
        cost_estimate=cost(4 << 30, 10 << 20, MIXER_HEADS * length * length * 2),
        name="state_space",
    )(unit, skip, attn, x, z, bc, dt, bias, rate, gain, state)


def settle_kernel(
    unit, pages, state, pages_in, state_in, rows_in, pages_out, state_out, rows_out, wide, sem
):
    slots = pages.shape[0]
    u = unit[0]
    copy = pltpu.make_async_copy(pages, pages_out.at[pl.ds((1 - u) * slots, slots)], sem.at[0])
    copy.start()
    wide[...] = state[...].astype(F32)
    other = pltpu.make_async_copy(wide, state_out.at[1 - u], sem.at[1])
    other.start()
    copy.wait()
    other.wait()


def settle(unit, pages, state, pages_held, state_held, rows):
    return pl.pallas_call(
        settle_kernel,
        out_shape=tuple(
            jax.ShapeDtypeStruct(x.shape, x.dtype) for x in (pages_held, state_held, rows)
        ),
        in_specs=[SMEM, ANY, VMEM, ANY, ANY, ANY],
        out_specs=(ANY, ANY, ANY),
        scratch_shapes=[pltpu.VMEM(state.shape, F32), pltpu.SemaphoreType.DMA((2,))],
        input_output_aliases={3: 0, 4: 1, 5: 2},
        compiler_params=PARAMS,
        cost_estimate=cost(0, 5 << 20),
        name="settle",
    )(unit, pages, state, pages_held, state_held, rows)


def cut_kernel(unit, weight_ref, kept, sent):
    half = weight_ref.shape[1] // 2
    for u, low_ref, high_ref in ((0, kept, sent), (1, sent, kept)):

        @pl.when(unit[0] == u)
        def _():
            low_ref[...] = weight_ref[:, :half]
            high_ref[...] = weight_ref[:, half:]


def cut(unit, weight):
    rows, width = weight.shape
    shape = jax.ShapeDtypeStruct((rows, width // 2), weight.dtype)
    return pl.pallas_call(
        cut_kernel,
        out_shape=(shape, shape),
        in_specs=[SMEM, VMEM],
        out_specs=(VMEM, VMEM),
        compiler_params=PARAMS,
        cost_estimate=cost(0, 3 << 20),
        name="cut",
    )(unit, weight)


def block_of(req, d, k, layers):
    layer, place = req // PLANE, req % PLANE
    source = ring_at((ring_place(layer, layers) + layers - k) % layers, layers)
    return source * PLANE + (place ^ d)


def spread_kernel(req, hidden, *refs):
    outs, sem = refs[:-1], refs[-1]
    rows, depth = outs[0].shape
    layers = sem.shape[0] // PLANE
    chip_rows = depth // layers
    copies = []
    for d in range(PLANE):
        for k in range(layers):
            column = pl.multiple_of(chip_rows * block_of(req[0], d, k, layers), 128)
            copies.append(
                pltpu.make_async_copy(
                    hidden.at[:, pl.ds(column, chip_rows)],
                    outs[d].at[:, k * chip_rows : (k + 1) * chip_rows],
                    sem.at[d * layers + k],
                )
            )
    for copy in copies:
        copy.start()
    for copy in copies:
        copy.wait()


def spread(req, hidden, chip_rows, layers):
    rows = hidden.shape[0]
    if chip_rows % 128:
        return [
            jnp.concatenate(
                [
                    lax.dynamic_slice(
                        hidden, (0, block_of(req[0], d, k, layers) * chip_rows), (rows, chip_rows)
                    )
                    for k in range(layers)
                ],
                axis=1,
            )
            for d in range(PLANE)
        ]
    return pl.pallas_call(
        spread_kernel,
        out_shape=(jax.ShapeDtypeStruct((rows, layers * chip_rows), hidden.dtype),) * PLANE,
        in_specs=[SMEM, ANY],
        out_specs=(VMEM,) * PLANE,
        scratch_shapes=[pltpu.SemaphoreType.DMA((PLANE * layers,))],
        compiler_params=PARAMS,
        cost_estimate=cost(0, 4 << 20),
        name="spread",
    )(req, hidden)


def product_kernel(bases, unit, *refs):
    count = len(bases)
    hidden, pieces = refs[: PLANE + 2], refs[PLANE + 2 : PLANE + 2 + count]
    own_ref, *parts = refs[PLANE + 2 + count : -1]
    weight = refs[-1]
    block_rows = pieces[0].shape[0] // 2
    u = unit[0]
    for k, piece in enumerate(pieces):
        for which, place in ((0, u), (1, 1 - u)):
            at = pl.multiple_of((2 * k + place) * block_rows, 16)
            rows = slice(which * block_rows, (which + 1) * block_rows)
            base = bases[k]
            weight[pl.ds(at, block_rows), :] = piece[rows, base : base + weight.shape[1]]
    rows = hidden[0].shape[0]
    for d in range(PLANE):
        place = d % (PLANE // 2) * rows
        other = hidden[PLANE + d // (PLANE // 2)][place : place + rows, :]
        both = jnp.concatenate([hidden[d][...], other], axis=0)
        result = jnp.dot(both, weight[...], preferred_element_type=F32)
        if d:
            parts[d - 1][...] = result.astype(BF16)
        else:
            own_ref[...] = result


def product(unit, hidden, pieces, low=0):
    rows, depth = hidden[0].shape
    width = pieces[-1].shape[1]
    bases = [0 if x.shape[1] == width else low for x in pieces]
    outs = pl.pallas_call(
        functools.partial(product_kernel, tuple(bases)),
        out_shape=(jax.ShapeDtypeStruct((2 * rows, width), F32),)
        + (jax.ShapeDtypeStruct((2 * rows, width), BF16),) * (PLANE - 1),
        in_specs=[SMEM] + [VMEM] * (PLANE + 2 + len(pieces)),
        out_specs=(VMEM,) * PLANE,
        scratch_shapes=[pltpu.VMEM((depth, width), BF16)],
        compiler_params=PARAMS,
        cost_estimate=cost(0, 6 << 20),
        name="product",
    )(unit, *hidden, *pieces)
    return outs[0], outs[1:]


def total_kernel(own_ref, *refs):
    came, (keep_ref, send_ref) = refs[:-2], refs[-2:]
    total = own_ref[...]
    for ref in came:
        total = total + ref[...].astype(F32)
    rows = keep_ref.shape[0]
    keep_ref[...] = total[:rows]
    send_ref[...] = total[rows:].astype(BF16)


def total(own, came):
    rows, width = own.shape
    return pl.pallas_call(
        total_kernel,
        out_shape=(
            jax.ShapeDtypeStruct((rows // 2, width), F32),
            jax.ShapeDtypeStruct((rows // 2, width), BF16),
        ),
        in_specs=[VMEM] * (1 + len(came)),
        out_specs=(VMEM, VMEM),
        compiler_params=PARAMS,
        cost_estimate=cost(0, 4 << 20),
        name="total",
    )(own, *came)


def finish_kernel(unit, resid_ref, mixed_ref, low_ref, high_ref, *refs):
    count = len(refs) // 2
    kept, came, out_ref = refs[:count], refs[count:-1], refs[-1]
    half = out_ref.shape[1] // 2
    for u in range(2):

        @pl.when(unit[0] == u)
        def _():
            for group, which in ((kept, u), (came, 1 - u)):
                base = 0
                other_ref = high_ref if which else low_ref
                for ref in group:
                    span = slice(which * half + base, which * half + base + ref.shape[1])
                    mixed = mixed_ref[:, span].astype(F32)
                    mixed = mixed + other_ref[:, base : base + ref.shape[1]].astype(F32)
                    sums = resid_ref[:, span].astype(F32) + mixed + ref[...].astype(F32)
                    out_ref[:, span] = sums.astype(BF16)
                    base += ref.shape[1]


def finish(unit, resid, mixed, mixed_came, kept, came):
    return pl.pallas_call(
        finish_kernel,
        out_shape=jax.ShapeDtypeStruct(resid.shape, BF16),
        in_specs=[SMEM] + [VMEM] * (4 + len(kept) + len(came)),
        out_specs=VMEM,
        compiler_params=PARAMS,
        cost_estimate=cost(0, 4 << 20),
        name="finish",
    )(unit, resid, mixed, *mixed_came, *kept, *came)


def project_kernel(stay_ref, a_ref, b_ref, weight_ref, keep_ref, low_ref, high_ref):
    rows = stay_ref.shape[0]
    half = pl.num_programs(0) // 2
    came = jnp.concatenate([a_ref[...], b_ref[...]], axis=1)
    both = jnp.concatenate([stay_ref[...], came], axis=0)
    result = jnp.dot(both, weight_ref[...], preferred_element_type=F32).astype(BF16)
    keep_ref[...] = result[:rows]

    @pl.when(pl.program_id(0) < half)
    def _():
        low_ref[...] = result[rows:]

    @pl.when(pl.program_id(0) >= half)
    def _():
        high_ref[...] = result[rows:]


def project(stay, came_a, came_b, weight):
    rows, depth = stay.shape
    width = weight.shape[1]
    tile = 512 if width % 1024 == 0 else width // 2
    half = width // tile // 2
    fixed = [pl.BlockSpec(x.shape, lambda i: (0, 0)) for x in (stay, came_a, came_b)]
    return pl.pallas_call(
        project_kernel,
        grid=(2 * half,),
        out_shape=(
            jax.ShapeDtypeStruct((rows, width), BF16),
            jax.ShapeDtypeStruct((rows, width // 2), BF16),
            jax.ShapeDtypeStruct((rows, width // 2), BF16),
        ),
        in_specs=fixed + [pl.BlockSpec((depth, tile), lambda i: (0, i))],
        out_specs=(
            pl.BlockSpec((rows, tile), lambda i: (0, i)),
            pl.BlockSpec((rows, tile), lambda i: (0, jnp.minimum(i, half - 1))),
            pl.BlockSpec((rows, tile), lambda i: (0, jnp.maximum(i - half, 0))),
        ),
        compiler_params=PARAMS,
        cost_estimate=cost(0, 15 << 20),
        name="project",
    )(stay, came_a, came_b, weight)


def split_kernel(x_ref, *outs):
    base = 0
    for out in outs:
        out[...] = x_ref[:, base : base + out.shape[1]]
        base += out.shape[1]


def split_columns(x, widths):
    return pl.pallas_call(
        split_kernel,
        out_shape=tuple(jax.ShapeDtypeStruct((x.shape[0], w), x.dtype) for w in widths),
        in_specs=[VMEM],
        out_specs=(VMEM,) * len(widths),
        compiler_params=PARAMS,
        cost_estimate=cost(0, 2 << 20),
        name="split_columns",
    )(x)


def stack_kernel(*refs):
    *parts, out = refs
    rows = parts[0].shape[0]
    for i, part in enumerate(parts):
        out[i * rows : (i + 1) * rows, :] = part[...]


def stack_rows(parts):
    rows, width = parts[0].shape
    return pl.pallas_call(
        stack_kernel,
        out_shape=jax.ShapeDtypeStruct((len(parts) * rows, width), parts[0].dtype),
        in_specs=[VMEM] * len(parts),
        out_specs=VMEM,
        compiler_params=PARAMS,
        cost_estimate=cost(0, 2 << 20),
        name="stack_rows",
    )(*parts)


def swap_units(x):
    return lax.ppermute(x, "unit", [(0, 1), (1, 0)])


def after(x, *others):
    return lax.optimization_barrier((x, *others))[0]


def ring_at(step, length):
    if isinstance(step, int):
        return 2 * step - min(step, 1) if 2 * step <= length else 2 * (length - step)
    return jnp.where(2 * step <= length, 2 * step - jnp.minimum(step, 1), 2 * (length - step))


def ring_place(place, length):
    return jnp.where(place % 2 == 1, (place + 1) // 2, (length - place // 2) % length)


def chunk_widths(width):
    first, last = width // 4 // 128 * 128, width // 3 // 128 * 128
    return [first, width - first - last, last]


def on_device(
    queries,
    kv_new,
    kv_pool,
    page_table,
    ctx_pages,
    ssm_x,
    ssm_z,
    ssm_bc,
    dt_raw,
    dt_bias,
    decay_rate,
    skip_gain,
    ssm_state,
    ssm_norm_gain,
    resid,
    out_weight,
    ffn_hidden,
    down_weight,
    page_owner,
):
    tok_rows = queries.shape[0]
    n_req = lax.axis_size("req")
    block_rows, width = down_weight.shape
    u = lax.axis_index("unit")
    unit = u.reshape(1)
    req = lax.axis_index("req")
    layers = n_req // PLANE

    ring = [ring_at(i, layers) for i in range(layers)]
    ring_pairs = [
        (ring[i] * PLANE + p, ring[(i + 1) % layers] * PLANE + p)
        for i in range(layers)
        for p in range(PLANE)
    ]

    def pass_on(x):
        return lax.ppermute(x, "req", ring_pairs)

    kept, sent = cut(unit, down_weight)
    hops = [stack_rows([kept, swap_units(sent)])]
    if layers > 2:
        hops.append(pass_on(hops[0]))

    def plane_swap(x, d):
        return lax.ppermute(
            x, "req", [(r, r - r % PLANE + ((r % PLANE) ^ d)) for r in range(n_req)]
        )

    mine = spread(req.reshape(1), after(ffn_hidden, hops[0]), 2 * block_rows, layers)
    hidden = [plane_swap(x, d) if d else x for d, x in enumerate(mine)]
    attn, pages_held, pages_leave = attend(
        page_table, ctx_pages, page_owner[:, :, 0], unit, after(queries, mine[0]), kv_new, kv_pool
    )
    while len(hops) < layers - 1:
        hops.append(pass_on(after(hops[-1], attn)))
    stay, leave_a, leave_b, state_held, state_leave = state_space(
        unit,
        skip_gain,
        after(attn, *hops[1:2]),
        ssm_x,
        ssm_z,
        ssm_bc,
        dt_raw,
        dt_bias[None, :],
        decay_rate[None, :],
        ssm_norm_gain[None, :],
        ssm_state,
    )
    hidden = after(hidden, stay)
    leave_came = [swap_units(x) for x in after((leave_a, leave_b), *hidden)]
    pair = PLANE // 2
    gathered = [after(stack_rows(x), *leave_came) for x in (hidden[:pair], hidden[pair:])]
    swapped = [swap_units(x) for x in gathered]
    hidden = list(hidden) + swapped
    mixed, *mixed_leave = project(stay, *leave_came, out_weight)
    mixed_came = [swap_units(x) for x in after(mixed_leave, hops[-1], *swapped)]
    widths = chunk_widths(width // 2)
    ends = [pass_on(x) for x in split_columns(after(hops[-1], mixed), widths)]
    sums, order, received, low = [], mixed_came, [], 0
    for n, end in enumerate(ends):
        own, parts = product(unit, hidden, hops + [after(end, *order)], low)
        order, low = list(parts) + [x[0] for x in sums], low + widths[n]
        if received:
            parts = after(parts, *received)
        if n == len(ends) - 1:
            state_leave, pages_leave = after((state_leave, pages_leave), *parts)
            state_came, pages_came = swap_units(state_leave), swap_units(pages_leave)
        received = [plane_swap(x, d) for d, x in enumerate(parts, 1)]
        token = sums[-1][0] if sums else own
        if n == len(ends) - 1:
            decode_kv, decode_state, token = settle(
                unit, pages_came, state_came, pages_held, state_held, token
            )
            sums[-1] = (token, sums[-1][1])
        sums.append(total(own, after(received, token)))
    kept, leave = zip(*sums)
    came = [swap_units(x) for x in leave]
    layer_out = finish(unit, resid, mixed, mixed_came, kept, came)
    return (layer_out, decode_kv, decode_state)


def solution(mesh):
    return jax.shard_map(
        on_device,
        mesh=mesh,
        in_specs=(
            P(("req", "unit"), None),
            P(("req", "unit"), None),
            P(("req", "unit"), None, None),
            P(("req", "unit"), None),
            P(("req", "unit")),
            P(("req", "unit"), None),
            P(("req", "unit"), None),
            P(("req", "unit"), None),
            P(("req", "unit"), None),
            P(),
            P(),
            P(),
            P(("req", "unit"), None, None, None),
            P(),
            P(("req", "unit"), None),
            P("unit", None),
            P(("req", "unit"), None),
            P(("req", "unit"), None),
            P(("req", "unit"), None, None),
        ),
        out_specs=(
            P(("req", "unit"), None),
            P(("req", "unit"), None, None),
            P("req", "unit", None, None),
        ),
        check_vma=False,
    )
```

```python
import functools
import math

import jax
import jax.numpy as jnp
from jax import lax
from jax.experimental import pallas as pl
from jax.experimental.pallas import tpu as pltpu
from jax.sharding import PartitionSpec as P

QUERY_HEADS = 12
KEY_VALUE_HEADS = 2
HEAD_WIDTH = 128
MIXER_HEADS = 24
PM = 128
NS = 256

PLANE = 4

norm_eps = 1e-05

F32, BF16 = jnp.float32, jnp.bfloat16
VMEM = pl.BlockSpec(memory_space=pltpu.VMEM)
SMEM = pl.BlockSpec(memory_space=pltpu.SMEM)
ANY = pl.BlockSpec(memory_space=pl.ANY)
PARAMS = pltpu.CompilerParams(vmem_limit_bytes=48 * 1024 * 1024)


def cost(flops, moved, exps=0):
    return pl.CostEstimate(flops=0, bytes_accessed=0, transcendentals=0)


def contract_last(a, b):
    return lax.dot_general(a, b, (((1,), (1,)), ((), ())), preferred_element_type=F32)


def two_terms(x):
    high = x.astype(BF16)
    return high, (x - high.astype(F32)).astype(BF16)


def attend_kernel(
    table, ctx, owner, unit, q_ref, new_ref, pool, out_ref, held, leave, pages, zero, sems, osems
):
    count, length, _ = pages.shape
    slots = leave.shape[0]
    live = ctx[0]
    u = unit[0]
    for j in range(count):

        @pl.when(j == live)
        def _():
            pltpu.make_async_copy(new_ref, pages.at[j], sems.at[j]).start()

        @pl.when(j != live)
        def _():
            pltpu.make_async_copy(pool.at[table[0, j]], pages.at[j], sems.at[j]).start()

    zero[...] = jnp.zeros_like(zero)
    for j in range(count):
        pltpu.make_async_copy(new_ref, pages.at[j], sems.at[j]).wait()

    named = [jnp.int32(0), jnp.int32(0)]
    for j in range(count):
        own = owner[0, j] == u
        rank = jnp.where(own, named[0], named[1])
        named = [named[0] + own.astype(jnp.int32), named[1] + 1 - own.astype(jnp.int32)]
        for source, when in ((pages.at[j], j <= live), (zero, j > live)):

            @pl.when(when & own)
            def _():
                pltpu.make_async_copy(source, held.at[u * slots + rank], osems.at[j]).start()

            @pl.when(when & jnp.logical_not(own))
            def _():
                pltpu.make_async_copy(source, leave.at[rank], osems.at[j]).start()

    for k in range(slots):

        @pl.when(k >= named[0])
        def _():
            pltpu.make_async_copy(zero, held.at[u * slots + k], osems.at[count + k]).start()

        @pl.when(k >= named[1])
        def _():
            pltpu.make_async_copy(zero, leave.at[k], osems.at[count + slots + k]).start()

    group = QUERY_HEADS // KEY_VALUE_HEADS
    heads = 3
    rows, keys = heads * length, count * length
    limit = live * length + lax.broadcasted_iota(jnp.int32, (rows, 1), 0) % length
    visible = lax.broadcasted_iota(jnp.int32, (rows, keys), 1) <= limit
    scale = 1.0 / math.sqrt(HEAD_WIDTH)
    for k in range(KEY_VALUE_HEADS):
        key_rows = pages[:, :, k * HEAD_WIDTH : (k + 1) * HEAD_WIDTH].reshape(keys, HEAD_WIDTH)
        lo = (KEY_VALUE_HEADS + k) * HEAD_WIDTH
        value_rows = pages[:, :, lo : lo + HEAD_WIDTH].reshape(keys, HEAD_WIDTH)
        for first in range(k * group, (k + 1) * group, heads):
            spans = [
                slice(h * HEAD_WIDTH, (h + 1) * HEAD_WIDTH) for h in range(first, first + heads)
            ]
            q = jnp.concatenate([q_ref[:, span] for span in spans], axis=0)
            scores = jnp.where(visible, contract_last(q, key_rows), -1e30)
            top = jnp.max(scores, axis=1, keepdims=True)
            exponent = jnp.exp((scores - top) * scale)
            weights = (exponent * (1.0 / jnp.sum(exponent, axis=1, keepdims=True))).astype(BF16)
            attended = jnp.dot(weights, value_rows, preferred_element_type=F32).astype(BF16)
            for i, span in enumerate(spans):
                out_ref[:, span] = attended[i * length : (i + 1) * length]

    for j in range(count):
        pltpu.make_async_copy(zero, leave.at[0], osems.at[j]).wait()
    for k in range(slots):

        @pl.when(k >= named[0])
        def _():
            pltpu.make_async_copy(zero, leave.at[0], osems.at[count + k]).wait()

        @pl.when(k >= named[1])
        def _():
            pltpu.make_async_copy(zero, leave.at[0], osems.at[count + slots + k]).wait()


def attend(table, ctx, owner, unit, queries, kv_new, pool):
    count, length, width = pool.shape
    slots = max(2, (count + 1) // 2)
    pairs = QUERY_HEADS * length * count * length
    return pl.pallas_call(
        attend_kernel,
        out_shape=(
            jax.ShapeDtypeStruct(queries.shape, BF16),
            jax.ShapeDtypeStruct((2 * slots, length, width), BF16),
            jax.ShapeDtypeStruct((slots, length, width), BF16),
        ),
        in_specs=[SMEM, SMEM, SMEM, SMEM, VMEM, VMEM, ANY],
        out_specs=(VMEM, ANY, ANY),
        scratch_shapes=[
            pltpu.VMEM((count, length, width), BF16),
            pltpu.VMEM((length, width), BF16),
            pltpu.SemaphoreType.DMA((count,)),
            pltpu.SemaphoreType.DMA((count + 2 * slots,)),
        ],
        compiler_params=PARAMS,
        cost_estimate=cost(4 * pairs * HEAD_WIDTH * 4, 6 << 20, pairs),
        name="attend",
    )(table, ctx, owner, unit, queries, kv_new, pool)


def state_kernel(
    unit,
    skip,
    attn_ref,
    x_ref,
    z_ref,
    bc_ref,
    dt_ref,
    bias_ref,
    rate_ref,
    gain_ref,
    state_ref,
    stay_ref,
    leave_a,
    leave_b,
    held,
    send_ref,
    gated,
    fresh,
    sems,
):
    length = x_ref.shape[0]
    heads, share = MIXER_HEADS, MIXER_HEADS // 2
    u = unit[0]
    rows = lax.broadcasted_iota(jnp.int32, (length, length), 0)
    cols = lax.broadcasted_iota(jnp.int32, (length, length), 1)
    causal = rows >= cols
    raw = dt_ref[...] + bias_ref[...]
    step = jnp.maximum(raw, 0.0) + jnp.log1p(jnp.exp(-jnp.abs(raw)))
    cum = jnp.dot(
        causal.astype(F32),
        -step * rate_ref[...],
        precision=lax.Precision.HIGHEST,
        preferred_element_type=F32,
    )
    blank = jnp.zeros((length, length - heads), F32)
    cum_rows = jnp.transpose(jnp.concatenate([cum, blank], axis=1))
    step_rows = jnp.transpose(jnp.concatenate([step, blank], axis=1))
    last = cum[length - 1 : length, :]
    b_rows, c_rows = bc_ref[:, :NS], bc_ref[:, NS:]
    dots = contract_last(c_rows, b_rows)
    square = jnp.zeros((length, PM), F32)
    for h in range(heads):
        span = slice(h * PM, (h + 1) * PM)
        cum_t, cum_s = cum[:, h : h + 1], cum_rows[h : h + 1, :]
        step_s, end = step_rows[h : h + 1, :], last[:, h : h + 1]
        decay = jnp.exp(jnp.where(causal, cum_t - cum_s, -1e30))
        mixing = (dots * decay * step_s).astype(BF16)
        x = x_ref[:, span]
        x_float = x.astype(F32)
        prior = state_ref[0, h]
        high, low = two_terms(prior)
        carried = contract_last(c_rows, high) + contract_last(c_rows, low)
        y = jnp.dot(mixing, x, preferred_element_type=F32)
        y = y + carried * jnp.exp(cum_t) + skip[h] * x_float
        z = z_ref[:, span].astype(F32)
        g = y * (z / (1.0 + jnp.exp(-z)))
        gated[:, span] = g
        square = square + g * g
        weighted = jnp.transpose(x_float) * (jnp.exp(end - cum_s) * step_s)
        high, low = two_terms(weighted)
        new = jnp.exp(end) * prior + (
            jnp.dot(high, b_rows, preferred_element_type=F32)
            + jnp.dot(low, b_rows, preferred_element_type=F32)
        )
        place = h % share

        @pl.when(u == h // share)
        def _():
            fresh[place] = new
            pltpu.make_async_copy(fresh.at[place], held.at[u, place], sems.at[place]).start()

        @pl.when(u != h // share)
        def _():
            send_ref[place] = new.astype(BF16)

    mean = jnp.sum(square, axis=1, keepdims=True) * (1.0 / (heads * PM))
    out = (gated[...] * lax.rsqrt(mean + norm_eps) * gain_ref[...]).astype(BF16)
    attn_width = attn_ref.shape[1]
    cut = stay_ref.shape[1] - attn_width
    part = leave_a.shape[1]

    @pl.when(u == 0)
    def _():
        stay_ref[:, :attn_width] = attn_ref[...]
        stay_ref[:, attn_width:] = out[:, :cut]
        leave_a[...] = out[:, cut : cut + part]
        leave_b[...] = out[:, cut + part :]

    @pl.when(u == 1)
    def _():
        stay_ref[...] = out[:, cut:]
        leave_a[...] = attn_ref[:, :part]
        leave_b[:, : attn_width - part] = attn_ref[:, part:]
        leave_b[:, attn_width - part :] = out[:, :cut]

    for place in range(share):
        pltpu.make_async_copy(fresh.at[place], held.at[0, place], sems.at[place]).wait()


def state_space(unit, skip, attn, x, z, bc, dt, bias, rate, gain, state):
    length, width = x.shape
    share = MIXER_HEADS // 2
    half = (attn.shape[1] + width) // 2
    return pl.pallas_call(
        state_kernel,
        out_shape=(
            jax.ShapeDtypeStruct((length, half), BF16),
            jax.ShapeDtypeStruct((length, half // 2), BF16),
            jax.ShapeDtypeStruct((length, half - half // 2), BF16),
            jax.ShapeDtypeStruct((2, share, PM, NS), F32),
            jax.ShapeDtypeStruct((share, PM, NS), BF16),
        ),
        in_specs=[SMEM, SMEM] + [VMEM] * 9,
        out_specs=(VMEM, VMEM, VMEM, ANY, VMEM),
        scratch_shapes=[
            pltpu.VMEM((length, width), F32),
            pltpu.VMEM((share, PM, NS), F32),
            pltpu.SemaphoreType.DMA((share,)),
        ],
        compiler_params=PARAMS,
        cost_estimate=cost(4 << 30, 10 << 20, MIXER_HEADS * length * length * 2),
        name="state_space",
    )(unit, skip, attn, x, z, bc, dt, bias, rate, gain, state)


def settle_kernel(
    unit, pages, state, pages_in, state_in, rows_in, pages_out, state_out, rows_out, wide, sem
):
    slots = pages.shape[0]
    u = unit[0]
    copy = pltpu.make_async_copy(pages, pages_out.at[pl.ds((1 - u) * slots, slots)], sem.at[0])
    copy.start()
    wide[...] = state[...].astype(F32)
    other = pltpu.make_async_copy(wide, state_out.at[1 - u], sem.at[1])
    other.start()
    copy.wait()
    other.wait()


def settle(unit, pages, state, pages_held, state_held, rows):
    return pl.pallas_call(
        settle_kernel,
        out_shape=tuple(
            jax.ShapeDtypeStruct(x.shape, x.dtype) for x in (pages_held, state_held, rows)
        ),
        in_specs=[SMEM, ANY, VMEM, ANY, ANY, ANY],
        out_specs=(ANY, ANY, ANY),
        scratch_shapes=[pltpu.VMEM(state.shape, F32), pltpu.SemaphoreType.DMA((2,))],
        input_output_aliases={3: 0, 4: 1, 5: 2},
        compiler_params=PARAMS,
        cost_estimate=cost(0, 5 << 20),
        name="settle",
    )(unit, pages, state, pages_held, state_held, rows)


def cut_kernel(unit, weight_ref, kept, sent):
    half = weight_ref.shape[1] // 2
    for u, low_ref, high_ref in ((0, kept, sent), (1, sent, kept)):

        @pl.when(unit[0] == u)
        def _():
            low_ref[...] = weight_ref[:, :half]
            high_ref[...] = weight_ref[:, half:]


def cut(unit, weight):
    rows, width = weight.shape
    shape = jax.ShapeDtypeStruct((rows, width // 2), weight.dtype)
    return pl.pallas_call(
        cut_kernel,
        out_shape=(shape, shape),
        in_specs=[SMEM, VMEM],
        out_specs=(VMEM, VMEM),
        compiler_params=PARAMS,
        cost_estimate=cost(0, 3 << 20),
        name="cut",
    )(unit, weight)


def block_of(req, d, k, layers):
    layer, place = req // PLANE, req % PLANE
    source = ring_at((ring_place(layer, layers) + layers - k) % layers, layers)
    return source * PLANE + (place ^ d)


def spread_kernel(req, hidden, *refs):
    outs, sem = refs[:-1], refs[-1]
    rows, depth = outs[0].shape
    layers = sem.shape[0] // PLANE
    chip_rows = depth // layers
    copies = []
    for d in range(PLANE):
        for k in range(layers):
            column = pl.multiple_of(chip_rows * block_of(req[0], d, k, layers), 128)
            copies.append(
                pltpu.make_async_copy(
                    hidden.at[:, pl.ds(column, chip_rows)],
                    outs[d].at[:, k * chip_rows : (k + 1) * chip_rows],
                    sem.at[d * layers + k],
                )
            )
    for copy in copies:
        copy.start()
    for copy in copies:
        copy.wait()


def spread(req, hidden, chip_rows, layers):
    rows = hidden.shape[0]
    if chip_rows % 128:
        return [
            jnp.concatenate(
                [
                    lax.dynamic_slice(
                        hidden, (0, block_of(req[0], d, k, layers) * chip_rows), (rows, chip_rows)
                    )
                    for k in range(layers)
                ],
                axis=1,
            )
            for d in range(PLANE)
        ]
    return pl.pallas_call(
        spread_kernel,
        out_shape=(jax.ShapeDtypeStruct((rows, layers * chip_rows), hidden.dtype),) * PLANE,
        in_specs=[SMEM, ANY],
        out_specs=(VMEM,) * PLANE,
        scratch_shapes=[pltpu.SemaphoreType.DMA((PLANE * layers,))],
        compiler_params=PARAMS,
        cost_estimate=cost(0, 4 << 20),
        name="spread",
    )(req, hidden)


def place_rows(weight, pieces, unit):
    block_rows = pieces[0].shape[0] // 2
    for k, piece in enumerate(pieces):
        for which, place in ((0, unit), (1, 1 - unit)):
            at = pl.multiple_of((2 * k + place) * block_rows, 16)
            weight[pl.ds(at, block_rows), :] = piece[which * block_rows : (which + 1) * block_rows, :]


def begin_kernel(unit, *refs):
    hidden, weight = refs[: PLANE + 2], refs[-1]
    depth, width = weight.shape
    count = depth // refs[PLANE + 2].shape[0]
    pieces, (last_ref, *outs) = refs[PLANE + 2 : PLANE + 2 + count], refs[PLANE + 2 + count : -1]
    place_rows(weight, pieces, unit[0])
    rows = hidden[0].shape[0]
    for d in range(PLANE):
        place = d % (PLANE // 2) * rows
        other = hidden[PLANE + d // (PLANE // 2)][place : place + rows, :]
        both = jnp.concatenate([hidden[d][...], other], axis=0)
        span = slice(2 * d * rows, 2 * (d + 1) * rows)
        last_ref[span, :] = both[:, depth:]
        low = 0
        for out in outs:
            chunk = weight[:, low : low + out.shape[1]]
            out[span, :] = jnp.dot(both[:, :depth], chunk, preferred_element_type=F32)
            low += out.shape[1]


def begin(unit, hidden, pieces, widths):
    rows, depth = hidden[0].shape
    done = len(pieces) * pieces[0].shape[0]
    every = 2 * PLANE * rows
    outs = pl.pallas_call(
        begin_kernel,
        out_shape=(jax.ShapeDtypeStruct((every, depth - done), BF16),)
        + tuple(jax.ShapeDtypeStruct((every, w), F32) for w in widths),
        in_specs=[SMEM] + [VMEM] * (PLANE + 2 + len(pieces)),
        out_specs=(VMEM,) * (1 + len(widths)),
        scratch_shapes=[pltpu.VMEM((done, pieces[0].shape[1]), BF16)],
        compiler_params=PARAMS,
        cost_estimate=cost(0, 12 << 20),
        name="begin",
    )(unit, *hidden, *pieces)
    return outs[0], outs[1:]


def product_kernel(unit, hidden, partial, piece, own_ref, *refs):
    parts, weight = refs[:-1], refs[-1]
    place_rows(weight, [piece], unit[0])
    rows = own_ref.shape[0]
    for d in range(PLANE):
        span = slice(d * rows, (d + 1) * rows)
        result = partial[span, :] + jnp.dot(
            hidden[span, :], weight[...], preferred_element_type=F32
        )
        if d:
            parts[d - 1][...] = result.astype(BF16)
        else:
            own_ref[...] = result


def product(unit, hidden, partial, piece):
    rows, width = partial.shape[0] // PLANE, partial.shape[1]
    outs = pl.pallas_call(
        product_kernel,
        out_shape=(jax.ShapeDtypeStruct((rows, width), F32),)
        + (jax.ShapeDtypeStruct((rows, width), BF16),) * (PLANE - 1),
        in_specs=[SMEM] + [VMEM] * 3,
        out_specs=(VMEM,) * PLANE,
        scratch_shapes=[pltpu.VMEM(piece.shape, BF16)],
        compiler_params=PARAMS,
        cost_estimate=cost(0, 6 << 20),
        name="product",
    )(unit, hidden, partial, piece)
    return outs[0], outs[1:]


def total_kernel(own_ref, *refs):
    came, (keep_ref, send_ref) = refs[:-2], refs[-2:]
    total = own_ref[...]
    for ref in came:
        total = total + ref[...].astype(F32)
    rows = keep_ref.shape[0]
    keep_ref[...] = total[:rows]
    send_ref[...] = total[rows:].astype(BF16)


def total(own, came):
    rows, width = own.shape
    return pl.pallas_call(
        total_kernel,
        out_shape=(
            jax.ShapeDtypeStruct((rows // 2, width), F32),
            jax.ShapeDtypeStruct((rows // 2, width), BF16),
        ),
        in_specs=[VMEM] * (1 + len(came)),
        out_specs=(VMEM, VMEM),
        compiler_params=PARAMS,
        cost_estimate=cost(0, 4 << 20),
        name="total",
    )(own, *came)


def finish_kernel(unit, resid_ref, mixed_ref, low_ref, high_ref, *refs):
    count = len(refs) // 2
    kept, came, out_ref = refs[:count], refs[count:-1], refs[-1]
    half = out_ref.shape[1] // 2
    for u in range(2):

        @pl.when(unit[0] == u)
        def _():
            for group, which in ((kept, u), (came, 1 - u)):
                base = 0
                other_ref = high_ref if which else low_ref
                for ref in group:
                    span = slice(which * half + base, which * half + base + ref.shape[1])
                    mixed = mixed_ref[:, span].astype(F32)
                    mixed = mixed + other_ref[:, base : base + ref.shape[1]].astype(F32)
                    sums = resid_ref[:, span].astype(F32) + mixed + ref[...].astype(F32)
                    out_ref[:, span] = sums.astype(BF16)
                    base += ref.shape[1]


def finish(unit, resid, mixed, mixed_came, kept, came):
    return pl.pallas_call(
        finish_kernel,
        out_shape=jax.ShapeDtypeStruct(resid.shape, BF16),
        in_specs=[SMEM] + [VMEM] * (4 + len(kept) + len(came)),
        out_specs=VMEM,
        compiler_params=PARAMS,
        cost_estimate=cost(0, 4 << 20),
        name="finish",
    )(unit, resid, mixed, *mixed_came, *kept, *came)


def project_kernel(stay_ref, a_ref, b_ref, weight_ref, keep_ref, low_ref, high_ref):
    rows = stay_ref.shape[0]
    half = pl.num_programs(0) // 2
    came = jnp.concatenate([a_ref[...], b_ref[...]], axis=1)
    both = jnp.concatenate([stay_ref[...], came], axis=0)
    result = jnp.dot(both, weight_ref[...], preferred_element_type=F32).astype(BF16)
    keep_ref[...] = result[:rows]

    @pl.when(pl.program_id(0) < half)
    def _():
        low_ref[...] = result[rows:]

    @pl.when(pl.program_id(0) >= half)
    def _():
        high_ref[...] = result[rows:]


def project(stay, came_a, came_b, weight):
    rows, depth = stay.shape
    width = weight.shape[1]
    tile = 512 if width % 1024 == 0 else width // 2
    half = width // tile // 2
    fixed = [pl.BlockSpec(x.shape, lambda i: (0, 0)) for x in (stay, came_a, came_b)]
    return pl.pallas_call(
        project_kernel,
        grid=(2 * half,),
        out_shape=(
            jax.ShapeDtypeStruct((rows, width), BF16),
            jax.ShapeDtypeStruct((rows, width // 2), BF16),
            jax.ShapeDtypeStruct((rows, width // 2), BF16),
        ),
        in_specs=fixed + [pl.BlockSpec((depth, tile), lambda i: (0, i))],
        out_specs=(
            pl.BlockSpec((rows, tile), lambda i: (0, i)),
            pl.BlockSpec((rows, tile), lambda i: (0, jnp.minimum(i, half - 1))),
            pl.BlockSpec((rows, tile), lambda i: (0, jnp.maximum(i - half, 0))),
        ),
        compiler_params=PARAMS,
        cost_estimate=cost(0, 15 << 20),
        name="project",
    )(stay, came_a, came_b, weight)


def split_kernel(x_ref, *outs):
    base = 0
    for out in outs:
        out[...] = x_ref[:, base : base + out.shape[1]]
        base += out.shape[1]


def split_columns(x, widths):
    return pl.pallas_call(
        split_kernel,
        out_shape=tuple(jax.ShapeDtypeStruct((x.shape[0], w), x.dtype) for w in widths),
        in_specs=[VMEM],
        out_specs=(VMEM,) * len(widths),
        compiler_params=PARAMS,
        cost_estimate=cost(0, 2 << 20),
        name="split_columns",
    )(x)


def stack_kernel(*refs):
    *parts, out = refs
    rows = parts[0].shape[0]
    for i, part in enumerate(parts):
        out[i * rows : (i + 1) * rows, :] = part[...]


def stack_rows(parts):
    rows, width = parts[0].shape
    return pl.pallas_call(
        stack_kernel,
        out_shape=jax.ShapeDtypeStruct((len(parts) * rows, width), parts[0].dtype),
        in_specs=[VMEM] * len(parts),
        out_specs=VMEM,
        compiler_params=PARAMS,
        cost_estimate=cost(0, 2 << 20),
        name="stack_rows",
    )(*parts)


def swap_units(x):
    return lax.ppermute(x, "unit", [(0, 1), (1, 0)])


def after(x, *others):
    return lax.optimization_barrier((x, *others))[0]


def ring_at(step, length):
    if isinstance(step, int):
        return 2 * step - min(step, 1) if 2 * step <= length else 2 * (length - step)
    return jnp.where(2 * step <= length, 2 * step - jnp.minimum(step, 1), 2 * (length - step))


def ring_place(place, length):
    return jnp.where(place % 2 == 1, (place + 1) // 2, (length - place // 2) % length)


def chunk_widths(width):
    first, last = width // 4 // 128 * 128, width // 3 // 128 * 128
    return [first, width - first - last, last]


def on_device(
    queries,
    kv_new,
    kv_pool,
    page_table,
    ctx_pages,
    ssm_x,
    ssm_z,
    ssm_bc,
    dt_raw,
    dt_bias,
    decay_rate,
    skip_gain,
    ssm_state,
    ssm_norm_gain,
    resid,
    out_weight,
    ffn_hidden,
    down_weight,
    page_owner,
):
    tok_rows = queries.shape[0]
    n_req = lax.axis_size("req")
    block_rows, width = down_weight.shape
    u = lax.axis_index("unit")
    unit = u.reshape(1)
    req = lax.axis_index("req")
    layers = n_req // PLANE

    ring = [ring_at(i, layers) for i in range(layers)]
    ring_pairs = [
        (ring[i] * PLANE + p, ring[(i + 1) % layers] * PLANE + p)
        for i in range(layers)
        for p in range(PLANE)
    ]

    def pass_on(x):
        return lax.ppermute(x, "req", ring_pairs)

    kept, sent = cut(unit, down_weight)
    hops = [stack_rows([kept, swap_units(sent)])]
    if layers > 2:
        hops.append(pass_on(hops[0]))

    def plane_swap(x, d):
        return lax.ppermute(
            x, "req", [(r, r - r % PLANE + ((r % PLANE) ^ d)) for r in range(n_req)]
        )

    mine = spread(req.reshape(1), after(ffn_hidden, hops[0]), 2 * block_rows, layers)
    hidden = [plane_swap(x, d) if d else x for d, x in enumerate(mine)]
    attn, pages_held, pages_leave = attend(
        page_table, ctx_pages, page_owner[:, :, 0], unit, after(queries, mine[0]), kv_new, kv_pool
    )
    while len(hops) < layers - 1:
        hops.append(pass_on(after(hops[-1], attn)))
    stay, leave_a, leave_b, state_held, state_leave = state_space(
        unit,
        skip_gain,
        after(attn, *hops[1:2]),
        ssm_x,
        ssm_z,
        ssm_bc,
        dt_raw,
        dt_bias[None, :],
        decay_rate[None, :],
        ssm_norm_gain[None, :],
        ssm_state,
    )
    hidden = after(hidden, stay)
    leave_came = [swap_units(x) for x in after((leave_a, leave_b), *hidden)]
    pair = PLANE // 2
    gathered = [after(stack_rows(x), *leave_came) for x in (hidden[:pair], hidden[pair:])]
    swapped = [swap_units(x) for x in gathered]
    hidden = list(hidden) + swapped
    mixed, *mixed_leave = project(stay, *leave_came, out_weight)
    state_leave, pages_leave = after((state_leave, pages_leave), stay)
    state_came, pages_came = swap_units(state_leave), swap_units(pages_leave)
    mixed_came = [
        swap_units(x) for x in after(mixed_leave, hops[-1], state_came, pages_came, *swapped)
    ]
    widths = chunk_widths(width // 2)
    ends = [pass_on(x) for x in split_columns(after(hops[-1], mixed), widths)]
    decode_kv, decode_state, mixed = settle(
        unit, pages_came, state_came, pages_held, state_held, mixed
    )
    last_hidden, partial = begin(unit, hidden, hops, widths)
    sums, order, received = [], [mixed, *mixed_came], []
    for n, (piece, end) in enumerate(zip(partial, ends)):
        own, parts = product(unit, last_hidden, piece, after(end, *order))
        order = list(parts) + [x[0] for x in sums]
        if received:
            parts = after(parts, *(received if n < len(ends) - 1 else received[:1]))
        received = [plane_swap(x, d) for d, x in enumerate(parts, 1)]
        token = sums[-1][0] if sums else own
        sums.append(total(own, after(received, token)))
    kept, leave = zip(*sums)
    came = [swap_units(x) for x in leave]
    layer_out = finish(unit, resid, mixed, mixed_came, kept, came)
    return (layer_out, decode_kv, decode_state)


def solution(mesh):
    return jax.shard_map(
        on_device,
        mesh=mesh,
        in_specs=(
            P(("req", "unit"), None),
            P(("req", "unit"), None),
            P(("req", "unit"), None, None),
            P(("req", "unit"), None),
            P(("req", "unit")),
            P(("req", "unit"), None),
            P(("req", "unit"), None),
            P(("req", "unit"), None),
            P(("req", "unit"), None),
            P(),
            P(),
            P(),
            P(("req", "unit"), None, None, None),
            P(),
            P(("req", "unit"), None),
            P("unit", None),
            P(("req", "unit"), None),
            P(("req", "unit"), None),
            P(("req", "unit"), None, None),
        ),
        out_specs=(
            P(("req", "unit"), None),
            P(("req", "unit"), None, None),
            P("req", "unit", None, None),
        ),
        check_vma=False,
    )
```

```python
import functools
import math

import jax
import jax.numpy as jnp
from jax import lax
from jax.experimental import pallas as pl
from jax.experimental.pallas import tpu as pltpu
from jax.sharding import PartitionSpec as P

QUERY_HEADS = 12
KEY_VALUE_HEADS = 2
HEAD_WIDTH = 128
MIXER_HEADS = 24
PM = 128
NS = 256

PLANE = 4

norm_eps = 1e-05

F32, BF16 = jnp.float32, jnp.bfloat16
VMEM = pl.BlockSpec(memory_space=pltpu.VMEM)
SMEM = pl.BlockSpec(memory_space=pltpu.SMEM)
ANY = pl.BlockSpec(memory_space=pl.ANY)
PARAMS = pltpu.CompilerParams(vmem_limit_bytes=48 * 1024 * 1024)


def cost(flops, moved, exps=0):
    return pl.CostEstimate(flops=0, bytes_accessed=0, transcendentals=0)


def contract_last(a, b):
    return lax.dot_general(a, b, (((1,), (1,)), ((), ())), preferred_element_type=F32)


def two_terms(x):
    high = x.astype(BF16)
    return high, (x - high.astype(F32)).astype(BF16)


def attend_kernel(
    table, ctx, owner, unit, q_ref, new_ref, pool, out_ref, held, leave, pages, zero, sems, osems
):
    count, length, _ = pages.shape
    slots = leave.shape[0]
    live = ctx[0]
    u = unit[0]
    for j in range(count):

        @pl.when(j == live)
        def _():
            pltpu.make_async_copy(new_ref, pages.at[j], sems.at[j]).start()

        @pl.when(j != live)
        def _():
            pltpu.make_async_copy(pool.at[table[0, j]], pages.at[j], sems.at[j]).start()

    zero[...] = jnp.zeros_like(zero)
    for j in range(count):
        pltpu.make_async_copy(new_ref, pages.at[j], sems.at[j]).wait()

    named = [jnp.int32(0), jnp.int32(0)]
    for j in range(count):
        own = owner[0, j] == u
        rank = jnp.where(own, named[0], named[1])
        named = [named[0] + own.astype(jnp.int32), named[1] + 1 - own.astype(jnp.int32)]
        for source, when in ((pages.at[j], j <= live), (zero, j > live)):

            @pl.when(when & own)
            def _():
                pltpu.make_async_copy(source, held.at[u * slots + rank], osems.at[j]).start()

            @pl.when(when & jnp.logical_not(own))
            def _():
                pltpu.make_async_copy(source, leave.at[rank], osems.at[j]).start()

    for k in range(slots):

        @pl.when(k >= named[0])
        def _():
            pltpu.make_async_copy(zero, held.at[u * slots + k], osems.at[count + k]).start()

        @pl.when(k >= named[1])
        def _():
            pltpu.make_async_copy(zero, leave.at[k], osems.at[count + slots + k]).start()

    group = QUERY_HEADS // KEY_VALUE_HEADS
    heads = 3
    rows, keys = heads * length, count * length
    limit = live * length + lax.broadcasted_iota(jnp.int32, (rows, 1), 0) % length
    visible = lax.broadcasted_iota(jnp.int32, (rows, keys), 1) <= limit
    scale = 1.0 / math.sqrt(HEAD_WIDTH)
    for k in range(KEY_VALUE_HEADS):
        key_rows = pages[:, :, k * HEAD_WIDTH : (k + 1) * HEAD_WIDTH].reshape(keys, HEAD_WIDTH)
        lo = (KEY_VALUE_HEADS + k) * HEAD_WIDTH
        value_rows = pages[:, :, lo : lo + HEAD_WIDTH].reshape(keys, HEAD_WIDTH)
        for first in range(k * group, (k + 1) * group, heads):
            spans = [
                slice(h * HEAD_WIDTH, (h + 1) * HEAD_WIDTH) for h in range(first, first + heads)
            ]
            q = jnp.concatenate([q_ref[:, span] for span in spans], axis=0)
            scores = jnp.where(visible, contract_last(q, key_rows), -1e30)
            top = jnp.max(scores, axis=1, keepdims=True)
            exponent = jnp.exp((scores - top) * scale)
            weights = (exponent * (1.0 / jnp.sum(exponent, axis=1, keepdims=True))).astype(BF16)
            attended = jnp.dot(weights, value_rows, preferred_element_type=F32).astype(BF16)
            for i, span in enumerate(spans):
                out_ref[:, span] = attended[i * length : (i + 1) * length]

    for j in range(count):
        pltpu.make_async_copy(zero, leave.at[0], osems.at[j]).wait()
    for k in range(slots):

        @pl.when(k >= named[0])
        def _():
            pltpu.make_async_copy(zero, leave.at[0], osems.at[count + k]).wait()

        @pl.when(k >= named[1])
        def _():
            pltpu.make_async_copy(zero, leave.at[0], osems.at[count + slots + k]).wait()


def attend(table, ctx, owner, unit, queries, kv_new, pool):
    count, length, width = pool.shape
    slots = max(2, (count + 1) // 2)
    pairs = QUERY_HEADS * length * count * length
    return pl.pallas_call(
        attend_kernel,
        out_shape=(
            jax.ShapeDtypeStruct(queries.shape, BF16),
            jax.ShapeDtypeStruct((2 * slots, length, width), BF16),
            jax.ShapeDtypeStruct((slots, length, width), BF16),
        ),
        in_specs=[SMEM, SMEM, SMEM, SMEM, VMEM, VMEM, ANY],
        out_specs=(VMEM, ANY, ANY),
        scratch_shapes=[
            pltpu.VMEM((count, length, width), BF16),
            pltpu.VMEM((length, width), BF16),
            pltpu.SemaphoreType.DMA((count,)),
            pltpu.SemaphoreType.DMA((count + 2 * slots,)),
        ],
        compiler_params=PARAMS,
        cost_estimate=cost(4 * pairs * HEAD_WIDTH * 4, 6 << 20, pairs),
        name="attend",
    )(table, ctx, owner, unit, queries, kv_new, pool)


def state_kernel(
    unit,
    skip,
    attn_ref,
    x_ref,
    z_ref,
    bc_ref,
    dt_ref,
    bias_ref,
    rate_ref,
    gain_ref,
    state_ref,
    stay_ref,
    leave_a,
    leave_b,
    held,
    send_ref,
    gated,
    fresh,
    sems,
):
    length = x_ref.shape[0]
    heads, share = MIXER_HEADS, MIXER_HEADS // 2
    u = unit[0]
    rows = lax.broadcasted_iota(jnp.int32, (length, length), 0)
    cols = lax.broadcasted_iota(jnp.int32, (length, length), 1)
    causal = rows >= cols
    raw = dt_ref[...] + bias_ref[...]
    step = jnp.maximum(raw, 0.0) + jnp.log1p(jnp.exp(-jnp.abs(raw)))
    cum = jnp.dot(
        causal.astype(F32),
        -step * rate_ref[...],
        precision=lax.Precision.HIGHEST,
        preferred_element_type=F32,
    )
    blank = jnp.zeros((length, length - heads), F32)
    cum_rows = jnp.transpose(jnp.concatenate([cum, blank], axis=1))
    step_rows = jnp.transpose(jnp.concatenate([step, blank], axis=1))
    last = cum[length - 1 : length, :]
    b_rows, c_rows = bc_ref[:, :NS], bc_ref[:, NS:]
    dots = contract_last(c_rows, b_rows)
    square = jnp.zeros((length, PM), F32)
    for h in range(heads):
        span = slice(h * PM, (h + 1) * PM)
        cum_t, cum_s = cum[:, h : h + 1], cum_rows[h : h + 1, :]
        step_s, end = step_rows[h : h + 1, :], last[:, h : h + 1]
        decay = jnp.exp(jnp.where(causal, cum_t - cum_s, -1e30))
        mixing = (dots * decay * step_s).astype(BF16)
        x = x_ref[:, span]
        x_float = x.astype(F32)
        prior = state_ref[0, h]
        high, low = two_terms(prior)
        carried = contract_last(c_rows, high) + contract_last(c_rows, low)
        y = jnp.dot(mixing, x, preferred_element_type=F32)
        y = y + carried * jnp.exp(cum_t) + skip[h] * x_float
        z = z_ref[:, span].astype(F32)
        g = y * (z / (1.0 + jnp.exp(-z)))
        gated[:, span] = g
        square = square + g * g
        weighted = jnp.transpose(x_float) * (jnp.exp(end - cum_s) * step_s)
        high, low = two_terms(weighted)
        new = jnp.exp(end) * prior + (
            jnp.dot(high, b_rows, preferred_element_type=F32)
            + jnp.dot(low, b_rows, preferred_element_type=F32)
        )
        place = h % share

        @pl.when(u == h // share)
        def _():
            fresh[place] = new
            pltpu.make_async_copy(fresh.at[place], held.at[u, place], sems.at[place]).start()

        @pl.when(u != h // share)
        def _():
            send_ref[place] = new.astype(BF16)

    mean = jnp.sum(square, axis=1, keepdims=True) * (1.0 / (heads * PM))
    out = (gated[...] * lax.rsqrt(mean + norm_eps) * gain_ref[...]).astype(BF16)
    attn_width = attn_ref.shape[1]
    cut = stay_ref.shape[1] - attn_width
    part = leave_a.shape[1]

    @pl.when(u == 0)
    def _():
        stay_ref[:, :attn_width] = attn_ref[...]
        stay_ref[:, attn_width:] = out[:, :cut]
        leave_a[...] = out[:, cut : cut + part]
        leave_b[...] = out[:, cut + part :]

    @pl.when(u == 1)
    def _():
        stay_ref[...] = out[:, cut:]
        leave_a[...] = attn_ref[:, :part]
        leave_b[:, : attn_width - part] = attn_ref[:, part:]
        leave_b[:, attn_width - part :] = out[:, :cut]

    for place in range(share):
        pltpu.make_async_copy(fresh.at[place], held.at[0, place], sems.at[place]).wait()


def state_space(unit, skip, attn, x, z, bc, dt, bias, rate, gain, state):
    length, width = x.shape
    share = MIXER_HEADS // 2
    half = (attn.shape[1] + width) // 2
    return pl.pallas_call(
        state_kernel,
        out_shape=(
            jax.ShapeDtypeStruct((length, half), BF16),
            jax.ShapeDtypeStruct((length, half // 2), BF16),
            jax.ShapeDtypeStruct((length, half - half // 2), BF16),
            jax.ShapeDtypeStruct((2, share, PM, NS), F32),
            jax.ShapeDtypeStruct((share, PM, NS), BF16),
        ),
        in_specs=[SMEM, SMEM] + [VMEM] * 9,
        out_specs=(VMEM, VMEM, VMEM, ANY, VMEM),
        scratch_shapes=[
            pltpu.VMEM((length, width), F32),
            pltpu.VMEM((share, PM, NS), F32),
            pltpu.SemaphoreType.DMA((share,)),
        ],
        compiler_params=PARAMS,
        cost_estimate=cost(4 << 30, 10 << 20, MIXER_HEADS * length * length * 2),
        name="state_space",
    )(unit, skip, attn, x, z, bc, dt, bias, rate, gain, state)


def settle_kernel(
    unit, pages, state, pages_in, state_in, rows_in, pages_out, state_out, rows_out, wide, sem
):
    slots = pages.shape[0]
    u = unit[0]
    copy = pltpu.make_async_copy(pages, pages_out.at[pl.ds((1 - u) * slots, slots)], sem.at[0])
    copy.start()
    wide[...] = state[...].astype(F32)
    other = pltpu.make_async_copy(wide, state_out.at[1 - u], sem.at[1])
    other.start()
    copy.wait()
    other.wait()


def settle(unit, pages, state, pages_held, state_held, rows):
    return pl.pallas_call(
        settle_kernel,
        out_shape=tuple(
            jax.ShapeDtypeStruct(x.shape, x.dtype) for x in (pages_held, state_held, rows)
        ),
        in_specs=[SMEM, ANY, VMEM, ANY, ANY, ANY],
        out_specs=(ANY, ANY, ANY),
        scratch_shapes=[pltpu.VMEM(state.shape, F32), pltpu.SemaphoreType.DMA((2,))],
        input_output_aliases={3: 0, 4: 1, 5: 2},
        compiler_params=PARAMS,
        cost_estimate=cost(0, 5 << 20),
        name="settle",
    )(unit, pages, state, pages_held, state_held, rows)


def cut_kernel(unit, weight_ref, kept, sent):
    half = weight_ref.shape[1] // 2
    for u, low_ref, high_ref in ((0, kept, sent), (1, sent, kept)):

        @pl.when(unit[0] == u)
        def _():
            low_ref[...] = weight_ref[:, :half]
            high_ref[...] = weight_ref[:, half:]


def cut(unit, weight):
    rows, width = weight.shape
    shape = jax.ShapeDtypeStruct((rows, width // 2), weight.dtype)
    return pl.pallas_call(
        cut_kernel,
        out_shape=(shape, shape),
        in_specs=[SMEM, VMEM],
        out_specs=(VMEM, VMEM),
        compiler_params=PARAMS,
        cost_estimate=cost(0, 3 << 20),
        name="cut",
    )(unit, weight)


def block_of(req, d, k, layers):
    layer, place = req // PLANE, req % PLANE
    source = ring_at((ring_place(layer, layers) + layers - k) % layers, layers)
    return source * PLANE + (place ^ d)


def spread_kernel(req, hidden, *refs):
    outs, sem = refs[:-1], refs[-1]
    rows, depth = outs[0].shape
    layers = sem.shape[0] // PLANE
    chip_rows = depth // layers
    copies = []
    for d in range(PLANE):
        for k in range(layers):
            column = pl.multiple_of(chip_rows * block_of(req[0], d, k, layers), 128)
            copies.append(
                pltpu.make_async_copy(
                    hidden.at[:, pl.ds(column, chip_rows)],
                    outs[d].at[:, k * chip_rows : (k + 1) * chip_rows],
                    sem.at[d * layers + k],
                )
            )
    for copy in copies:
        copy.start()
    for copy in copies:
        copy.wait()


def spread(req, hidden, chip_rows, layers):
    rows = hidden.shape[0]
    if chip_rows % 128:
        return [
            jnp.concatenate(
                [
                    lax.dynamic_slice(
                        hidden, (0, block_of(req[0], d, k, layers) * chip_rows), (rows, chip_rows)
                    )
                    for k in range(layers)
                ],
                axis=1,
            )
            for d in range(PLANE)
        ]
    return pl.pallas_call(
        spread_kernel,
        out_shape=(jax.ShapeDtypeStruct((rows, layers * chip_rows), hidden.dtype),) * PLANE,
        in_specs=[SMEM, ANY],
        out_specs=(VMEM,) * PLANE,
        scratch_shapes=[pltpu.SemaphoreType.DMA((PLANE * layers,))],
        compiler_params=PARAMS,
        cost_estimate=cost(0, 4 << 20),
        name="spread",
    )(req, hidden)


def place_rows(weight, pieces, unit, low=0):
    block_rows, width = pieces[0].shape[0] // 2, weight.shape[1]
    for k, piece in enumerate(pieces):
        for which, place in ((0, unit), (1, 1 - unit)):
            at = pl.multiple_of((2 * k + place) * block_rows, 16)
            rows = slice(which * block_rows, (which + 1) * block_rows)
            weight[pl.ds(at, block_rows), :] = piece[rows, low : low + width]


def order_kernel(*refs):
    hidden, (front_ref, last_ref) = refs[:-2], refs[-2:]
    rows, done = hidden[0].shape[0], front_ref.shape[1]
    for d in range(PLANE):
        place = d % (PLANE // 2) * rows
        pair = hidden[PLANE + d // (PLANE // 2)]
        for n, block in ((0, hidden[d][...]), (1, pair[place : place + rows, :])):
            span = slice((2 * d + n) * rows, (2 * d + n + 1) * rows)
            front_ref[span, :] = block[:, :done]
            last_ref[span, :] = block[:, done:]


def order_rows(hidden, done):
    rows, depth = hidden[0].shape
    every = 2 * PLANE * rows
    return pl.pallas_call(
        order_kernel,
        out_shape=(
            jax.ShapeDtypeStruct((every, done), BF16),
            jax.ShapeDtypeStruct((every, depth - done), BF16),
        ),
        in_specs=[VMEM] * len(hidden),
        out_specs=(VMEM, VMEM),
        compiler_params=PARAMS,
        cost_estimate=cost(0, 6 << 20),
        name="order_rows",
    )(*hidden)


def begin_kernel(low, unit, front, *refs):
    pieces, (out, weight) = refs[:-2], refs[-2:]
    place_rows(weight, pieces, unit[0], low)
    rows = out.shape[0] // PLANE
    for d in range(PLANE):
        span = slice(d * rows, (d + 1) * rows)
        out[span, :] = jnp.dot(front[span, :], weight[...], preferred_element_type=F32)


def begin(unit, front, pieces, low, width):
    every, done = front.shape
    return pl.pallas_call(
        functools.partial(begin_kernel, low),
        out_shape=jax.ShapeDtypeStruct((every, width), F32),
        in_specs=[SMEM] + [VMEM] * (1 + len(pieces)),
        out_specs=VMEM,
        scratch_shapes=[pltpu.VMEM((done, width), BF16)],
        compiler_params=PARAMS,
        cost_estimate=cost(0, 8 << 20),
        name="begin",
    )(unit, front, *pieces)


def product_kernel(unit, hidden, partial, piece, own_ref, *refs):
    parts, weight = refs[:-1], refs[-1]
    place_rows(weight, [piece], unit[0])
    rows = own_ref.shape[0]
    for d in range(PLANE):
        span = slice(d * rows, (d + 1) * rows)
        result = partial[span, :] + jnp.dot(
            hidden[span, :], weight[...], preferred_element_type=F32
        )
        if d:
            parts[d - 1][...] = result.astype(BF16)
        else:
            own_ref[...] = result


def product(unit, hidden, partial, piece):
    rows, width = partial.shape[0] // PLANE, partial.shape[1]
    outs = pl.pallas_call(
        product_kernel,
        out_shape=(jax.ShapeDtypeStruct((rows, width), F32),)
        + (jax.ShapeDtypeStruct((rows, width), BF16),) * (PLANE - 1),
        in_specs=[SMEM] + [VMEM] * 3,
        out_specs=(VMEM,) * PLANE,
        scratch_shapes=[pltpu.VMEM(piece.shape, BF16)],
        compiler_params=PARAMS,
        cost_estimate=cost(0, 6 << 20),
        name="product",
    )(unit, hidden, partial, piece)
    return outs[0], outs[1:]


def total_kernel(own_ref, *refs):
    came, (keep_ref, send_ref) = refs[:-2], refs[-2:]
    total = own_ref[...]
    for ref in came:
        total = total + ref[...].astype(F32)
    rows = keep_ref.shape[0]
    keep_ref[...] = total[:rows]
    send_ref[...] = total[rows:].astype(BF16)


def total(own, came):
    rows, width = own.shape
    return pl.pallas_call(
        total_kernel,
        out_shape=(
            jax.ShapeDtypeStruct((rows // 2, width), F32),
            jax.ShapeDtypeStruct((rows // 2, width), BF16),
        ),
        in_specs=[VMEM] * (1 + len(came)),
        out_specs=(VMEM, VMEM),
        compiler_params=PARAMS,
        cost_estimate=cost(0, 4 << 20),
        name="total",
    )(own, *came)


def finish_kernel(unit, resid_ref, mixed_ref, low_ref, high_ref, *refs):
    count = len(refs) // 2
    kept, came, out_ref = refs[:count], refs[count:-1], refs[-1]
    half = out_ref.shape[1] // 2
    for u in range(2):

        @pl.when(unit[0] == u)
        def _():
            for group, which in ((kept, u), (came, 1 - u)):
                base = 0
                other_ref = high_ref if which else low_ref
                for ref in group:
                    span = slice(which * half + base, which * half + base + ref.shape[1])
                    mixed = mixed_ref[:, span].astype(F32)
                    mixed = mixed + other_ref[:, base : base + ref.shape[1]].astype(F32)
                    sums = resid_ref[:, span].astype(F32) + mixed + ref[...].astype(F32)
                    out_ref[:, span] = sums.astype(BF16)
                    base += ref.shape[1]


def finish(unit, resid, mixed, mixed_came, kept, came):
    return pl.pallas_call(
        finish_kernel,
        out_shape=jax.ShapeDtypeStruct(resid.shape, BF16),
        in_specs=[SMEM] + [VMEM] * (4 + len(kept) + len(came)),
        out_specs=VMEM,
        compiler_params=PARAMS,
        cost_estimate=cost(0, 4 << 20),
        name="finish",
    )(unit, resid, mixed, *mixed_came, *kept, *came)


def project_kernel(stay_ref, a_ref, b_ref, weight_ref, keep_ref, low_ref, high_ref):
    rows = stay_ref.shape[0]
    half = pl.num_programs(0) // 2
    came = jnp.concatenate([a_ref[...], b_ref[...]], axis=1)
    both = jnp.concatenate([stay_ref[...], came], axis=0)
    result = jnp.dot(both, weight_ref[...], preferred_element_type=F32).astype(BF16)
    keep_ref[...] = result[:rows]

    @pl.when(pl.program_id(0) < half)
    def _():
        low_ref[...] = result[rows:]

    @pl.when(pl.program_id(0) >= half)
    def _():
        high_ref[...] = result[rows:]


def project(stay, came_a, came_b, weight):
    rows, depth = stay.shape
    width = weight.shape[1]
    tile = 512 if width % 1024 == 0 else width // 2
    half = width // tile // 2
    fixed = [pl.BlockSpec(x.shape, lambda i: (0, 0)) for x in (stay, came_a, came_b)]
    return pl.pallas_call(
        project_kernel,
        grid=(2 * half,),
        out_shape=(
            jax.ShapeDtypeStruct((rows, width), BF16),
            jax.ShapeDtypeStruct((rows, width // 2), BF16),
            jax.ShapeDtypeStruct((rows, width // 2), BF16),
        ),
        in_specs=fixed + [pl.BlockSpec((depth, tile), lambda i: (0, i))],
        out_specs=(
            pl.BlockSpec((rows, tile), lambda i: (0, i)),
            pl.BlockSpec((rows, tile), lambda i: (0, jnp.minimum(i, half - 1))),
            pl.BlockSpec((rows, tile), lambda i: (0, jnp.maximum(i - half, 0))),
        ),
        compiler_params=PARAMS,
        cost_estimate=cost(0, 15 << 20),
        name="project",
    )(stay, came_a, came_b, weight)


def split_kernel(x_ref, *outs):
    base = 0
    for out in outs:
        out[...] = x_ref[:, base : base + out.shape[1]]
        base += out.shape[1]


def split_columns(x, widths):
    return pl.pallas_call(
        split_kernel,
        out_shape=tuple(jax.ShapeDtypeStruct((x.shape[0], w), x.dtype) for w in widths),
        in_specs=[VMEM],
        out_specs=(VMEM,) * len(widths),
        compiler_params=PARAMS,
        cost_estimate=cost(0, 2 << 20),
        name="split_columns",
    )(x)


def stack_kernel(*refs):
    *parts, out = refs
    rows = parts[0].shape[0]
    for i, part in enumerate(parts):
        out[i * rows : (i + 1) * rows, :] = part[...]


def stack_rows(parts):
    rows, width = parts[0].shape
    return pl.pallas_call(
        stack_kernel,
        out_shape=jax.ShapeDtypeStruct((len(parts) * rows, width), parts[0].dtype),
        in_specs=[VMEM] * len(parts),
        out_specs=VMEM,
        compiler_params=PARAMS,
        cost_estimate=cost(0, 2 << 20),
        name="stack_rows",
    )(*parts)


def swap_units(x):
    return lax.ppermute(x, "unit", [(0, 1), (1, 0)])


def after(x, *others):
    return lax.optimization_barrier((x, *others))[0]


def ring_at(step, length):
    if isinstance(step, int):
        return 2 * step - min(step, 1) if 2 * step <= length else 2 * (length - step)
    return jnp.where(2 * step <= length, 2 * step - jnp.minimum(step, 1), 2 * (length - step))


def ring_place(place, length):
    return jnp.where(place % 2 == 1, (place + 1) // 2, (length - place // 2) % length)


def chunk_widths(width):
    first, last = width // 4 // 128 * 128, width // 3 // 128 * 128
    return [first, width - first - last, last]


def on_device(
    queries,
    kv_new,
    kv_pool,
    page_table,
    ctx_pages,
    ssm_x,
    ssm_z,
    ssm_bc,
    dt_raw,
    dt_bias,
    decay_rate,
    skip_gain,
    ssm_state,
    ssm_norm_gain,
    resid,
    out_weight,
    ffn_hidden,
    down_weight,
    page_owner,
):
    tok_rows = queries.shape[0]
    n_req = lax.axis_size("req")
    block_rows, width = down_weight.shape
    u = lax.axis_index("unit")
    unit = u.reshape(1)
    req = lax.axis_index("req")
    layers = n_req // PLANE

    ring = [ring_at(i, layers) for i in range(layers)]
    ring_pairs = [
        (ring[i] * PLANE + p, ring[(i + 1) % layers] * PLANE + p)
        for i in range(layers)
        for p in range(PLANE)
    ]

    def pass_on(x):
        return lax.ppermute(x, "req", ring_pairs)

    kept, sent = cut(unit, down_weight)
    hops = [stack_rows([kept, swap_units(sent)])]
    if layers > 2:
        hops.append(pass_on(hops[0]))

    def plane_swap(x, d):
        return lax.ppermute(
            x, "req", [(r, r - r % PLANE + ((r % PLANE) ^ d)) for r in range(n_req)]
        )

    mine = spread(req.reshape(1), after(ffn_hidden, hops[0]), 2 * block_rows, layers)
    hidden = [plane_swap(x, d) if d else x for d, x in enumerate(mine)]
    attn, pages_held, pages_leave = attend(
        page_table, ctx_pages, page_owner[:, :, 0], unit, after(queries, mine[0]), kv_new, kv_pool
    )
    while len(hops) < layers - 1:
        hops.append(pass_on(after(hops[-1], attn)))
    stay, leave_a, leave_b, state_held, state_leave = state_space(
        unit,
        skip_gain,
        after(attn, *hops[1:2]),
        ssm_x,
        ssm_z,
        ssm_bc,
        dt_raw,
        dt_bias[None, :],
        decay_rate[None, :],
        ssm_norm_gain[None, :],
        ssm_state,
    )
    hidden = after(hidden, stay)
    leave_came = [swap_units(x) for x in after((leave_a, leave_b), *hidden)]
    pair = PLANE // 2
    gathered = [after(stack_rows(x), *leave_came) for x in (hidden[:pair], hidden[pair:])]
    swapped = [swap_units(x) for x in gathered]
    hidden = list(hidden) + swapped
    mixed, *mixed_leave = project(stay, *leave_came, out_weight)
    state_leave, pages_leave = after((state_leave, pages_leave), stay)
    state_came, pages_came = swap_units(state_leave), swap_units(pages_leave)
    mixed_came = [
        swap_units(x) for x in after(mixed_leave, hops[-1], state_came, pages_came, *swapped)
    ]
    widths = chunk_widths(width // 2)
    ends = [pass_on(x) for x in split_columns(after(hops[-1], mixed), widths)]
    done = len(hops) * hops[0].shape[0]
    front, last_hidden = order_rows(hidden, done)
    sums, order, received, low = [], mixed_came, [], 0
    for n, end in enumerate(ends):
        if n == 1:
            decode_kv, decode_state, mixed = settle(
                unit, pages_came, state_came, pages_held, state_held, after(mixed, *order)
            )
            order = order + [mixed]
        piece = begin(unit, after(front, *order) if n else front, hops, low, widths[n])
        own, parts = product(unit, last_hidden, piece, after(end, piece, *order))
        order, low = list(parts) + [x[0] for x in sums], low + widths[n]
        if received:
            parts = after(parts, *(received if n < len(ends) - 1 else received[:1]))
        received = [plane_swap(x, d) for d, x in enumerate(parts, 1)]
        token = sums[-1][0] if sums else own
        sums.append(total(own, after(received, token)))
    kept, leave = zip(*sums)
    came = [swap_units(x) for x in leave]
    layer_out = finish(unit, resid, mixed, mixed_came, kept, came)
    return (layer_out, decode_kv, decode_state)


def solution(mesh):
    return jax.shard_map(
        on_device,
        mesh=mesh,
        in_specs=(
            P(("req", "unit"), None),
            P(("req", "unit"), None),
            P(("req", "unit"), None, None),
            P(("req", "unit"), None),
            P(("req", "unit")),
            P(("req", "unit"), None),
            P(("req", "unit"), None),
            P(("req", "unit"), None),
            P(("req", "unit"), None),
            P(),
            P(),
            P(),
            P(("req", "unit"), None, None, None),
            P(),
            P(("req", "unit"), None),
            P("unit", None),
            P(("req", "unit"), None),
            P(("req", "unit"), None),
            P(("req", "unit"), None, None),
        ),
        out_specs=(
            P(("req", "unit"), None),
            P(("req", "unit"), None, None),
            P("req", "unit", None, None),
        ),
        check_vma=False,
    )
```

```python
import functools
import math

import jax
import jax.numpy as jnp
from jax import lax
from jax.experimental import pallas as pl
from jax.experimental.pallas import tpu as pltpu
from jax.sharding import PartitionSpec as P

QUERY_HEADS = 12
KEY_VALUE_HEADS = 2
HEAD_WIDTH = 128
MIXER_HEADS = 24
PM = 128
NS = 256

PLANE = 4

norm_eps = 1e-05

F32, BF16 = jnp.float32, jnp.bfloat16
VMEM = pl.BlockSpec(memory_space=pltpu.VMEM)
SMEM = pl.BlockSpec(memory_space=pltpu.SMEM)
ANY = pl.BlockSpec(memory_space=pl.ANY)
PARAMS = pltpu.CompilerParams(vmem_limit_bytes=24 * 1024 * 1024)


def cost(flops, moved, exps=0):
    return pl.CostEstimate(flops=0, bytes_accessed=0, transcendentals=0)


def contract_last(a, b):
    return lax.dot_general(a, b, (((1,), (1,)), ((), ())), preferred_element_type=F32)


def two_terms(x):
    high = x.astype(BF16)
    return high, (x - high.astype(F32)).astype(BF16)


def attend_kernel(
    table, ctx, owner, unit, q_ref, new_ref, pool, out_ref, held, leave, pages, zero, sems, osems
):
    count, length, _ = pages.shape
    slots = leave.shape[0]
    live = ctx[0]
    u = unit[0]
    for j in range(count):

        @pl.when(j == live)
        def _():
            pltpu.make_async_copy(new_ref, pages.at[j], sems.at[j]).start()

        @pl.when(j != live)
        def _():
            pltpu.make_async_copy(pool.at[table[0, j]], pages.at[j], sems.at[j]).start()

    zero[...] = jnp.zeros_like(zero)
    for j in range(count):
        pltpu.make_async_copy(new_ref, pages.at[j], sems.at[j]).wait()

    named = [jnp.int32(0), jnp.int32(0)]
    for j in range(count):
        own = owner[0, j] == u
        rank = jnp.where(own, named[0], named[1])
        named = [named[0] + own.astype(jnp.int32), named[1] + 1 - own.astype(jnp.int32)]
        for source, when in ((pages.at[j], j <= live), (zero, j > live)):

            @pl.when(when & own)
            def _():
                pltpu.make_async_copy(source, held.at[u * slots + rank], osems.at[j]).start()

            @pl.when(when & jnp.logical_not(own))
            def _():
                pltpu.make_async_copy(source, leave.at[rank], osems.at[j]).start()

    for k in range(slots):

        @pl.when(k >= named[0])
        def _():
            pltpu.make_async_copy(zero, held.at[u * slots + k], osems.at[count + k]).start()

        @pl.when(k >= named[1])
        def _():
            pltpu.make_async_copy(zero, leave.at[k], osems.at[count + slots + k]).start()

    group = QUERY_HEADS // KEY_VALUE_HEADS
    heads = 3
    rows, keys = heads * length, count * length
    limit = live * length + lax.broadcasted_iota(jnp.int32, (rows, 1), 0) % length
    visible = lax.broadcasted_iota(jnp.int32, (rows, keys), 1) <= limit
    scale = 1.0 / math.sqrt(HEAD_WIDTH)
    for k in range(KEY_VALUE_HEADS):
        key_rows = pages[:, :, k * HEAD_WIDTH : (k + 1) * HEAD_WIDTH].reshape(keys, HEAD_WIDTH)
        lo = (KEY_VALUE_HEADS + k) * HEAD_WIDTH
        value_rows = pages[:, :, lo : lo + HEAD_WIDTH].reshape(keys, HEAD_WIDTH)
        for first in range(k * group, (k + 1) * group, heads):
            spans = [
                slice(h * HEAD_WIDTH, (h + 1) * HEAD_WIDTH) for h in range(first, first + heads)
            ]
            q = jnp.concatenate([q_ref[:, span] for span in spans], axis=0)
            scores = jnp.where(visible, contract_last(q, key_rows), -1e30)
            top = jnp.max(scores, axis=1, keepdims=True)
            exponent = jnp.exp((scores - top) * scale)
            weights = (exponent * (1.0 / jnp.sum(exponent, axis=1, keepdims=True))).astype(BF16)
            attended = jnp.dot(weights, value_rows, preferred_element_type=F32).astype(BF16)
            for i, span in enumerate(spans):
                out_ref[:, span] = attended[i * length : (i + 1) * length]

    for j in range(count):
        pltpu.make_async_copy(zero, leave.at[0], osems.at[j]).wait()
    for k in range(slots):

        @pl.when(k >= named[0])
        def _():
            pltpu.make_async_copy(zero, leave.at[0], osems.at[count + k]).wait()

        @pl.when(k >= named[1])
        def _():
            pltpu.make_async_copy(zero, leave.at[0], osems.at[count + slots + k]).wait()


def attend(table, ctx, owner, unit, queries, kv_new, pool):
    count, length, width = pool.shape
    slots = max(2, (count + 1) // 2)
    pairs = QUERY_HEADS * length * count * length
    return pl.pallas_call(
        attend_kernel,
        out_shape=(
            jax.ShapeDtypeStruct(queries.shape, BF16),
            jax.ShapeDtypeStruct((2 * slots, length, width), BF16),
            jax.ShapeDtypeStruct((slots, length, width), BF16),
        ),
        in_specs=[SMEM, SMEM, SMEM, SMEM, VMEM, VMEM, ANY],
        out_specs=(VMEM, ANY, ANY),
        scratch_shapes=[
            pltpu.VMEM((count, length, width), BF16),
            pltpu.VMEM((length, width), BF16),
            pltpu.SemaphoreType.DMA((count,)),
            pltpu.SemaphoreType.DMA((count + 2 * slots,)),
        ],
        compiler_params=PARAMS,
        cost_estimate=cost(4 * pairs * HEAD_WIDTH * 4, 6 << 20, pairs),
        name="attend",
    )(table, ctx, owner, unit, queries, kv_new, pool)


def state_kernel(
    unit,
    skip,
    attn_ref,
    x_ref,
    z_ref,
    bc_ref,
    dt_ref,
    bias_ref,
    rate_ref,
    gain_ref,
    state_ref,
    stay_ref,
    leave_a,
    leave_b,
    held,
    send_ref,
    gated,
    fresh,
    sems,
):
    length = x_ref.shape[0]
    heads, share = MIXER_HEADS, MIXER_HEADS // 2
    u = unit[0]
    rows = lax.broadcasted_iota(jnp.int32, (length, length), 0)
    cols = lax.broadcasted_iota(jnp.int32, (length, length), 1)
    causal = rows >= cols
    raw = dt_ref[...] + bias_ref[...]
    step = jnp.maximum(raw, 0.0) + jnp.log1p(jnp.exp(-jnp.abs(raw)))
    cum = jnp.dot(
        causal.astype(F32),
        -step * rate_ref[...],
        precision=lax.Precision.HIGHEST,
        preferred_element_type=F32,
    )
    blank = jnp.zeros((length, length - heads), F32)
    cum_rows = jnp.transpose(jnp.concatenate([cum, blank], axis=1))
    step_rows = jnp.transpose(jnp.concatenate([step, blank], axis=1))
    last = cum[length - 1 : length, :]
    b_rows, c_rows = bc_ref[:, :NS], bc_ref[:, NS:]
    dots = contract_last(c_rows, b_rows)
    square = jnp.zeros((length, PM), F32)
    for h in range(heads):
        span = slice(h * PM, (h + 1) * PM)
        cum_t, cum_s = cum[:, h : h + 1], cum_rows[h : h + 1, :]
        step_s, end = step_rows[h : h + 1, :], last[:, h : h + 1]
        decay = jnp.exp(jnp.where(causal, cum_t - cum_s, -1e30))
        mixing = (dots * decay * step_s).astype(BF16)
        x = x_ref[:, span]
        x_float = x.astype(F32)
        prior = state_ref[0, h]
        high, low = two_terms(prior)
        carried = contract_last(c_rows, high) + contract_last(c_rows, low)
        y = jnp.dot(mixing, x, preferred_element_type=F32)
        y = y + carried * jnp.exp(cum_t) + skip[h] * x_float
        z = z_ref[:, span].astype(F32)
        g = y * (z / (1.0 + jnp.exp(-z)))
        gated[:, span] = g
        square = square + g * g
        weighted = jnp.transpose(x_float) * (jnp.exp(end - cum_s) * step_s)
        high, low = two_terms(weighted)
        new = jnp.exp(end) * prior + (
            jnp.dot(high, b_rows, preferred_element_type=F32)
            + jnp.dot(low, b_rows, preferred_element_type=F32)
        )
        place = h % share

        @pl.when(u == h // share)
        def _():
            fresh[place] = new
            pltpu.make_async_copy(fresh.at[place], held.at[u, place], sems.at[place]).start()

        @pl.when(u != h // share)
        def _():
            send_ref[place] = new.astype(BF16)

    mean = jnp.sum(square, axis=1, keepdims=True) * (1.0 / (heads * PM))
    out = (gated[...] * lax.rsqrt(mean + norm_eps) * gain_ref[...]).astype(BF16)
    attn_width = attn_ref.shape[1]
    cut = stay_ref.shape[1] - attn_width
    part = leave_a.shape[1]

    @pl.when(u == 0)
    def _():
        stay_ref[:, :attn_width] = attn_ref[...]
        stay_ref[:, attn_width:] = out[:, :cut]
        leave_a[...] = out[:, cut : cut + part]
        leave_b[...] = out[:, cut + part :]

    @pl.when(u == 1)
    def _():
        stay_ref[...] = out[:, cut:]
        leave_a[...] = attn_ref[:, :part]
        leave_b[:, : attn_width - part] = attn_ref[:, part:]
        leave_b[:, attn_width - part :] = out[:, :cut]

    for place in range(share):
        pltpu.make_async_copy(fresh.at[place], held.at[0, place], sems.at[place]).wait()


def state_space(unit, skip, attn, x, z, bc, dt, bias, rate, gain, state):
    length, width = x.shape
    share = MIXER_HEADS // 2
    half = (attn.shape[1] + width) // 2
    return pl.pallas_call(
        state_kernel,
        out_shape=(
            jax.ShapeDtypeStruct((length, half), BF16),
            jax.ShapeDtypeStruct((length, half // 2), BF16),
            jax.ShapeDtypeStruct((length, half - half // 2), BF16),
            jax.ShapeDtypeStruct((2, share, PM, NS), F32),
            jax.ShapeDtypeStruct((share, PM, NS), BF16),
        ),
        in_specs=[SMEM, SMEM] + [VMEM] * 9,
        out_specs=(VMEM, VMEM, VMEM, ANY, VMEM),
        scratch_shapes=[
            pltpu.VMEM((length, width), F32),
            pltpu.VMEM((share, PM, NS), F32),
            pltpu.SemaphoreType.DMA((share,)),
        ],
        compiler_params=PARAMS,
        cost_estimate=cost(4 << 30, 10 << 20, MIXER_HEADS * length * length * 2),
        name="state_space",
    )(unit, skip, attn, x, z, bc, dt, bias, rate, gain, state)


def settle_kernel(
    unit, pages, state, pages_in, state_in, rows_in, pages_out, state_out, rows_out, wide, sem
):
    slots = pages.shape[0]
    u = unit[0]
    copy = pltpu.make_async_copy(pages, pages_out.at[pl.ds((1 - u) * slots, slots)], sem.at[0])
    copy.start()
    wide[...] = state[...].astype(F32)
    other = pltpu.make_async_copy(wide, state_out.at[1 - u], sem.at[1])
    other.start()
    copy.wait()
    other.wait()


def settle(unit, pages, state, pages_held, state_held, rows):
    return pl.pallas_call(
        settle_kernel,
        out_shape=tuple(
            jax.ShapeDtypeStruct(x.shape, x.dtype) for x in (pages_held, state_held, rows)
        ),
        in_specs=[SMEM, ANY, VMEM, ANY, ANY, ANY],
        out_specs=(ANY, ANY, ANY),
        scratch_shapes=[pltpu.VMEM(state.shape, F32), pltpu.SemaphoreType.DMA((2,))],
        input_output_aliases={3: 0, 4: 1, 5: 2},
        compiler_params=PARAMS,
        cost_estimate=cost(0, 5 << 20),
        name="settle",
    )(unit, pages, state, pages_held, state_held, rows)


def cut_kernel(unit, weight_ref, kept, sent):
    half = weight_ref.shape[1] // 2
    for u, low_ref, high_ref in ((0, kept, sent), (1, sent, kept)):

        @pl.when(unit[0] == u)
        def _():
            low_ref[...] = weight_ref[:, :half]
            high_ref[...] = weight_ref[:, half:]


def cut(unit, weight):
    rows, width = weight.shape
    shape = jax.ShapeDtypeStruct((rows, width // 2), weight.dtype)
    return pl.pallas_call(
        cut_kernel,
        out_shape=(shape, shape),
        in_specs=[SMEM, VMEM],
        out_specs=(VMEM, VMEM),
        compiler_params=PARAMS,
        cost_estimate=cost(0, 3 << 20),
        name="cut",
    )(unit, weight)


def block_of(req, d, k, layers):
    layer, place = req // PLANE, req % PLANE
    source = ring_at((ring_place(layer, layers) + layers - k) % layers, layers)
    return source * PLANE + (place ^ d)


def spread_kernel(req, hidden, *refs):
    outs, sem = refs[:-1], refs[-1]
    rows, depth = outs[0].shape
    layers = sem.shape[0] // PLANE
    chip_rows = depth // layers
    copies = []
    for d in range(PLANE):
        for k in range(layers):
            column = pl.multiple_of(chip_rows * block_of(req[0], d, k, layers), 128)
            copies.append(
                pltpu.make_async_copy(
                    hidden.at[:, pl.ds(column, chip_rows)],
                    outs[d].at[:, k * chip_rows : (k + 1) * chip_rows],
                    sem.at[d * layers + k],
                )
            )
    for copy in copies:
        copy.start()
    for copy in copies:
        copy.wait()


def spread(req, hidden, chip_rows, layers):
    rows = hidden.shape[0]
    if chip_rows % 128:
        return [
            jnp.concatenate(
                [
                    lax.dynamic_slice(
                        hidden, (0, block_of(req[0], d, k, layers) * chip_rows), (rows, chip_rows)
                    )
                    for k in range(layers)
                ],
                axis=1,
            )
            for d in range(PLANE)
        ]
    return pl.pallas_call(
        spread_kernel,
        out_shape=(jax.ShapeDtypeStruct((rows, layers * chip_rows), hidden.dtype),) * PLANE,
        in_specs=[SMEM, ANY],
        out_specs=(VMEM,) * PLANE,
        scratch_shapes=[pltpu.SemaphoreType.DMA((PLANE * layers,))],
        compiler_params=PARAMS,
        cost_estimate=cost(0, 4 << 20),
        name="spread",
    )(req, hidden)


def place_rows(weight, pieces, unit, low=0):
    block_rows, width = pieces[0].shape[0] // 2, weight.shape[1]
    for k, piece in enumerate(pieces):
        for which, place in ((0, unit), (1, 1 - unit)):
            at = pl.multiple_of((2 * k + place) * block_rows, 16)
            rows = slice(which * block_rows, (which + 1) * block_rows)
            weight[pl.ds(at, block_rows), :] = piece[rows, low : low + width]


def order_kernel(*refs):
    hidden, (front_ref, last_ref) = refs[:-2], refs[-2:]
    rows, done = hidden[0].shape[0], front_ref.shape[1]
    for d in range(PLANE):
        place = d % (PLANE // 2) * rows
        pair = hidden[PLANE + d // (PLANE // 2)]
        for n, block in ((0, hidden[d][...]), (1, pair[place : place + rows, :])):
            span = slice((2 * d + n) * rows, (2 * d + n + 1) * rows)
            front_ref[span, :] = block[:, :done]
            last_ref[span, :] = block[:, done:]


def order_rows(hidden, done):
    rows, depth = hidden[0].shape
    every = 2 * PLANE * rows
    return pl.pallas_call(
        order_kernel,
        out_shape=(
            jax.ShapeDtypeStruct((every, done), BF16),
            jax.ShapeDtypeStruct((every, depth - done), BF16),
        ),
        in_specs=[VMEM] * len(hidden),
        out_specs=(VMEM, VMEM),
        compiler_params=PARAMS,
        cost_estimate=cost(0, 6 << 20),
        name="order_rows",
    )(*hidden)


def begin_kernel(low, unit, front, *refs):
    pieces, (out, weight) = refs[:-2], refs[-2:]
    place_rows(weight, pieces, unit[0], low)
    rows = out.shape[0] // PLANE
    for d in range(PLANE):
        span = slice(d * rows, (d + 1) * rows)
        out[span, :] = jnp.dot(front[span, :], weight[...], preferred_element_type=F32)


def begin(unit, front, pieces, low, width):
    every, done = front.shape
    return pl.pallas_call(
        functools.partial(begin_kernel, low),
        out_shape=jax.ShapeDtypeStruct((every, width), F32),
        in_specs=[SMEM] + [VMEM] * (1 + len(pieces)),
        out_specs=VMEM,
        scratch_shapes=[pltpu.VMEM((done, width), BF16)],
        compiler_params=PARAMS,
        cost_estimate=cost(0, 8 << 20),
        name="begin",
    )(unit, front, *pieces)


def product_kernel(unit, hidden, partial, piece, own_ref, *refs):
    parts, weight = refs[:-1], refs[-1]
    place_rows(weight, [piece], unit[0])
    rows = own_ref.shape[0]
    for d in range(PLANE):
        span = slice(d * rows, (d + 1) * rows)
        result = partial[span, :] + jnp.dot(
            hidden[span, :], weight[...], preferred_element_type=F32
        )
        if d:
            parts[d - 1][...] = result.astype(BF16)
        else:
            own_ref[...] = result


def product(unit, hidden, partial, piece):
    rows, width = partial.shape[0] // PLANE, partial.shape[1]
    outs = pl.pallas_call(
        product_kernel,
        out_shape=(jax.ShapeDtypeStruct((rows, width), F32),)
        + (jax.ShapeDtypeStruct((rows, width), BF16),) * (PLANE - 1),
        in_specs=[SMEM] + [VMEM] * 3,
        out_specs=(VMEM,) * PLANE,
        scratch_shapes=[pltpu.VMEM(piece.shape, BF16)],
        compiler_params=PARAMS,
        cost_estimate=cost(0, 6 << 20),
        name="product",
    )(unit, hidden, partial, piece)
    return outs[0], outs[1:]


def total_kernel(own_ref, *refs):
    came, (keep_ref, send_ref) = refs[:-2], refs[-2:]
    total = own_ref[...]
    for ref in came:
        total = total + ref[...].astype(F32)
    rows = keep_ref.shape[0]
    keep_ref[...] = total[:rows]
    send_ref[...] = total[rows:].astype(BF16)


def total(own, came):
    rows, width = own.shape
    return pl.pallas_call(
        total_kernel,
        out_shape=(
            jax.ShapeDtypeStruct((rows // 2, width), F32),
            jax.ShapeDtypeStruct((rows // 2, width), BF16),
        ),
        in_specs=[VMEM] * (1 + len(came)),
        out_specs=(VMEM, VMEM),
        compiler_params=PARAMS,
        cost_estimate=cost(0, 4 << 20),
        name="total",
    )(own, *came)


def finish_kernel(unit, resid_ref, mixed_ref, low_ref, high_ref, *refs):
    count = len(refs) // 2
    kept, came, out_ref = refs[:count], refs[count:-1], refs[-1]
    half = out_ref.shape[1] // 2
    for u in range(2):

        @pl.when(unit[0] == u)
        def _():
            for group, which in ((kept, u), (came, 1 - u)):
                base = 0
                other_ref = high_ref if which else low_ref
                for ref in group:
                    span = slice(which * half + base, which * half + base + ref.shape[1])
                    mixed = mixed_ref[:, span].astype(F32)
                    mixed = mixed + other_ref[:, base : base + ref.shape[1]].astype(F32)
                    sums = resid_ref[:, span].astype(F32) + mixed + ref[...].astype(F32)
                    out_ref[:, span] = sums.astype(BF16)
                    base += ref.shape[1]


def finish(unit, resid, mixed, mixed_came, kept, came):
    return pl.pallas_call(
        finish_kernel,
        out_shape=jax.ShapeDtypeStruct(resid.shape, BF16),
        in_specs=[SMEM] + [VMEM] * (4 + len(kept) + len(came)),
        out_specs=VMEM,
        compiler_params=PARAMS,
        cost_estimate=cost(0, 4 << 20),
        name="finish",
    )(unit, resid, mixed, *mixed_came, *kept, *came)


def project_kernel(stay_ref, a_ref, b_ref, weight_ref, keep_ref, low_ref, high_ref, both):
    rows = stay_ref.shape[0]
    half = pl.num_programs(0) // 2
    cut_at = a_ref.shape[1]

    @pl.when(pl.program_id(0) == 0)
    def _():
        both[:rows, :] = stay_ref[...]
        both[rows:, :cut_at] = a_ref[...]
        both[rows:, cut_at:] = b_ref[...]

    result = jnp.dot(both[...], weight_ref[...], preferred_element_type=F32).astype(BF16)
    keep_ref[...] = result[:rows]

    @pl.when(pl.program_id(0) < half)
    def _():
        low_ref[...] = result[rows:]

    @pl.when(pl.program_id(0) >= half)
    def _():
        high_ref[...] = result[rows:]


def project(stay, came_a, came_b, weight):
    rows, depth = stay.shape
    width = weight.shape[1]
    tile = 512 if width % 1024 == 0 else width // 2
    half = width // tile // 2
    fixed = [pl.BlockSpec(x.shape, lambda i: (0, 0)) for x in (stay, came_a, came_b)]
    return pl.pallas_call(
        project_kernel,
        grid=(2 * half,),
        out_shape=(
            jax.ShapeDtypeStruct((rows, width), BF16),
            jax.ShapeDtypeStruct((rows, width // 2), BF16),
            jax.ShapeDtypeStruct((rows, width // 2), BF16),
        ),
        in_specs=fixed + [pl.BlockSpec((depth, tile), lambda i: (0, i))],
        out_specs=(
            pl.BlockSpec((rows, tile), lambda i: (0, i)),
            pl.BlockSpec((rows, tile), lambda i: (0, jnp.minimum(i, half - 1))),
            pl.BlockSpec((rows, tile), lambda i: (0, jnp.maximum(i - half, 0))),
        ),
        scratch_shapes=[pltpu.VMEM((2 * rows, depth), BF16)],
        compiler_params=PARAMS,
        cost_estimate=cost(0, 15 << 20),
        name="project",
    )(stay, came_a, came_b, weight)


def split_kernel(x_ref, *outs):
    base = 0
    for out in outs:
        out[...] = x_ref[:, base : base + out.shape[1]]
        base += out.shape[1]


def split_columns(x, widths):
    return pl.pallas_call(
        split_kernel,
        out_shape=tuple(jax.ShapeDtypeStruct((x.shape[0], w), x.dtype) for w in widths),
        in_specs=[VMEM],
        out_specs=(VMEM,) * len(widths),
        compiler_params=PARAMS,
        cost_estimate=cost(0, 2 << 20),
        name="split_columns",
    )(x)


def stack_kernel(*refs):
    *parts, out = refs
    rows = parts[0].shape[0]
    for i, part in enumerate(parts):
        out[i * rows : (i + 1) * rows, :] = part[...]


def stack_rows(parts):
    rows, width = parts[0].shape
    return pl.pallas_call(
        stack_kernel,
        out_shape=jax.ShapeDtypeStruct((len(parts) * rows, width), parts[0].dtype),
        in_specs=[VMEM] * len(parts),
        out_specs=VMEM,
        compiler_params=PARAMS,
        cost_estimate=cost(0, 2 << 20),
        name="stack_rows",
    )(*parts)


def swap_units(x):
    return lax.ppermute(x, "unit", [(0, 1), (1, 0)])


def after(x, *others):
    return lax.optimization_barrier((x, *others))[0]


def ring_at(step, length):
    if isinstance(step, int):
        return 2 * step - min(step, 1) if 2 * step <= length else 2 * (length - step)
    return jnp.where(2 * step <= length, 2 * step - jnp.minimum(step, 1), 2 * (length - step))


def ring_place(place, length):
    return jnp.where(place % 2 == 1, (place + 1) // 2, (length - place // 2) % length)


def chunk_widths(width):
    first, last = width // 4 // 128 * 128, width // 3 // 128 * 128
    return [first, width - first - last, last]


def on_device(
    queries,
    kv_new,
    kv_pool,
    page_table,
    ctx_pages,
    ssm_x,
    ssm_z,
    ssm_bc,
    dt_raw,
    dt_bias,
    decay_rate,
    skip_gain,
    ssm_state,
    ssm_norm_gain,
    resid,
    out_weight,
    ffn_hidden,
    down_weight,
    page_owner,
):
    tok_rows = queries.shape[0]
    n_req = lax.axis_size("req")
    block_rows, width = down_weight.shape
    u = lax.axis_index("unit")
    unit = u.reshape(1)
    req = lax.axis_index("req")
    layers = n_req // PLANE

    ring = [ring_at(i, layers) for i in range(layers)]
    ring_pairs = [
        (ring[i] * PLANE + p, ring[(i + 1) % layers] * PLANE + p)
        for i in range(layers)
        for p in range(PLANE)
    ]

    def pass_on(x):
        return lax.ppermute(x, "req", ring_pairs)

    kept, sent = cut(unit, down_weight)
    hops = [stack_rows([kept, swap_units(sent)])]
    if layers > 2:
        hops.append(pass_on(hops[0]))

    def plane_swap(x, d):
        return lax.ppermute(
            x, "req", [(r, r - r % PLANE + ((r % PLANE) ^ d)) for r in range(n_req)]
        )

    mine = spread(req.reshape(1), after(ffn_hidden, hops[0]), 2 * block_rows, layers)
    hidden = [plane_swap(x, d) if d else x for d, x in enumerate(mine)]
    attn, pages_held, pages_leave = attend(
        page_table, ctx_pages, page_owner[:, :, 0], unit, after(queries, mine[0]), kv_new, kv_pool
    )
    while len(hops) < layers - 1:
        hops.append(pass_on(after(hops[-1], attn)))
    stay, leave_a, leave_b, state_held, state_leave = state_space(
        unit,
        skip_gain,
        after(attn, *hops[1:2]),
        ssm_x,
        ssm_z,
        ssm_bc,
        dt_raw,
        dt_bias[None, :],
        decay_rate[None, :],
        ssm_norm_gain[None, :],
        ssm_state,
    )
    hidden = after(hidden, stay)
    leave_came = [swap_units(x) for x in after((leave_a, leave_b), *hidden)]
    pair = PLANE // 2
    gathered = [after(stack_rows(x), *leave_came) for x in (hidden[:pair], hidden[pair:])]
    swapped = [swap_units(x) for x in gathered]
    hidden = list(hidden) + swapped
    mixed, *mixed_leave = project(stay, *leave_came, out_weight)
    state_leave, pages_leave = after((state_leave, pages_leave), stay)
    state_came, pages_came = swap_units(state_leave), swap_units(pages_leave)
    mixed_came = [
        swap_units(x) for x in after(mixed_leave, hops[-1], state_came, pages_came, *swapped)
    ]
    widths = chunk_widths(width // 2)
    ends = [pass_on(x) for x in split_columns(after(hops[-1], mixed), widths)]
    done = len(hops) * hops[0].shape[0]
    front, last_hidden = order_rows(hidden, done)
    sums, order, received, low = [], mixed_came, [], 0
    for n, end in enumerate(ends):
        piece = begin(unit, after(front, *order) if n else front, hops, low, widths[n])
        own, parts = product(unit, last_hidden, piece, after(end, piece, *order))
        order, low = list(parts) + [x[0] for x in sums], low + widths[n]
        if n == len(ends) - 1:
            decode_kv, decode_state, mixed = settle(
                unit, pages_came, state_came, pages_held, state_held, after(mixed, *parts)
            )
        if received:
            parts = after(parts, *(received if n < len(ends) - 1 else received[:1]))
        received = [plane_swap(x, d) for d, x in enumerate(parts, 1)]
        token = sums[-1][0] if sums else own
        sums.append(total(own, after(received, token, *([mixed] if n == len(ends) - 1 else []))))
    kept, leave = zip(*sums)
    came = [swap_units(x) for x in leave]
    layer_out = finish(unit, resid, mixed, mixed_came, kept, came)
    return (layer_out, decode_kv, decode_state)


def solution(mesh):
    return jax.shard_map(
        on_device,
        mesh=mesh,
        in_specs=(
            P(("req", "unit"), None),
            P(("req", "unit"), None),
            P(("req", "unit"), None, None),
            P(("req", "unit"), None),
            P(("req", "unit")),
            P(("req", "unit"), None),
            P(("req", "unit"), None),
            P(("req", "unit"), None),
            P(("req", "unit"), None),
            P(),
            P(),
            P(),
            P(("req", "unit"), None, None, None),
            P(),
            P(("req", "unit"), None),
            P("unit", None),
            P(("req", "unit"), None),
            P(("req", "unit"), None),
            P(("req", "unit"), None, None),
        ),
        out_specs=(
            P(("req", "unit"), None),
            P(("req", "unit"), None, None),
            P("req", "unit", None, None),
        ),
        check_vma=False,
    )
```

```python
import functools
import math

import jax
import jax.numpy as jnp
from jax import lax
from jax.experimental import pallas as pl
from jax.experimental.pallas import tpu as pltpu
from jax.sharding import PartitionSpec as P

QUERY_HEADS = 12
KEY_VALUE_HEADS = 2
HEAD_WIDTH = 128
MIXER_HEADS = 24
PM = 128
NS = 256

PLANE = 4

norm_eps = 1e-05

F32, BF16 = jnp.float32, jnp.bfloat16
VMEM = pl.BlockSpec(memory_space=pltpu.VMEM)
SMEM = pl.BlockSpec(memory_space=pltpu.SMEM)
ANY = pl.BlockSpec(memory_space=pl.ANY)
PARAMS = pltpu.CompilerParams(vmem_limit_bytes=24 * 1024 * 1024)
LARGE = pltpu.CompilerParams(vmem_limit_bytes=48 * 1024 * 1024)


def cost(flops, moved, exps=0):
    return pl.CostEstimate(flops=0, bytes_accessed=0, transcendentals=0)


def contract_last(a, b):
    return lax.dot_general(a, b, (((1,), (1,)), ((), ())), preferred_element_type=F32)


def two_terms(x):
    high = x.astype(BF16)
    return high, (x - high.astype(F32)).astype(BF16)


def attend_kernel(
    table, ctx, owner, unit, q_ref, new_ref, pool, out_ref, held, leave, pages, zero, sems, osems
):
    count, length, _ = pages.shape
    slots = leave.shape[0]
    live = ctx[0]
    u = unit[0]
    for j in range(count):

        @pl.when(j == live)
        def _():
            pltpu.make_async_copy(new_ref, pages.at[j], sems.at[j]).start()

        @pl.when(j != live)
        def _():
            pltpu.make_async_copy(pool.at[table[0, j]], pages.at[j], sems.at[j]).start()

    zero[...] = jnp.zeros_like(zero)
    for j in range(count):
        pltpu.make_async_copy(new_ref, pages.at[j], sems.at[j]).wait()

    named = [jnp.int32(0), jnp.int32(0)]
    for j in range(count):
        own = owner[0, j] == u
        rank = jnp.where(own, named[0], named[1])
        named = [named[0] + own.astype(jnp.int32), named[1] + 1 - own.astype(jnp.int32)]
        for source, when in ((pages.at[j], j <= live), (zero, j > live)):

            @pl.when(when & own)
            def _():
                pltpu.make_async_copy(source, held.at[u * slots + rank], osems.at[j]).start()

            @pl.when(when & jnp.logical_not(own))
            def _():
                pltpu.make_async_copy(source, leave.at[rank], osems.at[j]).start()

    for k in range(slots):

        @pl.when(k >= named[0])
        def _():
            pltpu.make_async_copy(zero, held.at[u * slots + k], osems.at[count + k]).start()

        @pl.when(k >= named[1])
        def _():
            pltpu.make_async_copy(zero, leave.at[k], osems.at[count + slots + k]).start()

    group = QUERY_HEADS // KEY_VALUE_HEADS
    heads = 3
    rows, keys = heads * length, count * length
    limit = live * length + lax.broadcasted_iota(jnp.int32, (rows, 1), 0) % length
    visible = lax.broadcasted_iota(jnp.int32, (rows, keys), 1) <= limit
    scale = 1.0 / math.sqrt(HEAD_WIDTH)
    for k in range(KEY_VALUE_HEADS):
        key_rows = pages[:, :, k * HEAD_WIDTH : (k + 1) * HEAD_WIDTH].reshape(keys, HEAD_WIDTH)
        lo = (KEY_VALUE_HEADS + k) * HEAD_WIDTH
        value_rows = pages[:, :, lo : lo + HEAD_WIDTH].reshape(keys, HEAD_WIDTH)
        for first in range(k * group, (k + 1) * group, heads):
            spans = [
                slice(h * HEAD_WIDTH, (h + 1) * HEAD_WIDTH) for h in range(first, first + heads)
            ]
            q = jnp.concatenate([q_ref[:, span] for span in spans], axis=0)
            scores = jnp.where(visible, contract_last(q, key_rows), -1e30)
            top = jnp.max(scores, axis=1, keepdims=True)
            exponent = jnp.exp((scores - top) * scale)
            weights = (exponent * (1.0 / jnp.sum(exponent, axis=1, keepdims=True))).astype(BF16)
            attended = jnp.dot(weights, value_rows, preferred_element_type=F32).astype(BF16)
            for i, span in enumerate(spans):
                out_ref[:, span] = attended[i * length : (i + 1) * length]

    for j in range(count):
        pltpu.make_async_copy(zero, leave.at[0], osems.at[j]).wait()
    for k in range(slots):

        @pl.when(k >= named[0])
        def _():
            pltpu.make_async_copy(zero, leave.at[0], osems.at[count + k]).wait()

        @pl.when(k >= named[1])
        def _():
            pltpu.make_async_copy(zero, leave.at[0], osems.at[count + slots + k]).wait()


def attend(table, ctx, owner, unit, queries, kv_new, pool):
    count, length, width = pool.shape
    slots = max(2, (count + 1) // 2)
    pairs = QUERY_HEADS * length * count * length
    return pl.pallas_call(
        attend_kernel,
        out_shape=(
            jax.ShapeDtypeStruct(queries.shape, BF16),
            jax.ShapeDtypeStruct((2 * slots, length, width), BF16),
            jax.ShapeDtypeStruct((slots, length, width), BF16),
        ),
        in_specs=[SMEM, SMEM, SMEM, SMEM, VMEM, VMEM, ANY],
        out_specs=(VMEM, ANY, ANY),
        scratch_shapes=[
            pltpu.VMEM((count, length, width), BF16),
            pltpu.VMEM((length, width), BF16),
            pltpu.SemaphoreType.DMA((count,)),
            pltpu.SemaphoreType.DMA((count + 2 * slots,)),
        ],
        compiler_params=LARGE,
        cost_estimate=cost(4 * pairs * HEAD_WIDTH * 4, 6 << 20, pairs),
        name="attend",
    )(table, ctx, owner, unit, queries, kv_new, pool)


def state_kernel(
    unit,
    skip,
    attn_ref,
    x_ref,
    z_ref,
    bc_ref,
    dt_ref,
    bias_ref,
    rate_ref,
    gain_ref,
    state_ref,
    stay_ref,
    leave_a,
    leave_b,
    held,
    send_ref,
    gated,
    fresh,
    sems,
):
    length = x_ref.shape[0]
    heads, share = MIXER_HEADS, MIXER_HEADS // 2
    u = unit[0]
    rows = lax.broadcasted_iota(jnp.int32, (length, length), 0)
    cols = lax.broadcasted_iota(jnp.int32, (length, length), 1)
    causal = rows >= cols
    raw = dt_ref[...] + bias_ref[...]
    step = jnp.maximum(raw, 0.0) + jnp.log1p(jnp.exp(-jnp.abs(raw)))
    cum = jnp.dot(
        causal.astype(F32),
        -step * rate_ref[...],
        precision=lax.Precision.HIGHEST,
        preferred_element_type=F32,
    )
    blank = jnp.zeros((length, length - heads), F32)
    cum_rows = jnp.transpose(jnp.concatenate([cum, blank], axis=1))
    step_rows = jnp.transpose(jnp.concatenate([step, blank], axis=1))
    last = cum[length - 1 : length, :]
    b_rows, c_rows = bc_ref[:, :NS], bc_ref[:, NS:]
    dots = contract_last(c_rows, b_rows)
    square = jnp.zeros((length, PM), F32)
    for h in range(heads):
        span = slice(h * PM, (h + 1) * PM)
        cum_t, cum_s = cum[:, h : h + 1], cum_rows[h : h + 1, :]
        step_s, end = step_rows[h : h + 1, :], last[:, h : h + 1]
        decay = jnp.exp(jnp.where(causal, cum_t - cum_s, -1e30))
        mixing = (dots * decay * step_s).astype(BF16)
        x = x_ref[:, span]
        x_float = x.astype(F32)
        prior = state_ref[0, h]
        high, low = two_terms(prior)
        carried = contract_last(c_rows, high) + contract_last(c_rows, low)
        y = jnp.dot(mixing, x, preferred_element_type=F32)
        y = y + carried * jnp.exp(cum_t) + skip[h] * x_float
        z = z_ref[:, span].astype(F32)
        g = y * (z / (1.0 + jnp.exp(-z)))
        gated[:, span] = g
        square = square + g * g
        weighted = jnp.transpose(x_float) * (jnp.exp(end - cum_s) * step_s)
        high, low = two_terms(weighted)
        new = jnp.exp(end) * prior + (
            jnp.dot(high, b_rows, preferred_element_type=F32)
            + jnp.dot(low, b_rows, preferred_element_type=F32)
        )
        place = h % share

        @pl.when(u == h // share)
        def _():
            fresh[place] = new
            pltpu.make_async_copy(fresh.at[place], held.at[u, place], sems.at[place]).start()

        @pl.when(u != h // share)
        def _():
            send_ref[place] = new.astype(BF16)

    mean = jnp.sum(square, axis=1, keepdims=True) * (1.0 / (heads * PM))
    out = (gated[...] * lax.rsqrt(mean + norm_eps) * gain_ref[...]).astype(BF16)
    attn_width = attn_ref.shape[1]
    cut = stay_ref.shape[1] - attn_width
    part = leave_a.shape[1]

    @pl.when(u == 0)
    def _():
        stay_ref[:, :attn_width] = attn_ref[...]
        stay_ref[:, attn_width:] = out[:, :cut]
        leave_a[...] = out[:, cut : cut + part]
        leave_b[...] = out[:, cut + part :]

    @pl.when(u == 1)
    def _():
        stay_ref[...] = out[:, cut:]
        leave_a[...] = attn_ref[:, :part]
        leave_b[:, : attn_width - part] = attn_ref[:, part:]
        leave_b[:, attn_width - part :] = out[:, :cut]

    for place in range(share):
        pltpu.make_async_copy(fresh.at[place], held.at[0, place], sems.at[place]).wait()


def state_space(unit, skip, attn, x, z, bc, dt, bias, rate, gain, state):
    length, width = x.shape
    share = MIXER_HEADS // 2
    half = (attn.shape[1] + width) // 2
    return pl.pallas_call(
        state_kernel,
        out_shape=(
            jax.ShapeDtypeStruct((length, half), BF16),
            jax.ShapeDtypeStruct((length, half // 2), BF16),
            jax.ShapeDtypeStruct((length, half - half // 2), BF16),
            jax.ShapeDtypeStruct((2, share, PM, NS), F32),
            jax.ShapeDtypeStruct((share, PM, NS), BF16),
        ),
        in_specs=[SMEM, SMEM] + [VMEM] * 9,
        out_specs=(VMEM, VMEM, VMEM, ANY, VMEM),
        scratch_shapes=[
            pltpu.VMEM((length, width), F32),
            pltpu.VMEM((share, PM, NS), F32),
            pltpu.SemaphoreType.DMA((share,)),
        ],
        compiler_params=LARGE,
        cost_estimate=cost(4 << 30, 10 << 20, MIXER_HEADS * length * length * 2),
        name="state_space",
    )(unit, skip, attn, x, z, bc, dt, bias, rate, gain, state)


def settle_kernel(
    unit, pages, state, pages_in, state_in, rows_in, pages_out, state_out, rows_out, wide, sem
):
    slots = pages.shape[0]
    u = unit[0]
    copy = pltpu.make_async_copy(pages, pages_out.at[pl.ds((1 - u) * slots, slots)], sem.at[0])
    copy.start()
    wide[...] = state[...].astype(F32)
    other = pltpu.make_async_copy(wide, state_out.at[1 - u], sem.at[1])
    other.start()
    copy.wait()
    other.wait()


def settle(unit, pages, state, pages_held, state_held, rows):
    return pl.pallas_call(
        settle_kernel,
        out_shape=tuple(
            jax.ShapeDtypeStruct(x.shape, x.dtype) for x in (pages_held, state_held, rows)
        ),
        in_specs=[SMEM, ANY, VMEM, ANY, ANY, ANY],
        out_specs=(ANY, ANY, ANY),
        scratch_shapes=[pltpu.VMEM(state.shape, F32), pltpu.SemaphoreType.DMA((2,))],
        input_output_aliases={3: 0, 4: 1, 5: 2},
        compiler_params=PARAMS,
        cost_estimate=cost(0, 5 << 20),
        name="settle",
    )(unit, pages, state, pages_held, state_held, rows)


def cut_kernel(unit, weight_ref, kept, sent):
    half = weight_ref.shape[1] // 2
    for u, low_ref, high_ref in ((0, kept, sent), (1, sent, kept)):

        @pl.when(unit[0] == u)
        def _():
            low_ref[...] = weight_ref[:, :half]
            high_ref[...] = weight_ref[:, half:]


def cut(unit, weight):
    rows, width = weight.shape
    shape = jax.ShapeDtypeStruct((rows, width // 2), weight.dtype)
    return pl.pallas_call(
        cut_kernel,
        out_shape=(shape, shape),
        in_specs=[SMEM, VMEM],
        out_specs=(VMEM, VMEM),
        compiler_params=PARAMS,
        cost_estimate=cost(0, 3 << 20),
        name="cut",
    )(unit, weight)


def block_of(req, d, k, layers):
    layer, place = req // PLANE, req % PLANE
    source = ring_at((ring_place(layer, layers) + layers - k) % layers, layers)
    return source * PLANE + (place ^ d)


def spread_kernel(req, hidden, *refs):
    outs, sem = refs[:-1], refs[-1]
    rows, depth = outs[0].shape
    layers = sem.shape[0] // PLANE
    chip_rows = depth // layers
    copies = []
    for d in range(PLANE):
        for k in range(layers):
            column = pl.multiple_of(chip_rows * block_of(req[0], d, k, layers), 128)
            copies.append(
                pltpu.make_async_copy(
                    hidden.at[:, pl.ds(column, chip_rows)],
                    outs[d].at[:, k * chip_rows : (k + 1) * chip_rows],
                    sem.at[d * layers + k],
                )
            )
    for copy in copies:
        copy.start()
    for copy in copies:
        copy.wait()


def spread(req, hidden, chip_rows, layers):
    rows = hidden.shape[0]
    if chip_rows % 128:
        return [
            jnp.concatenate(
                [
                    lax.dynamic_slice(
                        hidden, (0, block_of(req[0], d, k, layers) * chip_rows), (rows, chip_rows)
                    )
                    for k in range(layers)
                ],
                axis=1,
            )
            for d in range(PLANE)
        ]
    return pl.pallas_call(
        spread_kernel,
        out_shape=(jax.ShapeDtypeStruct((rows, layers * chip_rows), hidden.dtype),) * PLANE,
        in_specs=[SMEM, ANY],
        out_specs=(VMEM,) * PLANE,
        scratch_shapes=[pltpu.SemaphoreType.DMA((PLANE * layers,))],
        compiler_params=PARAMS,
        cost_estimate=cost(0, 4 << 20),
        name="spread",
    )(req, hidden)


def place_rows(weight, pieces, unit, low=0):
    block_rows, width = pieces[0].shape[0] // 2, weight.shape[1]
    for k, piece in enumerate(pieces):
        for which, place in ((0, unit), (1, 1 - unit)):
            at = pl.multiple_of((2 * k + place) * block_rows, 16)
            rows = slice(which * block_rows, (which + 1) * block_rows)
            weight[pl.ds(at, block_rows), :] = piece[rows, low : low + width]


def order_kernel(*refs):
    hidden, (front_ref, last_ref) = refs[:-2], refs[-2:]
    rows, done = hidden[0].shape[0], front_ref.shape[1]
    for d in range(PLANE):
        place = d % (PLANE // 2) * rows
        pair = hidden[PLANE + d // (PLANE // 2)]
        for n, block in ((0, hidden[d][...]), (1, pair[place : place + rows, :])):
            span = slice((2 * d + n) * rows, (2 * d + n + 1) * rows)
            front_ref[span, :] = block[:, :done]
            last_ref[span, :] = block[:, done:]


def order_rows(hidden, done):
    rows, depth = hidden[0].shape
    every = 2 * PLANE * rows
    return pl.pallas_call(
        order_kernel,
        out_shape=(
            jax.ShapeDtypeStruct((every, done), BF16),
            jax.ShapeDtypeStruct((every, depth - done), BF16),
        ),
        in_specs=[VMEM] * len(hidden),
        out_specs=(VMEM, VMEM),
        compiler_params=PARAMS,
        cost_estimate=cost(0, 6 << 20),
        name="order_rows",
    )(*hidden)


def begin_kernel(low, unit, front, *refs):
    pieces, (out, weight) = refs[:-2], refs[-2:]
    place_rows(weight, pieces, unit[0], low)
    rows = out.shape[0] // PLANE
    for d in range(PLANE):
        span = slice(d * rows, (d + 1) * rows)
        out[span, :] = jnp.dot(front[span, :], weight[...], preferred_element_type=F32)


def begin(unit, front, pieces, low, width):
    every, done = front.shape
    return pl.pallas_call(
        functools.partial(begin_kernel, low),
        out_shape=jax.ShapeDtypeStruct((every, width), F32),
        in_specs=[SMEM] + [VMEM] * (1 + len(pieces)),
        out_specs=VMEM,
        scratch_shapes=[pltpu.VMEM((done, width), BF16)],
        compiler_params=PARAMS,
        cost_estimate=cost(0, 8 << 20),
        name="begin",
    )(unit, front, *pieces)


def product_kernel(unit, hidden, partial, piece, own_ref, *refs):
    parts, weight = refs[:-1], refs[-1]
    place_rows(weight, [piece], unit[0])
    rows = own_ref.shape[0]
    for d in range(PLANE):
        span = slice(d * rows, (d + 1) * rows)
        result = partial[span, :] + jnp.dot(
            hidden[span, :], weight[...], preferred_element_type=F32
        )
        if d:
            parts[d - 1][...] = result.astype(BF16)
        else:
            own_ref[...] = result


def product(unit, hidden, partial, piece):
    rows, width = partial.shape[0] // PLANE, partial.shape[1]
    outs = pl.pallas_call(
        product_kernel,
        out_shape=(jax.ShapeDtypeStruct((rows, width), F32),)
        + (jax.ShapeDtypeStruct((rows, width), BF16),) * (PLANE - 1),
        in_specs=[SMEM] + [VMEM] * 3,
        out_specs=(VMEM,) * PLANE,
        scratch_shapes=[pltpu.VMEM(piece.shape, BF16)],
        compiler_params=PARAMS,
        cost_estimate=cost(0, 6 << 20),
        name="product",
    )(unit, hidden, partial, piece)
    return outs[0], outs[1:]


def total_kernel(own_ref, *refs):
    came, (keep_ref, send_ref) = refs[:-2], refs[-2:]
    total = own_ref[...]
    for ref in came:
        total = total + ref[...].astype(F32)
    rows = keep_ref.shape[0]
    keep_ref[...] = total[:rows]
    send_ref[...] = total[rows:].astype(BF16)


def total(own, came):
    rows, width = own.shape
    return pl.pallas_call(
        total_kernel,
        out_shape=(
            jax.ShapeDtypeStruct((rows // 2, width), F32),
            jax.ShapeDtypeStruct((rows // 2, width), BF16),
        ),
        in_specs=[VMEM] * (1 + len(came)),
        out_specs=(VMEM, VMEM),
        compiler_params=PARAMS,
        cost_estimate=cost(0, 4 << 20),
        name="total",
    )(own, *came)


def finish_kernel(unit, resid_ref, mixed_ref, low_ref, high_ref, *refs):
    count = len(refs) // 2
    kept, came, out_ref = refs[:count], refs[count:-1], refs[-1]
    half = out_ref.shape[1] // 2
    for u in range(2):

        @pl.when(unit[0] == u)
        def _():
            for group, which in ((kept, u), (came, 1 - u)):
                base = 0
                other_ref = high_ref if which else low_ref
                for ref in group:
                    span = slice(which * half + base, which * half + base + ref.shape[1])
                    mixed = mixed_ref[:, span].astype(F32)
                    mixed = mixed + other_ref[:, base : base + ref.shape[1]].astype(F32)
                    sums = resid_ref[:, span].astype(F32) + mixed + ref[...].astype(F32)
                    out_ref[:, span] = sums.astype(BF16)
                    base += ref.shape[1]


def finish(unit, resid, mixed, mixed_came, kept, came):
    return pl.pallas_call(
        finish_kernel,
        out_shape=jax.ShapeDtypeStruct(resid.shape, BF16),
        in_specs=[SMEM] + [VMEM] * (4 + len(kept) + len(came)),
        out_specs=VMEM,
        compiler_params=PARAMS,
        cost_estimate=cost(0, 4 << 20),
        name="finish",
    )(unit, resid, mixed, *mixed_came, *kept, *came)


def project_kernel(stay_ref, a_ref, b_ref, weight_ref, keep_ref, low_ref, high_ref, both):
    rows = stay_ref.shape[0]
    half = pl.num_programs(0) // 2
    cut_at = a_ref.shape[1]

    @pl.when(pl.program_id(0) == 0)
    def _():
        both[:rows, :] = stay_ref[...]
        both[rows:, :cut_at] = a_ref[...]
        both[rows:, cut_at:] = b_ref[...]

    result = jnp.dot(both[...], weight_ref[...], preferred_element_type=F32).astype(BF16)
    keep_ref[...] = result[:rows]

    @pl.when(pl.program_id(0) < half)
    def _():
        low_ref[...] = result[rows:]

    @pl.when(pl.program_id(0) >= half)
    def _():
        high_ref[...] = result[rows:]


def project(stay, came_a, came_b, weight):
    rows, depth = stay.shape
    width = weight.shape[1]
    tile = 512 if width % 1024 == 0 else width // 2
    half = width // tile // 2
    fixed = [pl.BlockSpec(x.shape, lambda i: (0, 0)) for x in (stay, came_a, came_b)]
    return pl.pallas_call(
        project_kernel,
        grid=(2 * half,),
        out_shape=(
            jax.ShapeDtypeStruct((rows, width), BF16),
            jax.ShapeDtypeStruct((rows, width // 2), BF16),
            jax.ShapeDtypeStruct((rows, width // 2), BF16),
        ),
        in_specs=fixed + [pl.BlockSpec((depth, tile), lambda i: (0, i))],
        out_specs=(
            pl.BlockSpec((rows, tile), lambda i: (0, i)),
            pl.BlockSpec((rows, tile), lambda i: (0, jnp.minimum(i, half - 1))),
            pl.BlockSpec((rows, tile), lambda i: (0, jnp.maximum(i - half, 0))),
        ),
        scratch_shapes=[pltpu.VMEM((2 * rows, depth), BF16)],
        compiler_params=LARGE,
        cost_estimate=cost(0, 15 << 20),
        name="project",
    )(stay, came_a, came_b, weight)


def split_kernel(x_ref, *outs):
    base = 0
    for out in outs:
        out[...] = x_ref[:, base : base + out.shape[1]]
        base += out.shape[1]


def split_columns(x, widths):
    return pl.pallas_call(
        split_kernel,
        out_shape=tuple(jax.ShapeDtypeStruct((x.shape[0], w), x.dtype) for w in widths),
        in_specs=[VMEM],
        out_specs=(VMEM,) * len(widths),
        compiler_params=PARAMS,
        cost_estimate=cost(0, 2 << 20),
        name="split_columns",
    )(x)


def stack_kernel(*refs):
    *parts, out = refs
    rows = parts[0].shape[0]
    for i, part in enumerate(parts):
        out[i * rows : (i + 1) * rows, :] = part[...]


def stack_rows(parts):
    rows, width = parts[0].shape
    return pl.pallas_call(
        stack_kernel,
        out_shape=jax.ShapeDtypeStruct((len(parts) * rows, width), parts[0].dtype),
        in_specs=[VMEM] * len(parts),
        out_specs=VMEM,
        compiler_params=PARAMS,
        cost_estimate=cost(0, 2 << 20),
        name="stack_rows",
    )(*parts)


def swap_units(x):
    return lax.ppermute(x, "unit", [(0, 1), (1, 0)])


def after(x, *others):
    return lax.optimization_barrier((x, *others))[0]


def ring_at(step, length):
    if isinstance(step, int):
        return 2 * step - min(step, 1) if 2 * step <= length else 2 * (length - step)
    return jnp.where(2 * step <= length, 2 * step - jnp.minimum(step, 1), 2 * (length - step))


def ring_place(place, length):
    return jnp.where(place % 2 == 1, (place + 1) // 2, (length - place // 2) % length)


def chunk_widths(width):
    first, last = width // 4 // 128 * 128, width // 3 // 128 * 128
    return [first, width - first - last, last]


def on_device(
    queries,
    kv_new,
    kv_pool,
    page_table,
    ctx_pages,
    ssm_x,
    ssm_z,
    ssm_bc,
    dt_raw,
    dt_bias,
    decay_rate,
    skip_gain,
    ssm_state,
    ssm_norm_gain,
    resid,
    out_weight,
    ffn_hidden,
    down_weight,
    page_owner,
):
    tok_rows = queries.shape[0]
    n_req = lax.axis_size("req")
    block_rows, width = down_weight.shape
    u = lax.axis_index("unit")
    unit = u.reshape(1)
    req = lax.axis_index("req")
    layers = n_req // PLANE

    ring = [ring_at(i, layers) for i in range(layers)]
    ring_pairs = [
        (ring[i] * PLANE + p, ring[(i + 1) % layers] * PLANE + p)
        for i in range(layers)
        for p in range(PLANE)
    ]

    def pass_on(x):
        return lax.ppermute(x, "req", ring_pairs)

    kept, sent = cut(unit, down_weight)
    hops = [stack_rows([kept, swap_units(sent)])]
    if layers > 2:
        hops.append(pass_on(hops[0]))

    def plane_swap(x, d):
        return lax.ppermute(
            x, "req", [(r, r - r % PLANE + ((r % PLANE) ^ d)) for r in range(n_req)]
        )

    mine = spread(req.reshape(1), after(ffn_hidden, hops[0]), 2 * block_rows, layers)
    hidden = [plane_swap(x, d) if d else x for d, x in enumerate(mine)]
    attn, pages_held, pages_leave = attend(
        page_table, ctx_pages, page_owner[:, :, 0], unit, after(queries, mine[0]), kv_new, kv_pool
    )
    while len(hops) < layers - 1:
        hops.append(pass_on(after(hops[-1], attn)))
    stay, leave_a, leave_b, state_held, state_leave = state_space(
        unit,
        skip_gain,
        after(attn, *hops[1:2]),
        ssm_x,
        ssm_z,
        ssm_bc,
        dt_raw,
        dt_bias[None, :],
        decay_rate[None, :],
        ssm_norm_gain[None, :],
        ssm_state,
    )
    hidden = after(hidden, stay)
    leave_came = [swap_units(x) for x in after((leave_a, leave_b), *hidden)]
    pair = PLANE // 2
    gathered = [after(stack_rows(x), *leave_came) for x in (hidden[:pair], hidden[pair:])]
    swapped = [swap_units(x) for x in gathered]
    hidden = list(hidden) + swapped
    mixed, *mixed_leave = project(stay, *leave_came, out_weight)
    state_leave, pages_leave = after((state_leave, pages_leave), stay)
    state_came, pages_came = swap_units(state_leave), swap_units(pages_leave)
    mixed_came = [
        swap_units(x) for x in after(mixed_leave, hops[-1], state_came, pages_came, *swapped)
    ]
    widths = chunk_widths(width // 2)
    ends = [pass_on(x) for x in split_columns(after(hops[-1], mixed), widths)]
    done = len(hops) * hops[0].shape[0]
    front, last_hidden = order_rows(hidden, done)
    sums, order, received, low = [], mixed_came, [], 0
    for n, end in enumerate(ends):
        piece = begin(unit, after(front, *order) if n else front, hops, low, widths[n])
        own, parts = product(unit, last_hidden, piece, after(end, piece, *order))
        order, low = list(parts) + [x[0] for x in sums], low + widths[n]
        if n == len(ends) - 1:
            decode_kv, decode_state, mixed = settle(
                unit, pages_came, state_came, pages_held, state_held, after(mixed, *parts)
            )
        if received:
            parts = after(parts, *(received if n < len(ends) - 1 else received[:1]))
        received = [plane_swap(x, d) for d, x in enumerate(parts, 1)]
        token = sums[-1][0] if sums else own
        sums.append(total(own, after(received, token, *([mixed] if n == len(ends) - 1 else []))))
    kept, leave = zip(*sums)
    came = [swap_units(x) for x in leave]
    layer_out = finish(unit, resid, mixed, mixed_came, kept, came)
    return (layer_out, decode_kv, decode_state)


def solution(mesh):
    return jax.shard_map(
        on_device,
        mesh=mesh,
        in_specs=(
            P(("req", "unit"), None),
            P(("req", "unit"), None),
            P(("req", "unit"), None, None),
            P(("req", "unit"), None),
            P(("req", "unit")),
            P(("req", "unit"), None),
            P(("req", "unit"), None),
            P(("req", "unit"), None),
            P(("req", "unit"), None),
            P(),
            P(),
            P(),
            P(("req", "unit"), None, None, None),
            P(),
            P(("req", "unit"), None),
            P("unit", None),
            P(("req", "unit"), None),
            P(("req", "unit"), None),
            P(("req", "unit"), None, None),
        ),
        out_specs=(
            P(("req", "unit"), None),
            P(("req", "unit"), None, None),
            P("req", "unit", None, None),
        ),
        check_vma=False,
    )
```

```python
import functools
import math

import jax
import jax.numpy as jnp
from jax import lax
from jax.experimental import pallas as pl
from jax.experimental.pallas import tpu as pltpu
from jax.sharding import PartitionSpec as P

QUERY_HEADS = 12
KEY_VALUE_HEADS = 2
HEAD_WIDTH = 128
MIXER_HEADS = 24
PM = 128
NS = 256

PLANE = 4

norm_eps = 1e-05

F32, BF16 = jnp.float32, jnp.bfloat16
VMEM = pl.BlockSpec(memory_space=pltpu.VMEM)
SMEM = pl.BlockSpec(memory_space=pltpu.SMEM)
ANY = pl.BlockSpec(memory_space=pl.ANY)
PARAMS = pltpu.CompilerParams(vmem_limit_bytes=24 * 1024 * 1024)
LARGE = pltpu.CompilerParams(vmem_limit_bytes=48 * 1024 * 1024)


def cost(flops, moved, exps=0):
    return pl.CostEstimate(flops=0, bytes_accessed=0, transcendentals=0)


def contract_last(a, b):
    return lax.dot_general(a, b, (((1,), (1,)), ((), ())), preferred_element_type=F32)


def two_terms(x):
    high = x.astype(BF16)
    return high, (x - high.astype(F32)).astype(BF16)


def attend_kernel(
    table, ctx, owner, unit, q_ref, new_ref, pool, out_ref, held, leave, pages, zero, sems, osems
):
    count, length, _ = pages.shape
    slots = leave.shape[0]
    live = ctx[0]
    u = unit[0]
    for j in range(count):

        @pl.when(j == live)
        def _():
            pltpu.make_async_copy(new_ref, pages.at[j], sems.at[j]).start()

        @pl.when(j != live)
        def _():
            pltpu.make_async_copy(pool.at[table[0, j]], pages.at[j], sems.at[j]).start()

    zero[...] = jnp.zeros_like(zero)
    for j in range(count):
        pltpu.make_async_copy(new_ref, pages.at[j], sems.at[j]).wait()

    named = [jnp.int32(0), jnp.int32(0)]
    for j in range(count):
        own = owner[0, j] == u
        rank = jnp.where(own, named[0], named[1])
        named = [named[0] + own.astype(jnp.int32), named[1] + 1 - own.astype(jnp.int32)]
        for source, when in ((pages.at[j], j <= live), (zero, j > live)):

            @pl.when(when & own)
            def _():
                pltpu.make_async_copy(source, held.at[u * slots + rank], osems.at[j]).start()

            @pl.when(when & jnp.logical_not(own))
            def _():
                pltpu.make_async_copy(source, leave.at[rank], osems.at[j]).start()

    for k in range(slots):

        @pl.when(k >= named[0])
        def _():
            pltpu.make_async_copy(zero, held.at[u * slots + k], osems.at[count + k]).start()

        @pl.when(k >= named[1])
        def _():
            pltpu.make_async_copy(zero, leave.at[k], osems.at[count + slots + k]).start()

    group = QUERY_HEADS // KEY_VALUE_HEADS
    heads = 3
    rows, keys = heads * length, count * length
    limit = live * length + lax.broadcasted_iota(jnp.int32, (rows, 1), 0) % length
    visible = lax.broadcasted_iota(jnp.int32, (rows, keys), 1) <= limit
    scale = 1.0 / math.sqrt(HEAD_WIDTH)
    for k in range(KEY_VALUE_HEADS):
        key_rows = pages[:, :, k * HEAD_WIDTH : (k + 1) * HEAD_WIDTH].reshape(keys, HEAD_WIDTH)
        lo = (KEY_VALUE_HEADS + k) * HEAD_WIDTH
        value_rows = pages[:, :, lo : lo + HEAD_WIDTH].reshape(keys, HEAD_WIDTH)
        for first in range(k * group, (k + 1) * group, heads):
            spans = [
                slice(h * HEAD_WIDTH, (h + 1) * HEAD_WIDTH) for h in range(first, first + heads)
            ]
            q = jnp.concatenate([q_ref[:, span] for span in spans], axis=0)
            scores = jnp.where(visible, contract_last(q, key_rows), -1e30)
            top = jnp.max(scores, axis=1, keepdims=True)
            exponent = jnp.exp((scores - top) * scale)
            weights = (exponent * (1.0 / jnp.sum(exponent, axis=1, keepdims=True))).astype(BF16)
            attended = jnp.dot(weights, value_rows, preferred_element_type=F32).astype(BF16)
            for i, span in enumerate(spans):
                out_ref[:, span] = attended[i * length : (i + 1) * length]

    for j in range(count):
        pltpu.make_async_copy(zero, leave.at[0], osems.at[j]).wait()
    for k in range(slots):

        @pl.when(k >= named[0])
        def _():
            pltpu.make_async_copy(zero, leave.at[0], osems.at[count + k]).wait()

        @pl.when(k >= named[1])
        def _():
            pltpu.make_async_copy(zero, leave.at[0], osems.at[count + slots + k]).wait()


def attend(table, ctx, owner, unit, queries, kv_new, pool):
    count, length, width = pool.shape
    slots = max(2, (count + 1) // 2)
    pairs = QUERY_HEADS * length * count * length
    return pl.pallas_call(
        attend_kernel,
        out_shape=(
            jax.ShapeDtypeStruct(queries.shape, BF16),
            jax.ShapeDtypeStruct((2 * slots, length, width), BF16),
            jax.ShapeDtypeStruct((slots, length, width), BF16),
        ),
        in_specs=[SMEM, SMEM, SMEM, SMEM, VMEM, VMEM, ANY],
        out_specs=(VMEM, ANY, ANY),
        scratch_shapes=[
            pltpu.VMEM((count, length, width), BF16),
            pltpu.VMEM((length, width), BF16),
            pltpu.SemaphoreType.DMA((count,)),
            pltpu.SemaphoreType.DMA((count + 2 * slots,)),
        ],
        compiler_params=LARGE,
        cost_estimate=cost(4 * pairs * HEAD_WIDTH * 4, 6 << 20, pairs),
        name="attend",
    )(table, ctx, owner, unit, queries, kv_new, pool)


def state_kernel(
    unit,
    skip,
    attn_ref,
    x_ref,
    z_ref,
    bc_ref,
    dt_ref,
    bias_ref,
    rate_ref,
    gain_ref,
    state_ref,
    stay_ref,
    leave_a,
    leave_b,
    held,
    send_ref,
    gated,
    fresh,
    sems,
):
    length = x_ref.shape[0]
    heads, share = MIXER_HEADS, MIXER_HEADS // 2
    u = unit[0]
    rows = lax.broadcasted_iota(jnp.int32, (length, length), 0)
    cols = lax.broadcasted_iota(jnp.int32, (length, length), 1)
    causal = rows >= cols
    raw = dt_ref[...] + bias_ref[...]
    step = jnp.maximum(raw, 0.0) + jnp.log1p(jnp.exp(-jnp.abs(raw)))
    cum = jnp.dot(
        causal.astype(F32),
        -step * rate_ref[...],
        precision=lax.Precision.HIGHEST,
        preferred_element_type=F32,
    )
    blank = jnp.zeros((length, length - heads), F32)
    cum_rows = jnp.transpose(jnp.concatenate([cum, blank], axis=1))
    step_rows = jnp.transpose(jnp.concatenate([step, blank], axis=1))
    last = cum[length - 1 : length, :]
    b_rows, c_rows = bc_ref[:, :NS], bc_ref[:, NS:]
    dots = contract_last(c_rows, b_rows)
    square = jnp.zeros((length, PM), F32)
    for h in range(heads):
        span = slice(h * PM, (h + 1) * PM)
        cum_t, cum_s = cum[:, h : h + 1], cum_rows[h : h + 1, :]
        step_s, end = step_rows[h : h + 1, :], last[:, h : h + 1]
        decay = jnp.exp(jnp.where(causal, cum_t - cum_s, -1e30))
        mixing = (dots * decay * step_s).astype(BF16)
        x = x_ref[:, span]
        x_float = x.astype(F32)
        prior = state_ref[0, h]
        high, low = two_terms(prior)
        carried = contract_last(c_rows, high) + contract_last(c_rows, low)
        y = jnp.dot(mixing, x, preferred_element_type=F32)
        y = y + carried * jnp.exp(cum_t) + skip[h] * x_float
        z = z_ref[:, span].astype(F32)
        g = y * (z / (1.0 + jnp.exp(-z)))
        gated[:, span] = g
        square = square + g * g
        weighted = jnp.transpose(x_float) * (jnp.exp(end - cum_s) * step_s)
        high, low = two_terms(weighted)
        new = jnp.exp(end) * prior + (
            jnp.dot(high, b_rows, preferred_element_type=F32)
            + jnp.dot(low, b_rows, preferred_element_type=F32)
        )
        place = h % share

        @pl.when(u == h // share)
        def _():
            fresh[place] = new
            pltpu.make_async_copy(fresh.at[place], held.at[u, place], sems.at[place]).start()

        @pl.when(u != h // share)
        def _():
            send_ref[place] = new.astype(BF16)

    mean = jnp.sum(square, axis=1, keepdims=True) * (1.0 / (heads * PM))
    out = (gated[...] * lax.rsqrt(mean + norm_eps) * gain_ref[...]).astype(BF16)
    attn_width = attn_ref.shape[1]
    cut = stay_ref.shape[1] - attn_width
    part = leave_a.shape[1]

    @pl.when(u == 0)
    def _():
        stay_ref[:, :attn_width] = attn_ref[...]
        stay_ref[:, attn_width:] = out[:, :cut]
        leave_a[...] = out[:, cut : cut + part]
        leave_b[...] = out[:, cut + part :]

    @pl.when(u == 1)
    def _():
        stay_ref[...] = out[:, cut:]
        leave_a[...] = attn_ref[:, :part]
        leave_b[:, : attn_width - part] = attn_ref[:, part:]
        leave_b[:, attn_width - part :] = out[:, :cut]

    for place in range(share):
        pltpu.make_async_copy(fresh.at[place], held.at[0, place], sems.at[place]).wait()


def state_space(unit, skip, attn, x, z, bc, dt, bias, rate, gain, state):
    length, width = x.shape
    share = MIXER_HEADS // 2
    half = (attn.shape[1] + width) // 2
    return pl.pallas_call(
        state_kernel,
        out_shape=(
            jax.ShapeDtypeStruct((length, half), BF16),
            jax.ShapeDtypeStruct((length, half // 2), BF16),
            jax.ShapeDtypeStruct((length, half - half // 2), BF16),
            jax.ShapeDtypeStruct((2, share, PM, NS), F32),
            jax.ShapeDtypeStruct((share, PM, NS), BF16),
        ),
        in_specs=[SMEM, SMEM] + [VMEM] * 9,
        out_specs=(VMEM, VMEM, VMEM, ANY, VMEM),
        scratch_shapes=[
            pltpu.VMEM((length, width), F32),
            pltpu.VMEM((share, PM, NS), F32),
            pltpu.SemaphoreType.DMA((share,)),
        ],
        compiler_params=LARGE,
        cost_estimate=cost(4 << 30, 10 << 20, MIXER_HEADS * length * length * 2),
        name="state_space",
    )(unit, skip, attn, x, z, bc, dt, bias, rate, gain, state)


def settle_kernel(
    unit, pages, state, pages_in, state_in, rows_in, pages_out, state_out, rows_out, wide, sem
):
    slots = pages.shape[0]
    u = unit[0]
    copy = pltpu.make_async_copy(pages, pages_out.at[pl.ds((1 - u) * slots, slots)], sem.at[0])
    copy.start()
    wide[...] = state[...].astype(F32)
    other = pltpu.make_async_copy(wide, state_out.at[1 - u], sem.at[1])
    other.start()
    copy.wait()
    other.wait()


def settle(unit, pages, state, pages_held, state_held, rows):
    return pl.pallas_call(
        settle_kernel,
        out_shape=tuple(
            jax.ShapeDtypeStruct(x.shape, x.dtype) for x in (pages_held, state_held, rows)
        ),
        in_specs=[SMEM, ANY, VMEM, ANY, ANY, ANY],
        out_specs=(ANY, ANY, ANY),
        scratch_shapes=[pltpu.VMEM(state.shape, F32), pltpu.SemaphoreType.DMA((2,))],
        input_output_aliases={3: 0, 4: 1, 5: 2},
        compiler_params=PARAMS,
        cost_estimate=cost(0, 5 << 20),
        name="settle",
    )(unit, pages, state, pages_held, state_held, rows)


def cut_kernel(unit, weight_ref, kept, sent):
    half = weight_ref.shape[1] // 2
    for u, low_ref, high_ref in ((0, kept, sent), (1, sent, kept)):

        @pl.when(unit[0] == u)
        def _():
            low_ref[...] = weight_ref[:, :half]
            high_ref[...] = weight_ref[:, half:]


def cut(unit, weight):
    rows, width = weight.shape
    shape = jax.ShapeDtypeStruct((rows, width // 2), weight.dtype)
    return pl.pallas_call(
        cut_kernel,
        out_shape=(shape, shape),
        in_specs=[SMEM, VMEM],
        out_specs=(VMEM, VMEM),
        compiler_params=PARAMS,
        cost_estimate=cost(0, 3 << 20),
        name="cut",
    )(unit, weight)


def block_of(req, d, k, layers):
    layer, place = req // PLANE, req % PLANE
    source = ring_at((ring_place(layer, layers) + layers - k) % layers, layers)
    return source * PLANE + (place ^ d)


def spread_kernel(req, hidden, *refs):
    outs, sem = refs[:-1], refs[-1]
    rows, depth = outs[0].shape
    layers = sem.shape[0] // PLANE
    chip_rows = depth // layers
    copies = []
    for d in range(PLANE):
        for k in range(layers):
            column = pl.multiple_of(chip_rows * block_of(req[0], d, k, layers), 128)
            copies.append(
                pltpu.make_async_copy(
                    hidden.at[:, pl.ds(column, chip_rows)],
                    outs[d].at[:, k * chip_rows : (k + 1) * chip_rows],
                    sem.at[d * layers + k],
                )
            )
    for copy in copies:
        copy.start()
    for copy in copies:
        copy.wait()


def spread(req, hidden, chip_rows, layers):
    rows = hidden.shape[0]
    if chip_rows % 128:
        return [
            jnp.concatenate(
                [
                    lax.dynamic_slice(
                        hidden, (0, block_of(req[0], d, k, layers) * chip_rows), (rows, chip_rows)
                    )
                    for k in range(layers)
                ],
                axis=1,
            )
            for d in range(PLANE)
        ]
    return pl.pallas_call(
        spread_kernel,
        out_shape=(jax.ShapeDtypeStruct((rows, layers * chip_rows), hidden.dtype),) * PLANE,
        in_specs=[SMEM, ANY],
        out_specs=(VMEM,) * PLANE,
        scratch_shapes=[pltpu.SemaphoreType.DMA((PLANE * layers,))],
        compiler_params=PARAMS,
        cost_estimate=cost(0, 4 << 20),
        name="spread",
    )(req, hidden)


def place_rows(weight, pieces, unit, low=0):
    block_rows, width = pieces[0].shape[0] // 2, weight.shape[1]
    for k, piece in enumerate(pieces):
        for which, place in ((0, unit), (1, 1 - unit)):
            at = pl.multiple_of((2 * k + place) * block_rows, 16)
            rows = slice(which * block_rows, (which + 1) * block_rows)
            weight[pl.ds(at, block_rows), :] = piece[rows, low : low + width]


def order_kernel(*refs):
    hidden, (front_ref, last_ref) = refs[:-2], refs[-2:]
    rows, done = hidden[0].shape[0], front_ref.shape[1]
    for d in range(PLANE):
        place = d % (PLANE // 2) * rows
        pair = hidden[PLANE + d // (PLANE // 2)]
        for n, block in ((0, hidden[d][...]), (1, pair[place : place + rows, :])):
            span = slice((2 * d + n) * rows, (2 * d + n + 1) * rows)
            front_ref[span, :] = block[:, :done]
            last_ref[span, :] = block[:, done:]


def order_rows(hidden, done):
    rows, depth = hidden[0].shape
    every = 2 * PLANE * rows
    return pl.pallas_call(
        order_kernel,
        out_shape=(
            jax.ShapeDtypeStruct((every, done), BF16),
            jax.ShapeDtypeStruct((every, depth - done), BF16),
        ),
        in_specs=[VMEM] * len(hidden),
        out_specs=(VMEM, VMEM),
        compiler_params=PARAMS,
        cost_estimate=cost(0, 6 << 20),
        name="order_rows",
    )(*hidden)


def begin_kernel(low, unit, front, *refs):
    pieces, (out, weight) = refs[:-2], refs[-2:]
    place_rows(weight, pieces, unit[0], low)
    rows = out.shape[0] // PLANE
    for d in range(PLANE):
        span = slice(d * rows, (d + 1) * rows)
        out[span, :] = jnp.dot(front[span, :], weight[...], preferred_element_type=F32)


def begin(unit, front, pieces, low, width):
    every, done = front.shape
    return pl.pallas_call(
        functools.partial(begin_kernel, low),
        out_shape=jax.ShapeDtypeStruct((every, width), F32),
        in_specs=[SMEM] + [VMEM] * (1 + len(pieces)),
        out_specs=VMEM,
        scratch_shapes=[pltpu.VMEM((done, width), BF16)],
        compiler_params=PARAMS,
        cost_estimate=cost(0, 8 << 20),
        name="begin",
    )(unit, front, *pieces)


def product_kernel(unit, hidden, partial, piece, own_ref, *refs):
    parts, weight = refs[:-1], refs[-1]
    place_rows(weight, [piece], unit[0])
    rows = own_ref.shape[0]
    for d in range(PLANE):
        span = slice(d * rows, (d + 1) * rows)
        result = partial[span, :] + jnp.dot(
            hidden[span, :], weight[...], preferred_element_type=F32
        )
        if d:
            parts[d - 1][...] = result.astype(BF16)
        else:
            own_ref[...] = result


def product(unit, hidden, partial, piece):
    rows, width = partial.shape[0] // PLANE, partial.shape[1]
    outs = pl.pallas_call(
        product_kernel,
        out_shape=(jax.ShapeDtypeStruct((rows, width), F32),)
        + (jax.ShapeDtypeStruct((rows, width), BF16),) * (PLANE - 1),
        in_specs=[SMEM] + [VMEM] * 3,
        out_specs=(VMEM,) * PLANE,
        scratch_shapes=[pltpu.VMEM(piece.shape, BF16)],
        compiler_params=PARAMS,
        cost_estimate=cost(0, 6 << 20),
        name="product",
    )(unit, hidden, partial, piece)
    return outs[0], outs[1:]


def total_kernel(own_ref, *refs):
    came, (keep_ref, send_ref) = refs[:-2], refs[-2:]
    total = own_ref[...]
    for ref in came:
        total = total + ref[...].astype(F32)
    rows = keep_ref.shape[0]
    keep_ref[...] = total[:rows]
    send_ref[...] = total[rows:].astype(BF16)


def total(own, came):
    rows, width = own.shape
    return pl.pallas_call(
        total_kernel,
        out_shape=(
            jax.ShapeDtypeStruct((rows // 2, width), F32),
            jax.ShapeDtypeStruct((rows // 2, width), BF16),
        ),
        in_specs=[VMEM] * (1 + len(came)),
        out_specs=(VMEM, VMEM),
        compiler_params=PARAMS,
        cost_estimate=cost(0, 4 << 20),
        name="total",
    )(own, *came)


def finish_kernel(unit, resid_ref, mixed_ref, low_ref, high_ref, *refs):
    count = len(refs) // 2
    kept, came, out_ref = refs[:count], refs[count:-1], refs[-1]
    half = out_ref.shape[1] // 2
    for u in range(2):

        @pl.when(unit[0] == u)
        def _():
            for group, which in ((kept, u), (came, 1 - u)):
                base = 0
                other_ref = high_ref if which else low_ref
                for ref in group:
                    span = slice(which * half + base, which * half + base + ref.shape[1])
                    mixed = mixed_ref[:, span].astype(F32)
                    mixed = mixed + other_ref[:, base : base + ref.shape[1]].astype(F32)
                    sums = resid_ref[:, span].astype(F32) + mixed + ref[...].astype(F32)
                    out_ref[:, span] = sums.astype(BF16)
                    base += ref.shape[1]


def finish(unit, resid, mixed, mixed_came, kept, came):
    return pl.pallas_call(
        finish_kernel,
        out_shape=jax.ShapeDtypeStruct(resid.shape, BF16),
        in_specs=[SMEM] + [VMEM] * (4 + len(kept) + len(came)),
        out_specs=VMEM,
        compiler_params=PARAMS,
        cost_estimate=cost(0, 4 << 20),
        name="finish",
    )(unit, resid, mixed, *mixed_came, *kept, *came)


def project_kernel(stay_ref, a_ref, b_ref, weight_ref, keep_ref, low_ref, high_ref, both):
    rows = stay_ref.shape[0]
    half = pl.num_programs(0) // 2
    cut_at = a_ref.shape[1]

    @pl.when(pl.program_id(0) == 0)
    def _():
        both[:rows, :] = stay_ref[...]
        both[rows:, :cut_at] = a_ref[...]
        both[rows:, cut_at:] = b_ref[...]

    result = jnp.dot(both[...], weight_ref[...], preferred_element_type=F32).astype(BF16)
    keep_ref[...] = result[:rows]

    @pl.when(pl.program_id(0) < half)
    def _():
        low_ref[...] = result[rows:]

    @pl.when(pl.program_id(0) >= half)
    def _():
        high_ref[...] = result[rows:]


def project(stay, came_a, came_b, weight):
    rows, depth = stay.shape
    width = weight.shape[1]
    tile = 768 if width % 1536 == 0 else width // 2
    half = width // tile // 2
    fixed = [pl.BlockSpec(x.shape, lambda i: (0, 0)) for x in (stay, came_a, came_b)]
    return pl.pallas_call(
        project_kernel,
        grid=(2 * half,),
        out_shape=(
            jax.ShapeDtypeStruct((rows, width), BF16),
            jax.ShapeDtypeStruct((rows, width // 2), BF16),
            jax.ShapeDtypeStruct((rows, width // 2), BF16),
        ),
        in_specs=fixed + [pl.BlockSpec((depth, tile), lambda i: (0, i))],
        out_specs=(
            pl.BlockSpec((rows, tile), lambda i: (0, i)),
            pl.BlockSpec((rows, tile), lambda i: (0, jnp.minimum(i, half - 1))),
            pl.BlockSpec((rows, tile), lambda i: (0, jnp.maximum(i - half, 0))),
        ),
        scratch_shapes=[pltpu.VMEM((2 * rows, depth), BF16)],
        compiler_params=LARGE,
        cost_estimate=cost(0, 15 << 20),
        name="project",
    )(stay, came_a, came_b, weight)


def split_kernel(x_ref, *outs):
    base = 0
    for out in outs:
        out[...] = x_ref[:, base : base + out.shape[1]]
        base += out.shape[1]


def split_columns(x, widths):
    return pl.pallas_call(
        split_kernel,
        out_shape=tuple(jax.ShapeDtypeStruct((x.shape[0], w), x.dtype) for w in widths),
        in_specs=[VMEM],
        out_specs=(VMEM,) * len(widths),
        compiler_params=PARAMS,
        cost_estimate=cost(0, 2 << 20),
        name="split_columns",
    )(x)


def stack_kernel(*refs):
    *parts, out = refs
    rows = parts[0].shape[0]
    for i, part in enumerate(parts):
        out[i * rows : (i + 1) * rows, :] = part[...]


def stack_rows(parts):
    rows, width = parts[0].shape
    return pl.pallas_call(
        stack_kernel,
        out_shape=jax.ShapeDtypeStruct((len(parts) * rows, width), parts[0].dtype),
        in_specs=[VMEM] * len(parts),
        out_specs=VMEM,
        compiler_params=PARAMS,
        cost_estimate=cost(0, 2 << 20),
        name="stack_rows",
    )(*parts)


def swap_units(x):
    return lax.ppermute(x, "unit", [(0, 1), (1, 0)])


def after(x, *others):
    return lax.optimization_barrier((x, *others))[0]


def ring_at(step, length):
    if isinstance(step, int):
        return 2 * step - min(step, 1) if 2 * step <= length else 2 * (length - step)
    return jnp.where(2 * step <= length, 2 * step - jnp.minimum(step, 1), 2 * (length - step))


def ring_place(place, length):
    return jnp.where(place % 2 == 1, (place + 1) // 2, (length - place // 2) % length)


def chunk_widths(width):
    first, last = width // 4 // 128 * 128, width // 3 // 128 * 128
    return [first, width - first - last, last]


def on_device(
    queries,
    kv_new,
    kv_pool,
    page_table,
    ctx_pages,
    ssm_x,
    ssm_z,
    ssm_bc,
    dt_raw,
    dt_bias,
    decay_rate,
    skip_gain,
    ssm_state,
    ssm_norm_gain,
    resid,
    out_weight,
    ffn_hidden,
    down_weight,
    page_owner,
):
    tok_rows = queries.shape[0]
    n_req = lax.axis_size("req")
    block_rows, width = down_weight.shape
    u = lax.axis_index("unit")
    unit = u.reshape(1)
    req = lax.axis_index("req")
    layers = n_req // PLANE

    ring = [ring_at(i, layers) for i in range(layers)]
    ring_pairs = [
        (ring[i] * PLANE + p, ring[(i + 1) % layers] * PLANE + p)
        for i in range(layers)
        for p in range(PLANE)
    ]

    def pass_on(x):
        return lax.ppermute(x, "req", ring_pairs)

    kept, sent = cut(unit, down_weight)
    hops = [stack_rows([kept, swap_units(sent)])]
    if layers > 2:
        hops.append(pass_on(hops[0]))

    def plane_swap(x, d):
        return lax.ppermute(
            x, "req", [(r, r - r % PLANE + ((r % PLANE) ^ d)) for r in range(n_req)]
        )

    mine = spread(req.reshape(1), after(ffn_hidden, hops[0]), 2 * block_rows, layers)
    hidden = [plane_swap(x, d) if d else x for d, x in enumerate(mine)]
    attn, pages_held, pages_leave = attend(
        page_table, ctx_pages, page_owner[:, :, 0], unit, after(queries, mine[0]), kv_new, kv_pool
    )
    while len(hops) < layers - 1:
        hops.append(pass_on(after(hops[-1], attn)))
    stay, leave_a, leave_b, state_held, state_leave = state_space(
        unit,
        skip_gain,
        after(attn, *hops[1:2]),
        ssm_x,
        ssm_z,
        ssm_bc,
        dt_raw,
        dt_bias[None, :],
        decay_rate[None, :],
        ssm_norm_gain[None, :],
        ssm_state,
    )
    hidden = after(hidden, stay)
    leave_came = [swap_units(x) for x in after((leave_a, leave_b), *hidden)]
    pair = PLANE // 2
    gathered = [after(stack_rows(x), *leave_came) for x in (hidden[:pair], hidden[pair:])]
    swapped = [swap_units(x) for x in gathered]
    hidden = list(hidden) + swapped
    mixed, *mixed_leave = project(stay, *leave_came, out_weight)
    state_leave, pages_leave = after((state_leave, pages_leave), stay)
    state_came, pages_came = swap_units(state_leave), swap_units(pages_leave)
    mixed_came = [
        swap_units(x) for x in after(mixed_leave, hops[-1], state_came, pages_came, *swapped)
    ]
    widths = chunk_widths(width // 2)
    ends = [pass_on(x) for x in split_columns(after(hops[-1], mixed), widths)]
    done = len(hops) * hops[0].shape[0]
    front, last_hidden = order_rows(hidden, done)
    sums, order, received, low = [], mixed_came, [], 0
    for n, end in enumerate(ends):
        piece = begin(unit, after(front, *order) if n else front, hops, low, widths[n])
        own, parts = product(unit, last_hidden, piece, after(end, piece, *order))
        order, low = list(parts) + [x[0] for x in sums], low + widths[n]
        if n == len(ends) - 1:
            decode_kv, decode_state, mixed = settle(
                unit, pages_came, state_came, pages_held, state_held, after(mixed, *parts)
            )
        if received:
            parts = after(parts, *(received if n < len(ends) - 1 else received[:1]))
        received = [plane_swap(x, d) for d, x in enumerate(parts, 1)]
        token = sums[-1][0] if sums else own
        sums.append(total(own, after(received, token, *([mixed] if n == len(ends) - 1 else []))))
    kept, leave = zip(*sums)
    came = [swap_units(x) for x in leave]
    layer_out = finish(unit, resid, mixed, mixed_came, kept, came)
    return (layer_out, decode_kv, decode_state)


def solution(mesh):
    return jax.shard_map(
        on_device,
        mesh=mesh,
        in_specs=(
            P(("req", "unit"), None),
            P(("req", "unit"), None),
            P(("req", "unit"), None, None),
            P(("req", "unit"), None),
            P(("req", "unit")),
            P(("req", "unit"), None),
            P(("req", "unit"), None),
            P(("req", "unit"), None),
            P(("req", "unit"), None),
            P(),
            P(),
            P(),
            P(("req", "unit"), None, None, None),
            P(),
            P(("req", "unit"), None),
            P("unit", None),
            P(("req", "unit"), None),
            P(("req", "unit"), None),
            P(("req", "unit"), None, None),
        ),
        out_specs=(
            P(("req", "unit"), None),
            P(("req", "unit"), None, None),
            P("req", "unit", None, None),
        ),
        check_vma=False,
    )
```
